128 devices in a mesh: term: 8 (over z, y_lo), pencil: 16 (over x, y_hi, core).
Axes of the slice: x: 4, y: 4 (y_hi: 2, y_lo: 2; y = y_hi * 2 + y_lo), z: 4, core: 2. Of those that a mesh axis runs over, the one named last changes fastest.
Arguments:
- present_acoustic: float32 [512, 16, 512], P('pencil'), may hold values from -6 to 6
- prior_acoustic: float32 [512, 16, 512], P('pencil'), may hold values from -6 to 6
- location_factor: float32 [16, 512, 16, 512], P('term', 'pencil'), may hold values from -1 to 1
- spectral_multiplier: float32 [16, 16, 512, 512], P('term', None, 'pencil'), may hold values from -6 to 6
- medium_kinds: int32 [512, 16, 512], P('pencil', 'term'), may hold values from 0 to 2
- organ_properties: float32 [3, 2], replicated, may hold values from 0.05 to 0.3
- thermal_increase: float32 [512, 16, 512], P('pencil', 'term'), may hold values from -6 to 6
Outputs:
- pressure_final: float32 [512, 16, 512], P('pencil', 'term')
- temperature_final: float32 [512, 16, 512], P('pencil', 'term')
The draws below stay inside these ranges and needn't reach their ends.
Inputs may be any that keep to these rules, and one draw needn't show every extreme that they name: `medium_kinds`: tissue class of each cell: 0 bone, 1 brain, 2 water.
All inputs are finite; a program needn't handle non-finite values.
Results may differ from the reference program's by a relative error of at most 0.0001.
Values sent between devices are 32-bit elements; how exact they have to be, the bound alone decides.
A program may use at most 128 MiB of HBM per device.

```python
import jax
import jax.numpy as jnp

MESH_COUNT_INITIAL = 512
MESH_COUNT_FINAL = 512
MESH_COUNT_MIDDLE = 16
TERMS = 16
WAVE_STEPS = 2
HEAT_STEPS = 2


def place_ends(drawn, key, least, top_value):
    place = [jax.random.randint(jax.random.fold_in(key, axis), (), 0, length) for axis, length in enumerate(drawn.shape)]
    widest = drawn.shape.index(max(drawn.shape))
    neighbour = place[:widest] + [(place[widest] + 1) % drawn.shape[widest]] + place[widest + 1:]
    return drawn.at[tuple(place)].set(least).at[tuple(neighbour)].set(top_value)


def shard_levels(key, shape, pieces, smallest, largest):
    def one(dim, blocks):
        draws = jax.random.uniform(jax.random.fold_in(jax.random.fold_in(key, 6), dim), (blocks,), jnp.float32, smallest / len(pieces), largest / len(pieces))
        return jnp.repeat(jnp.exp(draws), shape[dim] // blocks).reshape((-1,) + (1,) * (len(shape) - dim - 1))

    loudness = one(*pieces[0])
    for cut in pieces[1:]:
        loudness = loudness * one(*cut)
    return loudness


def normal_values(key, extent, width, most, pieces=(), kind=jnp.bfloat16):
    array = width * jax.random.normal(key, extent, jnp.float32)
    if pieces:
        array = array * shard_levels(key, extent, pieces, -0.22, 0.18)
    return jnp.clip(array, -most, most).astype(kind)


def setup_inputs(seed: int = 0) -> dict:
    arg_keys = jax.random.split(jax.random.key(seed), 8)
    return {
        "present_acoustic": normal_values(arg_keys[0], (MESH_COUNT_INITIAL, MESH_COUNT_MIDDLE, MESH_COUNT_FINAL), 1.0, 6.0, ((0, 16),), jnp.float32),
        "prior_acoustic": normal_values(arg_keys[1], (MESH_COUNT_INITIAL, MESH_COUNT_MIDDLE, MESH_COUNT_FINAL), 1.0, 6.0, ((0, 16),), jnp.float32),
        "location_factor": normal_values(arg_keys[2], (TERMS, MESH_COUNT_INITIAL, MESH_COUNT_MIDDLE, MESH_COUNT_FINAL), 0.125, 1.0, ((0, 8), (1, 16)), jnp.float32),
        "spectral_multiplier": normal_values(arg_keys[3], (TERMS, MESH_COUNT_MIDDLE, MESH_COUNT_FINAL, MESH_COUNT_INITIAL), 1.0, 6.0, ((0, 8), (2, 16)), jnp.float32),
        "medium_kinds": place_ends(jax.random.randint(arg_keys[4], (MESH_COUNT_INITIAL, MESH_COUNT_MIDDLE, MESH_COUNT_FINAL), 0, 3), jax.random.fold_in(arg_keys[4], 1), 0, 2).astype(jnp.int32),
        "organ_properties": jnp.clip(jax.random.uniform(arg_keys[5], (3, 2), jnp.float32, 0.05, 0.3), 0.05, 0.3),
        "thermal_increase": normal_values(arg_keys[6], (MESH_COUNT_INITIAL, MESH_COUNT_MIDDLE, MESH_COUNT_FINAL), 1.0, 6.0, ((0, 16), (1, 8)), jnp.float32),
    }


DIFFUSION = 0.125


def spectral_sum(pressure, location_factor, spectral_multiplier):
    spectrum = jnp.fft.fftn(pressure, axes=(0, 1, 2))
    summed = jnp.zeros(pressure.shape, pressure.dtype)
    for term_index in range(TERMS):
        factor = jnp.transpose(spectral_multiplier[term_index], (2, 0, 1))
        restored = jnp.real(jnp.fft.ifftn(factor * spectrum, axes=(0, 1, 2)))
        summed = summed + location_factor[term_index] * restored
    return summed


def heat_step(present_thermal, perfuse, source):
    padded = jnp.pad(present_thermal, 1)
    near_sum = padded[2:, 1:-1, 1:-1] + padded[:-2, 1:-1, 1:-1]
    near_sum = near_sum + padded[1:-1, 2:, 1:-1] + padded[1:-1, :-2, 1:-1]
    near_sum = near_sum + padded[1:-1, 1:-1, 2:] + padded[1:-1, 1:-1, :-2]
    return present_thermal + DIFFUSION * (near_sum - 6.0 * present_thermal) - perfuse * present_thermal + source


def reference(present_acoustic, prior_acoustic, location_factor, spectral_multiplier, medium_kinds, organ_properties, thermal_increase):
    previous = prior_acoustic
    current = present_acoustic
    dose_sum = jnp.zeros(present_acoustic.shape, present_acoustic.dtype)
    for turn_index in range(WAVE_STEPS):
        advanced = 2.0 * spectral_sum(current, location_factor, spectral_multiplier) - previous
        dose_sum = dose_sum + advanced * advanced
        previous = current
        current = advanced
    absorb = jnp.where(medium_kinds == 0, organ_properties[0, 0], jnp.where(medium_kinds == 1, organ_properties[1, 0], organ_properties[2, 0]))
    perfuse = jnp.where(medium_kinds == 0, organ_properties[0, 1], jnp.where(medium_kinds == 1, organ_properties[1, 1], organ_properties[2, 1]))
    source = absorb * dose_sum
    present_thermal = thermal_increase
    for turn_index in range(HEAT_STEPS):
        present_thermal = heat_step(present_thermal, perfuse, source)
    return current, present_thermal
```

```python
import math

import numpy as np

import jax
import jax.numpy as jnp
from jax import lax
from jax.experimental import pallas as pl
from jax.experimental.pallas import tpu as pltpu
from jax.sharding import PartitionSpec as P

WAVE_STEPS = 2
HEAT_STEPS = 2
DIFFUSION = 0.125
MESH = pl.DeviceIdType.MESH
F32 = jnp.float32
BF16 = jnp.bfloat16

NX = 512
NY = 16
NZ = 512
NT = 8
NP = 16
XR = NX // NP
SCALE = 2.0 / (NX * NY * NZ)


def high_low(table):
    high = table.astype(BF16)
    low = (table - high.astype(np.float32)).astype(BF16)
    return np.stack([high, low])


def z_table():
    rows = np.zeros((2, NP, 2, 8, NZ), np.float64)
    z = np.arange(NZ)
    for h in range(2):
        for p in range(NP):
            for i in range(8):
                s = 8 * h + i
                if s == 0 and p == 8:
                    rows[h, p, 0, i] = 1.0
                    rows[h, p, 1, i] = 1.0 - 2.0 * (z % 2)
                    continue
                kz = 32 * p + s
                if s == 0 and p < 8:
                    kz = 32 * p + 16
                angle = 2.0 * math.pi * ((kz * z) % NZ) / NZ
                rows[h, p, 0, i] = np.cos(angle)
                rows[h, p, 1, i] = -np.sin(angle)
    return high_low(rows.reshape(NZ, NZ).astype(np.float32))


def x_table():
    k = np.arange(256)[:, None]
    tables = []
    for c in range(2):
        x = 2 * np.arange(256)[None, :] + c
        angle = 2.0 * math.pi * ((k * x) % NX) / NX
        co, si = np.cos(angle), np.sin(angle)
        tables.append(high_low(np.block([[co, si], [-si, co]]).astype(np.float32)))
    return np.stack(tables)


def split(x):
    high = x.astype(BF16)
    low = (x - high.astype(F32)).astype(BF16)
    return high, low


def dot(a, b, ca, cb):
    return lax.dot_general(a, b, (((ca,), (cb,)), ((), ())), preferred_element_type=F32)


def dot3(a, b, ca, cb):
    return dot(a[0], b[0], ca, cb) + dot(a[0], b[1], ca, cb) + dot(a[1], b[0], ca, cb)


def fft16(re, im, sign):
    n = len(re)
    if n == 1:
        return re, im
    er, ei = fft16(re[0::2], im[0::2], sign)
    orr, oi = fft16(re[1::2], im[1::2], sign)
    half = n // 2
    out_r, out_i = [None] * n, [None] * n
    for k in range(half):
        angle = sign * 2.0 * math.pi * k / n
        c, s = math.cos(angle), math.sin(angle)
        a, b = orr[k], oi[k]
        if k == 0:
            tr, ti = a, b
        elif 4 * k == n:
            tr, ti = (b, -a) if sign < 0 else (-b, a)
        elif abs(abs(c) - abs(s)) < 1e-12:
            r = math.sqrt(0.5)
            sc, ss = math.copysign(1.0, c), math.copysign(1.0, s)
            tr = r * ((a if sc > 0 else -a) - (b if ss > 0 else -b))
            ti = r * ((b if sc > 0 else -b) + (a if ss > 0 else -a))
        else:
            tr = c * a - s * b
            ti = c * b + s * a
        out_r[k], out_i[k] = er[k] + tr, ei[k] + ti
        out_r[k + half], out_i[k + half] = er[k] - tr, ei[k] - ti
    return out_r, out_i


def exchange_groups(tiles):
    rows = tiles[0].shape[0]
    lane = lax.broadcasted_iota(jnp.int32, (rows, 128), 1)
    tiles = list(tiles)
    for bit in (4, 2, 1):
        width = bit * 16
        keep_low = (lane % (2 * width)) < width
        new = list(tiles)
        for i in range(8):
            if i & bit:
                continue
            a, b = tiles[i], tiles[i + bit]
            new[i] = jnp.where(keep_low, a, pltpu.roll(b, width, 1))
            new[i + bit] = jnp.where(keep_low, pltpu.roll(a, 128 - width, 1), b)
        tiles = new
    return tiles


def reverse_lanes(tiles):
    lane = lax.broadcasted_iota(jnp.int32, (8, 128), 1)
    index = (128 - lane) % 128
    moved = [jnp.take_along_axis(x, index, axis=1) for x in tiles]
    return [jnp.where(lane == 0, moved[(4 - a) % 4], moved[3 - a]) for a in range(4)]


def wave_kernel(
    pres, prior, loc, spec, ztab, xtab, final_o, dose_o,
    pres_v, prior_v, loc_v, lr, spec_v, srecv, row0, row0r, amp, bmp, zt, xt,
    cur, prev, dose, fsend, frecv, vsend, agb, w, xo, snd, rcv, psend, rsr,
    lsem, ssem, sx, fs, fr, gs, gr, as0, ar0, as1, ar1, rs, rr,
):
    t = lax.axis_index("term")
    p = lax.axis_index("pencil")

    barrier = pltpu.get_barrier_semaphore()

    @pl.loop(1, NP)
    def _(o):
        pl.semaphore_signal(barrier, inc=1, device_id=(t, lax.rem(p + o, NP)), device_id_type=MESH)

    @pl.loop(1, NT)
    def _(o):
        pl.semaphore_signal(barrier, inc=1, device_id=(lax.rem(t + o, NT), p), device_id_type=MESH)

    loads = [
        pltpu.make_async_copy(src, dst, lsem.at[i])
        for i, (src, dst) in enumerate(
            [(pres, pres_v), (ztab, zt), (xtab, xt), (spec, spec_v), (prior, prior_v), (loc, loc_v)]
        )
    ]
    for load in loads:
        load.start()

    pl.semaphore_wait(barrier, NP + NT - 2)

    def remote(src, dst, send, recv, device):
        return pltpu.make_async_remote_copy(
            src_ref=src, dst_ref=dst, send_sem=send, recv_sem=recv, device_id=device, device_id_type=MESH
        )

    mirror = (t, NP - 1 - p)
    swap = remote(spec.at[:, :, pl.ds(16, 16), :], srecv, sx.at[0], sx.at[1], mirror)
    swap.start()

    loads[0].wait()
    for y in range(2):
        for x in range(XR):
            row = y * XR + (x % 2) * 16 + x // 2
            cur[pl.ds(row, 1), :] = pres_v[x, pl.ds(2 * t + y, 1), :]
    loads[3].wait()
    for q in range(2):
        row0[pl.ds(16 * q, 16), 0, :] = spec_v[q, :, 0, :]
    give = jnp.where(p == 0, 8, lax.rem(NP - p, NP))
    rowcopy = remote(row0, row0r, sx.at[2], sx.at[3], (t, give))

    @pl.when(p < 8)
    def _():
        rowcopy.start()

    loads[4].wait()
    for y in range(2):
        for x in range(XR):
            row = y * XR + (x % 2) * 16 + x // 2
            prev[pl.ds(row, 1), :] = prior_v[x, pl.ds(2 * t + y, 1), :]
    dose[...] = jnp.zeros_like(dose)
    loads[1].wait()
    loads[2].wait()

    lane = lax.broadcasted_iota(jnp.int32, (8, 128), 1)
    sub = lax.broadcasted_iota(jnp.int32, (8, 128), 0)
    flip = (8 - sub) % 8

    def build_amp():
        swap.wait()

        @pl.when(p < 8)
        def _():
            rowcopy.wait_send()

        @pl.when(p >= 8)
        def _():
            rowcopy.wait_recv()

        low_p = jnp.where(p < 8, 1, 0)

        @pl.loop(0, 32)
        def _(n):
            q = n // 16
            ky = lax.rem(n, 16)
            kr = lax.rem(16 - ky, 16)
            pick_own = (sub == 0) & (low_p == 1)
            pick_row = (sub == 0) & (low_p == 0)
            mirrored = [[], []]
            for a in range(4):
                cols = pl.ds(128 * a, 128)
                r0 = srecv[q, kr, pl.ds(0, 8), cols]
                r1 = srecv[q, kr, pl.ds(8, 8), cols]
                extra = jnp.broadcast_to(row0r[16 * q + kr, :, cols], (8, 128))
                f0 = jnp.take_along_axis(r0, flip, axis=0)
                f1 = jnp.take_along_axis(r1, flip, axis=0)
                m0 = jnp.where(sub == 0, r0, f1)
                m0 = jnp.where(pick_row, extra, m0)
                m1 = jnp.where(sub == 0, r1, f0)
                mirrored[0].append(m0)
                mirrored[1].append(m1)
            for h in range(2):
                rev = reverse_lanes(mirrored[h])
                for a in range(4):
                    cols = pl.ds(128 * a, 128)
                    own = spec_v[q, ky, pl.ds(8 * h, 8), cols]
                    if h == 0:
                        own = jnp.where(pick_own, spec_v[q, ky, pl.ds(16, 8), cols], own)
                    amp[q, ky, pl.ds(8 * h, 8), cols] = own + rev[a]

        @pl.when(p == 8)
        def _():
            @pl.loop(0, 32)
            def _(n):
                q = n // 16
                ky = lax.rem(n, 16)
                kr = lax.rem(16 - ky, 16)
                own_r, zero_r = [], []
                for a in range(4):
                    cols = pl.ds(128 * a, 128)
                    own_r.append(spec_v[q, kr, pl.ds(0, 8), cols])
                    zero_r.append(jnp.broadcast_to(row0r[16 * q + kr, :, cols], (8, 128)))
                own_r = reverse_lanes(own_r)
                zero_r = reverse_lanes(zero_r)
                for a in range(4):
                    cols = pl.ds(128 * a, 128)
                    last = spec_v[q, ky, pl.ds(0, 8), cols] + own_r[a]
                    first = jnp.broadcast_to(row0r[16 * q + ky, :, cols], (8, 128)) + zero_r[a]
                    old = amp[q, ky, pl.ds(0, 8), cols]
                    amp[q, ky, pl.ds(0, 8), cols] = jnp.where(sub == 0, 0.25 * (first + last), old)
                    bmp[q, ky, :, cols] = jnp.where(sub == 0, 0.25 * (first - last), 0.0)

    def y_stage(re, im, weight, store):
        re, im = fft16(re, im, -1)
        for q in range(2):
            wr, wi = [], []
            for ky in range(16):
                m = weight(q, ky)
                wr.append(m * re[ky])
                wi.append(m * im[ky])
            wr, wi = fft16(wr, wi, 1)
            for y in range(16):
                store(q, 0, y, wr[y])
                store(q, 1, y, wi[y])

    def wait_bytes(ref, sem):
        pltpu.make_async_copy(ref, ref, sem).wait()

    @pl.loop(0, WAVE_STEPS)
    def _(step):
        b = split(cur[...])
        b = tuple(jnp.concatenate([v, v], axis=0) for v in b)
        out = dot3((zt[0], zt[1]), b, 1, 1).reshape(2, NP, 2, 8, 128)
        wide = lax.broadcasted_iota(jnp.int32, (NP, 8, 128), 2)
        for h in range(2):
            fsend[:, pl.ds(8 * h, 8), :] = jnp.where(wide < 64, out[h, :, 0], out[h, :, 1])

        @pl.loop(1, NP)
        def _(o):
            d = lax.rem(p + o, NP)
            remote(fsend.at[d], frecv.at[step, p], fs.at[0], fr.at[step], (t, d)).start()

        frecv[step, p] = fsend[p]
        wait_bytes(frecv.at[step, pl.ds(0, NP - 1)], fr.at[step])

        groups = [exchange_groups([frecv[step, 8 * a + i] for i in range(8)]) for a in range(2)]
        parts = []
        for c in range(2):
            rows = [
                jnp.concatenate(
                    [groups[0][y * 2 + c], groups[1][y * 2 + c], groups[0][4 + y * 2 + c], groups[1][4 + y * 2 + c]],
                    axis=1,
                )
                for y in range(2)
            ]
            lhs = split(jnp.concatenate(rows, axis=0))
            parts.append(dot3(lhs, (xt[c, 0], xt[c, 1]), 1, 1))
        for lo, v in ((0, parts[0] + parts[1]), (256, parts[0] - parts[1])):
            for h in range(2):
                for y in range(2):
                    for ri in range(2):
                        vsend[h, y, ri, :, pl.ds(lo, 256)] = v[
                            y * 16 + 8 * h : y * 16 + 8 * h + 8, ri * 256 : ri * 256 + 256
                        ]
        wait_bytes(fsend.at[pl.ds(0, NP - 1)], fs.at[0])

        for h in range(2):

            @pl.loop(1, NT)
            def _(o):
                d = lax.rem(t + o, NT)
                remote(vsend.at[h], agb.at[step, h, t], gs.at[h], gr.at[step, h], (d, p)).start()

            agb[step, h, t] = vsend[h]

        @pl.when(step == 0)
        def _():
            build_amp()
            loads[5].wait()
            @pl.loop(0, 8)
            def _(n):
                q = n // 4
                cols = pl.ds(pl.multiple_of(lax.rem(n, 4) * 128, 128), 128)
                for y in range(NY):
                    rows = loc_v[q, :, y, cols]
                    for c in range(2):
                        index = (2 * sub + c) % 8
                        for i in range(2):
                            pair = [
                                jnp.take_along_axis(rows[16 * i + 8 * j : 16 * i + 8 * j + 8], index, axis=0)
                                for j in range(2)
                            ]
                            lr[q, y, pl.ds(16 * c + 8 * i, 8), cols] = jnp.where(sub < 4, pair[0], pair[1])

        for h in range(2):
            wait_bytes(agb.at[step, h, pl.ds(0, NT - 1)], gr.at[step, h])

            @pl.loop(0, 4)
            def _(a):
                cols = pl.ds(pl.multiple_of(a * 128, 128), 128)

                def weight(q, ky):
                    return amp[q, ky, pl.ds(8 * h, 8), cols]

                def store(q, ri, y, value):
                    w[q, ri, y, :, cols] = value

                y_stage(
                    [agb[step, h, y // 2, y % 2, 0, :, cols] for y in range(16)],
                    [agb[step, h, y // 2, y % 2, 1, :, cols] for y in range(16)],
                    weight,
                    store,
                )

            if h == 0:

                @pl.when(p == 8)
                def _():
                    @pl.loop(0, 4)
                    def _(a):
                        cols = pl.ds(pl.multiple_of(a * 128, 128), 128)
                        far = pl.ds(pl.multiple_of((3 - a) * 128, 128), 128)
                        near = pl.ds(pl.multiple_of(lax.rem(4 - a, 4) * 128, 128), 128)
                        index = (128 - lane) % 128

                        def load(y, ri):
                            v0 = jnp.take_along_axis(agb[step, 0, y // 2, y % 2, ri, :, near], index, axis=1)
                            v1 = jnp.take_along_axis(agb[step, 0, y // 2, y % 2, ri, :, far], index, axis=1)
                            return jnp.where(lane == 0, v0, v1)

                        def weight(q, ky):
                            return bmp[q, ky, :, cols]

                        def store(q, ri, y, value):
                            w[q, ri, y, :, cols] += value

                        y_stage(
                            [load(y, 0) for y in range(16)],
                            [-load(y, 1) for y in range(16)],
                            weight,
                            store,
                        )

            @pl.loop(0, 2)
            def _(q):
                low = [w[q, ri, :, :, pl.ds(0, 256)].reshape(128, 256) for ri in range(2)]
                high = [w[q, ri, :, :, pl.ds(256, 256)].reshape(128, 256) for ri in range(2)]
                for c in range(2):
                    mix = [(lo + hi) if c == 0 else (lo - hi) for lo, hi in zip(low, high)]
                    lhs = split(jnp.concatenate(mix, axis=1))
                    xo[c] = dot3(lhs, (xt[c, 0], xt[c, 1]), 1, 0).reshape(16, 8, 512)

                @pl.loop(0, 16)
                def _(n):
                    yh = n // 4
                    ra = lax.rem(n, 4)
                    ri = ra // 2
                    first = 8 * lax.rem(ra, 2)
                    cols = pl.ds(pl.multiple_of(ra * 128, 128), 128)
                    tiles = exchange_groups([xo[i % 2, 4 * yh + i // 2, :, cols] for i in range(8)])
                    for i in range(8):
                        snd[h, first + i, yh, q, ri] = tiles[i]

            if h == 0:

                @pl.loop(1, NP)
                def _(o):
                    d = lax.rem(p + o, NP)
                    remote(snd.at[0, d], rcv.at[step, 0, p], as0.at[0], ar0.at[step], (t, d)).start()

            else:

                @pl.loop(0, 4)
                def _(i):
                    yh = lax.rem(t // 2 + 1 + i, 4)

                    @pl.loop(1, NP)
                    def _(o):
                        d = lax.rem(p + o, NP)
                        remote(
                            snd.at[1, d, yh], rcv.at[step, 1, p, yh], as1.at[0], ar1.at[step, yh], (t, d)
                        ).start()

            rcv[step, h, p] = snd[h, p]

        for h in range(2):
            wait_bytes(agb.at[step, h, pl.ds(0, NT - 1)], gs.at[h])

        wait_bytes(rcv.at[step, 0, pl.ds(0, NP - 1)], ar0.at[step])

        @pl.loop(0, 4)
        def _(i):
            yh = lax.rem(t // 2 + 1 + i, 4)
            wait_bytes(rcv.at[step, 1, pl.ds(0, NP - 1), yh], ar1.at[step, yh])
            total = None
            for q in range(2):
                d = jnp.concatenate(
                    [rcv[step, h, :, yh, q].reshape(256, 128) for h in range(2)], axis=0
                )
                field = dot3(split(d), (zt[0], zt[1]), 0, 0)
                field = field * lr[q, pl.ds(4 * yh, 4)].reshape(128, 512)
                total = field if total is None else total + field
            psend[pl.ds(2 * yh, 2)] = total.reshape(2, 64, 512)
            for j in range(2):
                d = 2 * yh + j

                @pl.when(d != t)
                def _():
                    remote(psend.at[d], rsr.at[step, t], rs.at[0], rr.at[step], (d, p)).start()

        wait_bytes(snd.at[0, pl.ds(0, NP - 1)], as0.at[0])
        wait_bytes(snd.at[1, pl.ds(0, NP - 1)], as1.at[0])
        rsr[step, t] = psend[t]
        wait_bytes(rsr.at[step, pl.ds(0, NT - 1)], rr.at[step])
        wait_bytes(psend.at[pl.ds(0, NT - 1)], rs.at[0])
        total = rsr[step, 0]
        for i in range(1, NT):
            total = total + rsr[step, i]
        advanced = SCALE * total - prev[...]
        dose[...] = dose[...] + advanced * advanced
        prev[...] = cur[...]
        cur[...] = advanced

    for y in range(2):
        for x in range(XR):
            row = y * XR + (x % 2) * 16 + x // 2
            final_o[x, pl.ds(y, 1), :] = cur[pl.ds(row, 1), :]
            dose_o[x, pl.ds(y, 1), :] = dose[pl.ds(row, 1), :]


def wave(pres, prior, loc, spec):
    brick = jax.ShapeDtypeStruct((XR, 2, NZ), F32)
    any_spec = pl.BlockSpec(memory_space=pl.ANY)
    vmem_spec = pl.BlockSpec(memory_space=pltpu.VMEM)
    scratch = [
        pltpu.VMEM((XR, NY, NZ), F32),
        pltpu.VMEM((XR, NY, NZ), F32),
        pltpu.VMEM((2, XR, NY, NZ), F32),
        pltpu.VMEM((2, NY, XR, NZ), F32),
        pltpu.VMEM((2, NY, 32, NX), F32),
        pltpu.VMEM((2, NY, 16, NX), F32),
        pltpu.VMEM((32, 1, NX), F32),
        pltpu.VMEM((32, 1, NX), F32),
        pltpu.VMEM((2, NY, 16, NX), F32),
        pltpu.VMEM((2, NY, 8, NX), F32),
        pltpu.VMEM((2, NZ, NZ), BF16),
        pltpu.VMEM((2, 2, NX, NX), BF16),
        pltpu.VMEM((64, NZ), F32),
        pltpu.VMEM((64, NZ), F32),
        pltpu.VMEM((64, NZ), F32),
        pltpu.VMEM((NP, 16, 128), F32),
        pltpu.VMEM((2, NP, 16, 128), F32),
        pltpu.VMEM((2, 2, 2, 8, NX), F32),
        pltpu.VMEM((2, 2, NT, 2, 2, 8, NX), F32),
        pltpu.VMEM((2, 2, NY, 8, NX), F32),
        pltpu.VMEM((2, NY, 8, NX), F32),
        pltpu.VMEM((2, NP, 4, 2, 2, 8, 128), F32),
        pltpu.VMEM((2, 2, NP, 4, 2, 2, 8, 128), F32),
        pltpu.VMEM((NT, 64, NZ), F32),
        pltpu.VMEM((2, NT, 64, NZ), F32),
        pltpu.SemaphoreType.DMA((6,)),
        pltpu.SemaphoreType.DMA((1,)),
        pltpu.SemaphoreType.DMA((4,)),
        pltpu.SemaphoreType.DMA((1,)),
        pltpu.SemaphoreType.DMA((2,)),
        pltpu.SemaphoreType.DMA((2,)),
        pltpu.SemaphoreType.DMA((2, 2)),
        pltpu.SemaphoreType.DMA((1,)),
        pltpu.SemaphoreType.DMA((2,)),
        pltpu.SemaphoreType.DMA((1,)),
        pltpu.SemaphoreType.DMA((2, 4)),
        pltpu.SemaphoreType.DMA((1,)),
        pltpu.SemaphoreType.DMA((2,)),
    ]
    return pl.pallas_call(
        wave_kernel,
        name="wave",
        out_shape=(brick, brick),
        in_specs=[any_spec] * 6,
        out_specs=(vmem_spec, vmem_spec),
        scratch_shapes=scratch,
        compiler_params=pltpu.CompilerParams(
            collective_id=0, has_side_effects=True, vmem_limit_bytes=60 * 2**20
        ),
    )(pres, prior, loc, spec, jnp.asarray(z_table()), jnp.asarray(x_table()))


def padded_2(block, sides, width):
    for axis, dim in sides:
        count = lax.axis_size(axis)
        forward = [(i, i + 1) for i in range(count - 1)]
        backward = [(target, source) for source, target in forward]
        low = lax.ppermute(
            lax.slice_in_dim(block, block.shape[dim] - width, None, axis=dim), axis, forward
        )
        high = lax.ppermute(lax.slice_in_dim(block, 0, width, axis=dim), axis, backward)
        block = jnp.concatenate([low, block, high], axis=dim)
    return block


def stencil_sum(padded):
    center = padded[1:-1, 1:-1, :]
    depth_pad = jnp.pad(center, ((0, 0), (0, 0), (1, 1)))
    near_sum = padded[2:, 1:-1, :] + padded[:-2, 1:-1, :]
    near_sum = near_sum + padded[1:-1, 2:, :] + padded[1:-1, :-2, :]
    near_sum = near_sum + depth_pad[:, :, 2:] + depth_pad[:, :, :-2]
    return (center, near_sum)


def heat_update(center, near_sum, perfuse, source):
    return center + DIFFUSION * (near_sum - 6.0 * center) - perfuse * center + source


def on_device(
    present_acoustic,
    prior_acoustic,
    location_factor,
    spectral_multiplier,
    medium_kinds,
    organ_properties,
    thermal_increase,
):
    final_brick, dose_sum = wave(present_acoustic, prior_acoustic, location_factor, spectral_multiplier)
    absorb = jnp.where(
        medium_kinds == 0,
        organ_properties[0, 0],
        jnp.where(medium_kinds == 1, organ_properties[1, 0], organ_properties[2, 0]),
    )
    perfuse = jnp.where(
        medium_kinds == 0,
        organ_properties[0, 1],
        jnp.where(medium_kinds == 1, organ_properties[1, 1], organ_properties[2, 1]),
    )
    source = absorb * dose_sum
    present_thermal = thermal_increase
    for _ in range(HEAT_STEPS):
        padded = padded_2(present_thermal, (("term", 1), ("pencil", 0)), 1)
        center, near_sum = stencil_sum(padded)
        present_thermal = heat_update(center, near_sum, perfuse, source)
    return (final_brick, present_thermal)


def solution(mesh):
    return jax.shard_map(
        on_device,
        mesh=mesh,
        in_specs=(
            P("pencil", None, None),
            P("pencil", None, None),
            P("term", "pencil", None, None),
            P("term", None, "pencil", None),
            P("pencil", "term", None),
            P(),
            P("pencil", "term", None),
        ),
        out_specs=(P("pencil", "term", None), P("pencil", "term", None)),
        check_vma=False,
    )
```

```python
import math

import numpy as np

import jax
import jax.numpy as jnp
from jax import lax
from jax.experimental import pallas as pl
from jax.experimental.pallas import tpu as pltpu
from jax.sharding import PartitionSpec as P

WAVE_STEPS = 2
DIFFUSION = 0.125
MESH = pl.DeviceIdType.MESH
F32 = jnp.float32
BF16 = jnp.bfloat16

NX = 512
NY = 16
NZ = 512
NT = 8
NP = 16
XR = NX // NP
SCALE = 2.0 / (NX * NY * NZ)


def high_low(table):
    high = table.astype(BF16)
    low = (table - high.astype(np.float32)).astype(BF16)
    return np.stack([high, low])


def z_table():
    rows = np.zeros((2, NP, 2, 8, NZ), np.float64)
    z = np.arange(NZ)
    for h in range(2):
        for p in range(NP):
            for i in range(8):
                s = 8 * h + i
                if s == 0 and p == 8:
                    rows[h, p, 0, i] = 1.0
                    rows[h, p, 1, i] = 1.0 - 2.0 * (z % 2)
                    continue
                kz = 32 * p + s
                if s == 0 and p < 8:
                    kz = 32 * p + 16
                angle = 2.0 * math.pi * ((kz * z) % NZ) / NZ
                rows[h, p, 0, i] = np.cos(angle)
                rows[h, p, 1, i] = -np.sin(angle)
    return high_low(rows.reshape(NZ, NZ).astype(np.float32))


def x_table():
    k = np.arange(256)[:, None]
    tables = []
    for c in range(2):
        x = 2 * np.arange(256)[None, :] + c
        angle = 2.0 * math.pi * ((k * x) % NX) / NX
        co, si = np.cos(angle), np.sin(angle)
        tables.append(high_low(np.block([[co, si], [-si, co]]).astype(np.float32)))
    return np.stack(tables)


def split(x):
    high = x.astype(BF16)
    low = (x - high.astype(F32)).astype(BF16)
    return high, low


def dot(a, b, ca, cb):
    return lax.dot_general(a, b, (((ca,), (cb,)), ((), ())), preferred_element_type=F32)


def dot3(a, b, ca, cb):
    return dot(a[0], b[0], ca, cb) + dot(a[0], b[1], ca, cb) + dot(a[1], b[0], ca, cb)


def fft16(re, im, sign):
    n = len(re)
    if n == 1:
        return re, im
    er, ei = fft16(re[0::2], im[0::2], sign)
    orr, oi = fft16(re[1::2], im[1::2], sign)
    half = n // 2
    out_r, out_i = [None] * n, [None] * n
    for k in range(half):
        angle = sign * 2.0 * math.pi * k / n
        c, s = math.cos(angle), math.sin(angle)
        a, b = orr[k], oi[k]
        if k == 0:
            tr, ti = a, b
        elif 4 * k == n:
            tr, ti = (b, -a) if sign < 0 else (-b, a)
        elif abs(abs(c) - abs(s)) < 1e-12:
            r = math.sqrt(0.5)
            sc, ss = math.copysign(1.0, c), math.copysign(1.0, s)
            tr = r * ((a if sc > 0 else -a) - (b if ss > 0 else -b))
            ti = r * ((b if sc > 0 else -b) + (a if ss > 0 else -a))
        else:
            tr = c * a - s * b
            ti = c * b + s * a
        out_r[k], out_i[k] = er[k] + tr, ei[k] + ti
        out_r[k + half], out_i[k + half] = er[k] - tr, ei[k] - ti
    return out_r, out_i


def exchange_groups(tiles):
    rows = tiles[0].shape[0]
    lane = lax.broadcasted_iota(jnp.int32, (rows, 128), 1)
    tiles = list(tiles)
    for bit in (4, 2, 1):
        width = bit * 16
        keep_low = (lane % (2 * width)) < width
        new = list(tiles)
        for i in range(8):
            if i & bit:
                continue
            a, b = tiles[i], tiles[i + bit]
            new[i] = jnp.where(keep_low, a, pltpu.roll(b, width, 1))
            new[i + bit] = jnp.where(keep_low, pltpu.roll(a, 128 - width, 1), b)
        tiles = new
    return tiles


def reverse_lanes(tiles):
    lane = lax.broadcasted_iota(jnp.int32, (8, 128), 1)
    index = (128 - lane) % 128
    moved = [jnp.take_along_axis(x, index, axis=1) for x in tiles]
    return [jnp.where(lane == 0, moved[(4 - a) % 4], moved[3 - a]) for a in range(4)]


def wave_kernel(
    pres, prior, loc, spec, ztab, xtab, kinds, thermal, props, final_o, heat_o,
    pres_v, prior_v, loc_v, lr, spec_v, srecv, row0, row0r, amp, bmp, zt, xt,
    kind_v, heat_v, absorb, perfuse, heat, field, hxs, hx, hy,
    cur, prev, dose, fsend, frecv, vsend, agb, w, xo, snd, rcv, psend, rsr,
    lsem, ssem, sx, fs, fr, gs, gr, as0, ar0, as1, ar1, rs, rr, hs, hr,
):
    t = lax.axis_index("term")
    p = lax.axis_index("pencil")

    barrier = pltpu.get_barrier_semaphore()

    @pl.loop(1, NP)
    def _(o):
        pl.semaphore_signal(barrier, inc=1, device_id=(t, lax.rem(p + o, NP)), device_id_type=MESH)

    @pl.loop(1, NT)
    def _(o):
        pl.semaphore_signal(barrier, inc=1, device_id=(lax.rem(t + o, NT), p), device_id_type=MESH)

    loads = [
        pltpu.make_async_copy(src, dst, lsem.at[i])
        for i, (src, dst) in enumerate(
            [(pres, pres_v), (ztab, zt), (xtab, xt), (spec, spec_v), (prior, prior_v), (loc, loc_v), (kinds, kind_v), (thermal, heat_v)]
        )
    ]
    for load in loads:
        load.start()

    pl.semaphore_wait(barrier, NP + NT - 2)

    def remote(src, dst, send, recv, device):
        return pltpu.make_async_remote_copy(
            src_ref=src, dst_ref=dst, send_sem=send, recv_sem=recv, device_id=device, device_id_type=MESH
        )

    mirror = (t, NP - 1 - p)
    swap = remote(spec.at[:, :, pl.ds(16, 16), :], srecv, sx.at[0], sx.at[1], mirror)
    swap.start()

    loads[0].wait()
    for y in range(2):
        for x in range(XR):
            row = y * XR + (x % 2) * 16 + x // 2
            cur[pl.ds(row, 1), :] = pres_v[x, pl.ds(2 * t + y, 1), :]
    loads[3].wait()
    for q in range(2):
        row0[pl.ds(16 * q, 16), 0, :] = spec_v[q, :, 0, :]
    give = jnp.where(p == 0, 8, lax.rem(NP - p, NP))
    rowcopy = remote(row0, row0r, sx.at[2], sx.at[3], (t, give))

    @pl.when(p < 8)
    def _():
        rowcopy.start()

    loads[4].wait()
    for y in range(2):
        for x in range(XR):
            row = y * XR + (x % 2) * 16 + x // 2
            prev[pl.ds(row, 1), :] = prior_v[x, pl.ds(2 * t + y, 1), :]
    dose[...] = jnp.zeros_like(dose)
    loads[1].wait()
    loads[2].wait()

    lane = lax.broadcasted_iota(jnp.int32, (8, 128), 1)
    sub = lax.broadcasted_iota(jnp.int32, (8, 128), 0)
    flip = (8 - sub) % 8

    edges = [
        (t > 0, (t - 1, p)),
        (t < NT - 1, (t + 1, p)),
        (p > 0, (t, p - 1)),
        (p < NP - 1, (t, p + 1)),
    ]

    def halo_copy(k, e):
        if e < 2:
            src, dst = field.at[k, pl.ds(32 * e, 32)], hy.at[k, 1 - e]
        else:
            src, dst = hxs.at[k, e - 2], hx.at[k, 3 - e]
        return remote(src, dst, hs.at[k, e], hr.at[k, 1 - e if e < 2 else 5 - e], edges[e][1])

    def halo_start(k):
        for y in range(2):
            hxs[k, 0, pl.ds(y, 1), :] = field[k, pl.ds(32 * y, 1), :]
            hxs[k, 1, pl.ds(y, 1), :] = field[k, pl.ds(32 * y + 31, 1), :]
        for e in range(4):

            @pl.when(edges[e][0])
            def _():
                halo_copy(k, e).start()

            @pl.when(jnp.logical_not(edges[e][0]))
            def _():
                if e < 2:
                    hy[k, e] = jnp.zeros((32, NZ), F32)
                else:
                    hx[k, e - 2] = jnp.zeros((2, NZ), F32)

    def halo_wait(k):
        for e in range(4):

            @pl.when(edges[e][0])
            def _():
                halo_copy(k, e).wait_send()
                ref = hy.at[k, e] if e < 2 else hx.at[k, e - 2]
                pltpu.make_async_copy(ref, ref, hr.at[k, e]).wait()

    row16 = lax.broadcasted_iota(jnp.int32, (16, NZ), 0)
    col16 = lax.broadcasted_iota(jnp.int32, (16, NZ), 1)

    def heat_apply(k, y, c):
        mine = field[k, pl.ds(32 * y + 16 * c, 16), :]
        other = field[k, pl.ds(32 * y + 16 * (1 - c), 16), :]
        if c == 0:
            shifted = jnp.where(row16 == 0, hx[k, 0, pl.ds(y, 1), :], pltpu.roll(other, 1, 0))
        else:
            shifted = jnp.where(row16 == 15, hx[k, 1, pl.ds(y, 1), :], pltpu.roll(other, 15, 0))
        near = other + shifted
        near = near + field[k, pl.ds(32 * (1 - y) + 16 * c, 16), :] + hy[k, y, pl.ds(16 * c, 16), :]
        near = near + jnp.where(col16 == 0, 0.0, pltpu.roll(mine, 1, 1))
        near = near + jnp.where(col16 == NZ - 1, 0.0, pltpu.roll(mine, NZ - 1, 1))
        rows = pl.ds(32 * y + 16 * c, 16)
        return mine + DIFFUSION * (near - 6.0 * mine) - perfuse[rows, :] * mine

    def heat_begin():
        loads[6].wait()
        loads[7].wait()
        for y in range(2):
            for x in range(XR):
                row = y * XR + (x % 2) * 16 + x // 2
                field[0, pl.ds(row, 1), :] = heat_v[x, pl.ds(y, 1), :]
                kind = kind_v[x, pl.ds(y, 1), :]
                for ref, j in ((absorb, 0), (perfuse, 1)):
                    ref[pl.ds(row, 1), :] = jnp.where(
                        kind == 0, props[0, j], jnp.where(kind == 1, props[1, j], props[2, j])
                    )
        halo_start(0)

    def heat_middle():
        halo_wait(0)
        for y in range(2):
            for c in range(2):
                field[1, pl.ds(32 * y + 16 * c, 16), :] = heat_apply(0, y, c)
        halo_start(1)

    def heat_late():
        halo_wait(1)
        for y in range(2):
            for c in range(2):
                heat[pl.ds(32 * y + 16 * c, 16), :] = heat_apply(1, y, c)

    def heat_finish():
        field[2] = absorb[...] * dose[...]
        halo_start(2)
        halo_wait(2)
        for y in range(2):
            for c in range(2):
                rows = pl.ds(32 * y + 16 * c, 16)
                heat[rows, :] = heat[rows, :] + (field[2, rows, :] + heat_apply(2, y, c))

    def build_amp():
        swap.wait()

        @pl.when(p < 8)
        def _():
            rowcopy.wait_send()

        @pl.when(p >= 8)
        def _():
            rowcopy.wait_recv()

        low_p = jnp.where(p < 8, 1, 0)

        @pl.loop(0, 32)
        def _(n):
            q = n // 16
            ky = lax.rem(n, 16)
            kr = lax.rem(16 - ky, 16)
            pick_own = (sub == 0) & (low_p == 1)
            pick_row = (sub == 0) & (low_p == 0)
            mirrored = [[], []]
            for a in range(4):
                cols = pl.ds(128 * a, 128)
                r0 = srecv[q, kr, pl.ds(0, 8), cols]
                r1 = srecv[q, kr, pl.ds(8, 8), cols]
                extra = jnp.broadcast_to(row0r[16 * q + kr, :, cols], (8, 128))
                f0 = jnp.take_along_axis(r0, flip, axis=0)
                f1 = jnp.take_along_axis(r1, flip, axis=0)
                m0 = jnp.where(sub == 0, r0, f1)
                m0 = jnp.where(pick_row, extra, m0)
                m1 = jnp.where(sub == 0, r1, f0)
                mirrored[0].append(m0)
                mirrored[1].append(m1)
            for h in range(2):
                rev = reverse_lanes(mirrored[h])
                for a in range(4):
                    cols = pl.ds(128 * a, 128)
                    own = spec_v[q, ky, pl.ds(8 * h, 8), cols]
                    if h == 0:
                        own = jnp.where(pick_own, spec_v[q, ky, pl.ds(16, 8), cols], own)
                    amp[q, ky, pl.ds(8 * h, 8), cols] = own + rev[a]

        @pl.when(p == 8)
        def _():
            @pl.loop(0, 32)
            def _(n):
                q = n // 16
                ky = lax.rem(n, 16)
                kr = lax.rem(16 - ky, 16)
                own_r, zero_r = [], []
                for a in range(4):
                    cols = pl.ds(128 * a, 128)
                    own_r.append(spec_v[q, kr, pl.ds(0, 8), cols])
                    zero_r.append(jnp.broadcast_to(row0r[16 * q + kr, :, cols], (8, 128)))
                own_r = reverse_lanes(own_r)
                zero_r = reverse_lanes(zero_r)
                for a in range(4):
                    cols = pl.ds(128 * a, 128)
                    last = spec_v[q, ky, pl.ds(0, 8), cols] + own_r[a]
                    first = jnp.broadcast_to(row0r[16 * q + ky, :, cols], (8, 128)) + zero_r[a]
                    old = amp[q, ky, pl.ds(0, 8), cols]
                    amp[q, ky, pl.ds(0, 8), cols] = jnp.where(sub == 0, 0.25 * (first + last), old)
                    bmp[q, ky, :, cols] = jnp.where(sub == 0, 0.25 * (first - last), 0.0)

    def y_stage(re, im, weight, store):
        re, im = fft16(re, im, -1)
        for q in range(2):
            wr, wi = [], []
            for ky in range(16):
                m = weight(q, ky)
                wr.append(m * re[ky])
                wi.append(m * im[ky])
            wr, wi = fft16(wr, wi, 1)
            for y in range(16):
                store(q, 0, y, wr[y])
                store(q, 1, y, wi[y])

    def wait_bytes(ref, sem):
        pltpu.make_async_copy(ref, ref, sem).wait()

    @pl.loop(0, WAVE_STEPS)
    def _(step):
        b = split(cur[...])
        b = tuple(jnp.concatenate([v, v], axis=0) for v in b)
        out = dot3((zt[0], zt[1]), b, 1, 1).reshape(2, NP, 2, 8, 128)
        wide = lax.broadcasted_iota(jnp.int32, (NP, 8, 128), 2)
        for h in range(2):
            fsend[:, pl.ds(8 * h, 8), :] = jnp.where(wide < 64, out[h, :, 0], out[h, :, 1])

        @pl.loop(1, NP)
        def _(o):
            d = lax.rem(p + o, NP)
            remote(fsend.at[d], frecv.at[step, p], fs.at[0], fr.at[step], (t, d)).start()

        frecv[step, p] = fsend[p]
        wait_bytes(frecv.at[step, pl.ds(0, NP - 1)], fr.at[step])

        groups = [exchange_groups([frecv[step, 8 * a + i] for i in range(8)]) for a in range(2)]
        parts = []
        for c in range(2):
            rows = [
                jnp.concatenate(
                    [groups[0][y * 2 + c], groups[1][y * 2 + c], groups[0][4 + y * 2 + c], groups[1][4 + y * 2 + c]],
                    axis=1,
                )
                for y in range(2)
            ]
            lhs = split(jnp.concatenate(rows, axis=0))
            parts.append(dot3(lhs, (xt[c, 0], xt[c, 1]), 1, 1))
        for lo, v in ((0, parts[0] + parts[1]), (256, parts[0] - parts[1])):
            for h in range(2):
                for y in range(2):
                    for ri in range(2):
                        vsend[h, y, ri, :, pl.ds(lo, 256)] = v[
                            y * 16 + 8 * h : y * 16 + 8 * h + 8, ri * 256 : ri * 256 + 256
                        ]
        wait_bytes(fsend.at[pl.ds(0, NP - 1)], fs.at[0])

        for h in range(2):

            @pl.loop(1, NT)
            def _(o):
                d = lax.rem(t + o, NT)
                remote(vsend.at[h], agb.at[step, h, t], gs.at[h], gr.at[step, h], (d, p)).start()

            agb[step, h, t] = vsend[h]

        @pl.when(step == 0)
        def _():
            heat_begin()
            heat_middle()
            heat_late()
            build_amp()
            loads[5].wait()
            @pl.loop(0, 8)
            def _(n):
                q = n // 4
                cols = pl.ds(pl.multiple_of(lax.rem(n, 4) * 128, 128), 128)
                for y in range(NY):
                    rows = loc_v[q, :, y, cols]
                    for c in range(2):
                        index = (2 * sub + c) % 8
                        for i in range(2):
                            pair = [
                                jnp.take_along_axis(rows[16 * i + 8 * j : 16 * i + 8 * j + 8], index, axis=0)
                                for j in range(2)
                            ]
                            lr[q, y, pl.ds(16 * c + 8 * i, 8), cols] = jnp.where(sub < 4, pair[0], pair[1])

        for h in range(2):
            wait_bytes(agb.at[step, h, pl.ds(0, NT - 1)], gr.at[step, h])

            @pl.loop(0, 4)
            def _(a):
                cols = pl.ds(pl.multiple_of(a * 128, 128), 128)

                def weight(q, ky):
                    return amp[q, ky, pl.ds(8 * h, 8), cols]

                def store(q, ri, y, value):
                    w[q, ri, y, :, cols] = value

                y_stage(
                    [agb[step, h, y // 2, y % 2, 0, :, cols] for y in range(16)],
                    [agb[step, h, y // 2, y % 2, 1, :, cols] for y in range(16)],
                    weight,
                    store,
                )

            if h == 0:

                @pl.when(p == 8)
                def _():
                    @pl.loop(0, 4)
                    def _(a):
                        cols = pl.ds(pl.multiple_of(a * 128, 128), 128)
                        far = pl.ds(pl.multiple_of((3 - a) * 128, 128), 128)
                        near = pl.ds(pl.multiple_of(lax.rem(4 - a, 4) * 128, 128), 128)
                        index = (128 - lane) % 128

                        def load(y, ri):
                            v0 = jnp.take_along_axis(agb[step, 0, y // 2, y % 2, ri, :, near], index, axis=1)
                            v1 = jnp.take_along_axis(agb[step, 0, y // 2, y % 2, ri, :, far], index, axis=1)
                            return jnp.where(lane == 0, v0, v1)

                        def weight(q, ky):
                            return bmp[q, ky, :, cols]

                        def store(q, ri, y, value):
                            w[q, ri, y, :, cols] += value

                        y_stage(
                            [load(y, 0) for y in range(16)],
                            [-load(y, 1) for y in range(16)],
                            weight,
                            store,
                        )

            @pl.loop(0, 2)
            def _(q):
                low = [w[q, ri, :, :, pl.ds(0, 256)].reshape(128, 256) for ri in range(2)]
                high = [w[q, ri, :, :, pl.ds(256, 256)].reshape(128, 256) for ri in range(2)]
                for c in range(2):
                    mix = [(lo + hi) if c == 0 else (lo - hi) for lo, hi in zip(low, high)]
                    lhs = split(jnp.concatenate(mix, axis=1))
                    xo[c] = dot3(lhs, (xt[c, 0], xt[c, 1]), 1, 0).reshape(16, 8, 512)

                @pl.loop(0, 16)
                def _(n):
                    yh = n // 4
                    ra = lax.rem(n, 4)
                    ri = ra // 2
                    first = 8 * lax.rem(ra, 2)
                    cols = pl.ds(pl.multiple_of(ra * 128, 128), 128)
                    tiles = exchange_groups([xo[i % 2, 4 * yh + i // 2, :, cols] for i in range(8)])
                    for i in range(8):
                        snd[h, first + i, yh, q, ri] = tiles[i]

            if h == 0:

                @pl.loop(1, NP)
                def _(o):
                    d = lax.rem(p + o, NP)
                    remote(snd.at[0, d], rcv.at[step, 0, p], as0.at[0], ar0.at[step], (t, d)).start()

            else:

                @pl.loop(0, 4)
                def _(i):
                    yh = lax.rem(t // 2 + 1 + i, 4)

                    @pl.loop(1, NP)
                    def _(o):
                        d = lax.rem(p + o, NP)
                        remote(
                            snd.at[1, d, yh], rcv.at[step, 1, p, yh], as1.at[0], ar1.at[step, yh], (t, d)
                        ).start()

            rcv[step, h, p] = snd[h, p]

        for h in range(2):
            wait_bytes(agb.at[step, h, pl.ds(0, NT - 1)], gs.at[h])

        wait_bytes(rcv.at[step, 0, pl.ds(0, NP - 1)], ar0.at[step])

        @pl.loop(0, 4)
        def _(i):
            yh = lax.rem(t // 2 + 1 + i, 4)
            wait_bytes(rcv.at[step, 1, pl.ds(0, NP - 1), yh], ar1.at[step, yh])
            total = None
            for q in range(2):
                d = jnp.concatenate(
                    [rcv[step, h, :, yh, q].reshape(256, 128) for h in range(2)], axis=0
                )
                field = dot3(split(d), (zt[0], zt[1]), 0, 0)
                field = field * lr[q, pl.ds(4 * yh, 4)].reshape(128, 512)
                total = field if total is None else total + field
            psend[pl.ds(2 * yh, 2)] = total.reshape(2, 64, 512)
            for j in range(2):
                d = 2 * yh + j

                @pl.when(d != t)
                def _():
                    remote(psend.at[d], rsr.at[step, t], rs.at[0], rr.at[step], (d, p)).start()

        wait_bytes(snd.at[0, pl.ds(0, NP - 1)], as0.at[0])
        wait_bytes(snd.at[1, pl.ds(0, NP - 1)], as1.at[0])
        rsr[step, t] = psend[t]
        wait_bytes(rsr.at[step, pl.ds(0, NT - 1)], rr.at[step])
        wait_bytes(psend.at[pl.ds(0, NT - 1)], rs.at[0])
        total = rsr[step, 0]
        for i in range(1, NT):
            total = total + rsr[step, i]
        advanced = SCALE * total - prev[...]
        dose[...] = dose[...] + advanced * advanced
        prev[...] = cur[...]
        cur[...] = advanced

    heat_finish()
    for y in range(2):
        for x in range(XR):
            row = y * XR + (x % 2) * 16 + x // 2
            final_o[x, pl.ds(y, 1), :] = cur[pl.ds(row, 1), :]
            heat_o[x, pl.ds(y, 1), :] = heat[pl.ds(row, 1), :]


def wave(pres, prior, loc, spec, kinds, props, thermal):
    brick = jax.ShapeDtypeStruct((XR, 2, NZ), F32)
    any_spec = pl.BlockSpec(memory_space=pl.ANY)
    vmem_spec = pl.BlockSpec(memory_space=pltpu.VMEM)
    scratch = [
        pltpu.VMEM((XR, NY, NZ), F32),
        pltpu.VMEM((XR, NY, NZ), F32),
        pltpu.VMEM((2, XR, NY, NZ), F32),
        pltpu.VMEM((2, NY, XR, NZ), F32),
        pltpu.VMEM((2, NY, 32, NX), F32),
        pltpu.VMEM((2, NY, 16, NX), F32),
        pltpu.VMEM((32, 1, NX), F32),
        pltpu.VMEM((32, 1, NX), F32),
        pltpu.VMEM((2, NY, 16, NX), F32),
        pltpu.VMEM((2, NY, 8, NX), F32),
        pltpu.VMEM((2, NZ, NZ), BF16),
        pltpu.VMEM((2, 2, NX, NX), BF16),
        pltpu.VMEM((XR, 2, NZ), jnp.int32),
        pltpu.VMEM((XR, 2, NZ), F32),
        pltpu.VMEM((64, NZ), F32),
        pltpu.VMEM((64, NZ), F32),
        pltpu.VMEM((64, NZ), F32),
        pltpu.VMEM((3, 64, NZ), F32),
        pltpu.VMEM((3, 2, 2, NZ), F32),
        pltpu.VMEM((3, 2, 2, NZ), F32),
        pltpu.VMEM((3, 2, 32, NZ), F32),
        pltpu.VMEM((64, NZ), F32),
        pltpu.VMEM((64, NZ), F32),
        pltpu.VMEM((64, NZ), F32),
        pltpu.VMEM((NP, 16, 128), F32),
        pltpu.VMEM((2, NP, 16, 128), F32),
        pltpu.VMEM((2, 2, 2, 8, NX), F32),
        pltpu.VMEM((2, 2, NT, 2, 2, 8, NX), F32),
        pltpu.VMEM((2, 2, NY, 8, NX), F32),
        pltpu.VMEM((2, NY, 8, NX), F32),
        pltpu.VMEM((2, NP, 4, 2, 2, 8, 128), F32),
        pltpu.VMEM((2, 2, NP, 4, 2, 2, 8, 128), F32),
        pltpu.VMEM((NT, 64, NZ), F32),
        pltpu.VMEM((2, NT, 64, NZ), F32),
        pltpu.SemaphoreType.DMA((8,)),
        pltpu.SemaphoreType.DMA((1,)),
        pltpu.SemaphoreType.DMA((4,)),
        pltpu.SemaphoreType.DMA((1,)),
        pltpu.SemaphoreType.DMA((2,)),
        pltpu.SemaphoreType.DMA((2,)),
        pltpu.SemaphoreType.DMA((2, 2)),
        pltpu.SemaphoreType.DMA((1,)),
        pltpu.SemaphoreType.DMA((2,)),
        pltpu.SemaphoreType.DMA((1,)),
        pltpu.SemaphoreType.DMA((2, 4)),
        pltpu.SemaphoreType.DMA((1,)),
        pltpu.SemaphoreType.DMA((2,)),
        pltpu.SemaphoreType.DMA((3, 4)),
        pltpu.SemaphoreType.DMA((3, 4)),
    ]
    return pl.pallas_call(
        wave_kernel,
        name="wave",
        out_shape=(brick, brick),
        in_specs=[any_spec] * 8 + [pl.BlockSpec(memory_space=pltpu.SMEM)],
        out_specs=(vmem_spec, vmem_spec),
        scratch_shapes=scratch,
        compiler_params=pltpu.CompilerParams(
            collective_id=0, has_side_effects=True, vmem_limit_bytes=60 * 2**20
        ),
    )(pres, prior, loc, spec, jnp.asarray(z_table()), jnp.asarray(x_table()), kinds, thermal, props)


def solution(mesh):
    return jax.shard_map(
        wave,
        mesh=mesh,
        in_specs=(
            P("pencil", None, None),
            P("pencil", None, None),
            P("term", "pencil", None, None),
            P("term", None, "pencil", None),
            P("pencil", "term", None),
            P(),
            P("pencil", "term", None),
        ),
        out_specs=(P("pencil", "term", None), P("pencil", "term", None)),
        check_vma=False,
    )
```

```python
import math

import numpy as np

import jax
import jax.numpy as jnp
from jax import lax
from jax.experimental import pallas as pl
from jax.experimental.pallas import tpu as pltpu
from jax.sharding import PartitionSpec as P

WAVE_STEPS = 2
DIFFUSION = 0.125
MESH = pl.DeviceIdType.MESH
F32 = jnp.float32
BF16 = jnp.bfloat16

NX = 512
NY = 16
NZ = 512
NT = 8
NP = 16
XR = NX // NP
SCALE = 2.0 / (NX * NY * NZ)


PENCIL_ORDER = (
    (1, 0, 0), (0, 1, 0), (3, 1, 1), (2, 0, 0), (0, 1, 1), (1, 1, 0), (3, 0, 0), (2, 1, 1),
    (1, 0, 1), (3, 1, 0), (2, 0, 1), (2, 1, 0), (3, 0, 1), (1, 1, 1), (0, 0, 1),
)
TERM_ORDER = ((1, 0), (0, 1), (3, 1), (2, 0), (3, 0), (1, 1), (2, 1))


def high_low(table):
    high = table.astype(BF16)
    low = (table - high.astype(np.float32)).astype(BF16)
    return np.stack([high, low])


def z_table():
    rows = np.zeros((2, NP, 2, 8, NZ), np.float64)
    z = np.arange(NZ)
    for h in range(2):
        for p in range(NP):
            for i in range(8):
                if h == 1 and i == 0 and p == 8:
                    rows[h, p, 0, i] = 1.0
                    rows[h, p, 1, i] = 1.0 - 2.0 * (z % 2)
                    continue
                j = 8 * h + i
                if i == 0:
                    j = 8 if h == 0 else (16 if p < 8 else 0)
                kz = 32 * p + j
                angle = 2.0 * math.pi * ((kz * z) % NZ) / NZ
                rows[h, p, 0, i] = np.cos(angle)
                rows[h, p, 1, i] = -np.sin(angle)
    return high_low(rows.reshape(NZ, NZ).astype(np.float32))


def x_table():
    k = np.arange(256)[:, None]
    tables = []
    for c in range(2):
        x = 2 * np.arange(256)[None, :] + c
        angle = 2.0 * math.pi * ((k * x) % NX) / NX
        co, si = np.cos(angle), np.sin(angle)
        tables.append(high_low(np.block([[co, si], [-si, co]]).astype(np.float32)))
    return np.stack(tables)


def split(x):
    high = x.astype(BF16)
    low = (x - high.astype(F32)).astype(BF16)
    return high, low


def dot(a, b, ca, cb):
    return lax.dot_general(a, b, (((ca,), (cb,)), ((), ())), preferred_element_type=F32)


def dot3(a, b, ca, cb):
    return dot(a[0], b[0], ca, cb) + dot(a[0], b[1], ca, cb) + dot(a[1], b[0], ca, cb)


def fft16(re, im, sign):
    n = len(re)
    if n == 1:
        return re, im
    er, ei = fft16(re[0::2], im[0::2], sign)
    orr, oi = fft16(re[1::2], im[1::2], sign)
    half = n // 2
    out_r, out_i = [None] * n, [None] * n
    for k in range(half):
        angle = sign * 2.0 * math.pi * k / n
        c, s = math.cos(angle), math.sin(angle)
        a, b = orr[k], oi[k]
        if k == 0:
            tr, ti = a, b
        elif 4 * k == n:
            tr, ti = (b, -a) if sign < 0 else (-b, a)
        elif abs(abs(c) - abs(s)) < 1e-12:
            r = math.sqrt(0.5)
            sc, ss = math.copysign(1.0, c), math.copysign(1.0, s)
            tr = r * ((a if sc > 0 else -a) - (b if ss > 0 else -b))
            ti = r * ((b if sc > 0 else -b) + (a if ss > 0 else -a))
        else:
            tr = c * a - s * b
            ti = c * b + s * a
        out_r[k], out_i[k] = er[k] + tr, ei[k] + ti
        out_r[k + half], out_i[k + half] = er[k] - tr, ei[k] - ti
    return out_r, out_i


def exchange_groups(tiles):
    rows = tiles[0].shape[0]
    lane = lax.broadcasted_iota(jnp.int32, (rows, 128), 1)
    tiles = list(tiles)
    for bit in (4, 2, 1):
        width = bit * 16
        keep_low = (lane % (2 * width)) < width
        new = list(tiles)
        for i in range(8):
            if i & bit:
                continue
            a, b = tiles[i], tiles[i + bit]
            new[i] = jnp.where(keep_low, a, pltpu.roll(b, width, 1))
            new[i + bit] = jnp.where(keep_low, pltpu.roll(a, 128 - width, 1), b)
        tiles = new
    return tiles


def reverse_lanes(tiles):
    lane = lax.broadcasted_iota(jnp.int32, (8, 128), 1)
    index = (128 - lane) % 128
    moved = [jnp.take_along_axis(x, index, axis=1) for x in tiles]
    return [jnp.where(lane == 0, moved[(4 - a) % 4], moved[3 - a]) for a in range(4)]


def wave_kernel(
    pres, prior, loc, spec, ztab, xtab, kinds, thermal, props, final_o, heat_o,
    pres_v, prior_v, loc_v, lr, spec_v, srecv, row0, row0r, amp, bmp, zt, xt,
    kind_v, heat_v, absorb, perfuse, heat, field, hxs, hx, hy,
    cur, prev, dose, fsend, frecv, vsend, agb, w, xo, snd, rcv, psend, rsr,
    lsem, sx, fs, fr, gs, gr, as0, ar0, as1, ar1, rs, rr, hs, hr,
):
    t = lax.axis_index("term")
    p = lax.axis_index("pencil")

    barrier = pltpu.get_barrier_semaphore()

    @pl.loop(1, NP)
    def _(o):
        pl.semaphore_signal(barrier, inc=1, device_id=(t, lax.rem(p + o, NP)), device_id_type=MESH)

    @pl.loop(1, NT)
    def _(o):
        pl.semaphore_signal(barrier, inc=1, device_id=(lax.rem(t + o, NT), p), device_id_type=MESH)

    loads = [
        pltpu.make_async_copy(src, dst, lsem.at[i])
        for i, (src, dst) in enumerate(
            [
                (pres, pres_v), (ztab, zt), (thermal, heat_v), (kinds, kind_v),
                (spec, spec_v), (xtab, xt), (prior, prior_v), (loc, loc_v),
            ]
        )
    ]
    for load in loads:
        load.start()

    def remote(src, dst, send, recv, device):
        return pltpu.make_async_remote_copy(
            src_ref=src, dst_ref=dst, send_sem=send, recv_sem=recv, device_id=device, device_id_type=MESH
        )

    def pencil_peers():
        for dx, dy, dc in PENCIL_ORDER:
            yield (
                lax.rem(p // 4 + dx, 4) * 4 + lax.rem(lax.rem(p // 2, 2) + dy, 2) * 2 + lax.rem(lax.rem(p, 2) + dc, 2)
            )

    def term_peers():
        for dz, dy in TERM_ORDER:
            yield lax.rem(t // 2 + dz, 4) * 2 + lax.rem(lax.rem(t, 2) + dy, 2)

    mirror = (t, NP - 1 - p)
    swaps = [
        remote(spec.at[:, :, pl.ds(24 - 8 * h, 8), :], srecv.at[h], sx.at[h], sx.at[2 + h], mirror)
        for h in range(2)
    ]
    give = jnp.where(p == 0, 8, lax.rem(NP - p, NP))
    rowcopy = remote(row0, row0r, sx.at[4], sx.at[5], (t, give))

    lane = lax.broadcasted_iota(jnp.int32, (8, 128), 1)
    sub = lax.broadcasted_iota(jnp.int32, (8, 128), 0)
    flip = (8 - sub) % 8

    edges = [
        (t > 0, (t - 1, p)),
        (t < NT - 1, (t + 1, p)),
        (p > 0, (t, p - 1)),
        (p < NP - 1, (t, p + 1)),
    ]

    def halo_copy(k, e):
        if e < 2:
            src, dst = field.at[k, pl.ds(32 * e, 32)], hy.at[k, 1 - e]
        else:
            src, dst = hxs.at[k, e - 2], hx.at[k, 3 - e]
        return remote(src, dst, hs.at[k, e], hr.at[k, 1 - e if e < 2 else 5 - e], edges[e][1])

    def halo_start(k):
        for y in range(2):
            hxs[k, 0, pl.ds(y, 1), :] = field[k, pl.ds(32 * y, 1), :]
            hxs[k, 1, pl.ds(y, 1), :] = field[k, pl.ds(32 * y + 31, 1), :]
        for e in range(4):

            @pl.when(edges[e][0])
            def _():
                halo_copy(k, e).start()

            @pl.when(jnp.logical_not(edges[e][0]))
            def _():
                if e < 2:
                    hy[k, e] = jnp.zeros((32, NZ), F32)
                else:
                    hx[k, e - 2] = jnp.zeros((2, NZ), F32)

    def halo_wait(k):
        for e in range(4):

            @pl.when(edges[e][0])
            def _():
                halo_copy(k, e).wait_send()
                ref = hy.at[k, e] if e < 2 else hx.at[k, e - 2]
                pltpu.make_async_copy(ref, ref, hr.at[k, e]).wait()

    row16 = lax.broadcasted_iota(jnp.int32, (16, NZ), 0)
    col16 = lax.broadcasted_iota(jnp.int32, (16, NZ), 1)

    def heat_apply(k, y, c):
        mine = field[k, pl.ds(32 * y + 16 * c, 16), :]
        other = field[k, pl.ds(32 * y + 16 * (1 - c), 16), :]
        if c == 0:
            shifted = jnp.where(row16 == 0, hx[k, 0, pl.ds(y, 1), :], pltpu.roll(other, 1, 0))
        else:
            shifted = jnp.where(row16 == 15, hx[k, 1, pl.ds(y, 1), :], pltpu.roll(other, 15, 0))
        near = other + shifted
        near = near + field[k, pl.ds(32 * (1 - y) + 16 * c, 16), :] + hy[k, y, pl.ds(16 * c, 16), :]
        near = near + jnp.where(col16 == 0, 0.0, pltpu.roll(mine, 1, 1))
        near = near + jnp.where(col16 == NZ - 1, 0.0, pltpu.roll(mine, NZ - 1, 1))
        rows = pl.ds(32 * y + 16 * c, 16)
        return mine + DIFFUSION * (near - 6.0 * mine) - perfuse[rows, :] * mine

    def heat_begin():
        loads[2].wait()
        for y in range(2):
            for x in range(XR):
                row = y * XR + (x % 2) * 16 + x // 2
                field[0, pl.ds(row, 1), :] = heat_v[x, pl.ds(y, 1), :]

    def heat_coefficients():
        loads[3].wait()
        for y in range(2):
            for x in range(XR):
                row = y * XR + (x % 2) * 16 + x // 2
                kind = kind_v[x, pl.ds(y, 1), :]
                for ref, j in ((absorb, 0), (perfuse, 1)):
                    ref[pl.ds(row, 1), :] = jnp.where(
                        kind == 0, props[0, j], jnp.where(kind == 1, props[1, j], props[2, j])
                    )

    def heat_middle():
        halo_wait(0)
        for y in range(2):
            for c in range(2):
                field[1, pl.ds(32 * y + 16 * c, 16), :] = heat_apply(0, y, c)
        halo_start(1)

    def heat_late():
        halo_wait(1)
        for y in range(2):
            for c in range(2):
                heat[pl.ds(32 * y + 16 * c, 16), :] = heat_apply(1, y, c)

    def heat_finish():
        field[2] = absorb[...] * dose[...]
        halo_start(2)
        for y in range(2):
            for x in range(XR):
                row = y * XR + (x % 2) * 16 + x // 2
                final_o[x, pl.ds(y, 1), :] = cur[pl.ds(row, 1), :]
        halo_wait(2)
        for y in range(2):
            for c in range(2):
                rows = pl.ds(32 * y + 16 * c, 16)
                heat[rows, :] = heat[rows, :] + (field[2, rows, :] + heat_apply(2, y, c))

    def build_amp(h):
        swaps[h].wait()
        if h == 1:

            @pl.when(p < 8)
            def _():
                rowcopy.wait_send()

            @pl.when(p >= 8)
            def _():
                rowcopy.wait_recv()

        low_p = jnp.where(p < 8, 1, 0)
        special = pl.multiple_of(16 * low_p, 8)

        @pl.loop(0, 32)
        def _(n):
            q = n // 16
            ky = lax.rem(n, 16)
            kr = lax.rem(16 - ky, 16)
            pick_row = (sub == 0) & (low_p == 0)
            mirrored = []
            for a in range(4):
                cols = pl.ds(128 * a, 128)
                m = jnp.take_along_axis(srecv[h, q, kr, :, cols], flip, axis=0)
                if h == 1:
                    extra = jnp.broadcast_to(row0r[16 * q + kr, :, cols], (8, 128))
                    m = jnp.where(pick_row, extra, m)
                mirrored.append(m)
            mirrored = reverse_lanes(mirrored)
            for a in range(4):
                cols = pl.ds(128 * a, 128)
                if h == 0:
                    first, rest = spec_v[q, ky, pl.ds(8, 8), cols], spec_v[q, ky, pl.ds(0, 8), cols]
                else:
                    first, rest = spec_v[q, ky, pl.ds(special, 8), cols], spec_v[q, ky, pl.ds(8, 8), cols]
                amp[q, ky, pl.ds(8 * h, 8), cols] = jnp.where(sub == 0, first, rest) + mirrored[a]

        if h == 0:
            return

        @pl.when(p == 8)
        def _():
            @pl.loop(0, 32)
            def _(n):
                q = n // 16
                ky = lax.rem(n, 16)
                kr = lax.rem(16 - ky, 16)
                own_r, zero_r = [], []
                for a in range(4):
                    cols = pl.ds(128 * a, 128)
                    own_r.append(spec_v[q, kr, pl.ds(0, 8), cols])
                    zero_r.append(jnp.broadcast_to(row0r[16 * q + kr, :, cols], (8, 128)))
                own_r = reverse_lanes(own_r)
                zero_r = reverse_lanes(zero_r)
                for a in range(4):
                    cols = pl.ds(128 * a, 128)
                    last = spec_v[q, ky, pl.ds(0, 8), cols] + own_r[a]
                    first = jnp.broadcast_to(row0r[16 * q + ky, :, cols], (8, 128)) + zero_r[a]
                    old = amp[q, ky, pl.ds(8, 8), cols]
                    amp[q, ky, pl.ds(8, 8), cols] = jnp.where(sub == 0, 0.25 * (first + last), old)
                    bmp[q, ky, :, cols] = jnp.where(sub == 0, 0.25 * (first - last), 0.0)

    def y_stage(re, im, weight, store):
        re, im = fft16(re, im, -1)
        for q in range(2):
            wr, wi = [], []
            for ky in range(16):
                m = weight(q, ky)
                wr.append(m * re[ky])
                wi.append(m * im[ky])
            wr, wi = fft16(wr, wi, 1)
            for y in range(16):
                store(q, 0, y, wr[y])
                store(q, 1, y, wi[y])

    def wait_bytes(ref, sem):
        pltpu.make_async_copy(ref, ref, sem).wait()

    def forward_z():
        b = split(cur[...])
        b = tuple(jnp.concatenate([v, v], axis=0) for v in b)
        out = dot3((zt[0], zt[1]), b, 1, 1).reshape(2, NP, 2, 8, 128)
        wide = lax.broadcasted_iota(jnp.int32, (NP, 8, 128), 2)
        for h in range(2):
            fsend[:, pl.ds(8 * h, 8), :] = jnp.where(wide < 64, out[h, :, 0], out[h, :, 1])

    def forward_send(step):
        for d in pencil_peers():
            remote(fsend.at[d], frecv.at[step, p], fs.at[0], fr.at[step], (t, d)).start()

    loads[0].wait()
    for y in range(2):
        for x in range(XR):
            row = y * XR + (x % 2) * 16 + x // 2
            cur[pl.ds(row, 1), :] = pres_v[x, pl.ds(2 * t + y, 1), :]
    loads[1].wait()
    forward_z()
    heat_begin()
    loads[4].wait()
    for q in range(2):
        row0[pl.ds(16 * q, 16), 0, :] = spec_v[q, :, 0, :]

    pl.semaphore_wait(barrier, NP + NT - 2)
    forward_send(0)
    halo_start(0)

    @pl.when(p < 8)
    def _():
        rowcopy.start()

    for swap in swaps:
        swap.start()
    loads[5].wait()

    @pl.loop(0, WAVE_STEPS)
    def _(step):
        frecv[step, p] = fsend[p]
        wait_bytes(frecv.at[step, pl.ds(0, NP - 1)], fr.at[step])

        groups = [exchange_groups([frecv[step, 8 * a + i] for i in range(8)]) for a in range(2)]
        parts = []
        for c in range(2):
            rows = [
                jnp.concatenate(
                    [groups[0][y * 2 + c], groups[1][y * 2 + c], groups[0][4 + y * 2 + c], groups[1][4 + y * 2 + c]],
                    axis=1,
                )
                for y in range(2)
            ]
            lhs = split(jnp.concatenate(rows, axis=0))
            parts.append(dot3(lhs, (xt[c, 0], xt[c, 1]), 1, 1))
        for lo, v in ((0, parts[0] + parts[1]), (256, parts[0] - parts[1])):
            for h in range(2):
                for y in range(2):
                    for ri in range(2):
                        vsend[h, y, ri, :, pl.ds(lo, 256)] = v[
                            y * 16 + 8 * h : y * 16 + 8 * h + 8, ri * 256 : ri * 256 + 256
                        ]
        wait_bytes(fsend.at[pl.ds(0, NP - 1)], fs.at[0])

        for h in range(2):

            for d in term_peers():
                remote(vsend.at[h], agb.at[step, h, t], gs.at[h], gr.at[step, h], (d, p)).start()

            agb[step, h, t] = vsend[h]

        @pl.when(step == 0)
        def _():
            loads[6].wait()
            for y in range(2):
                for x in range(XR):
                    row = y * XR + (x % 2) * 16 + x // 2
                    prev[pl.ds(row, 1), :] = prior_v[x, pl.ds(2 * t + y, 1), :]
            dose[...] = jnp.zeros_like(dose)
            heat_coefficients()
            heat_middle()
            loads[7].wait()
            @pl.loop(0, 8)
            def _(n):
                q = n // 4
                cols = pl.ds(pl.multiple_of(lax.rem(n, 4) * 128, 128), 128)
                for y in range(NY):
                    rows = loc_v[q, :, y, cols]
                    for c in range(2):
                        index = (2 * sub + c) % 8
                        for i in range(2):
                            pair = [
                                jnp.take_along_axis(rows[16 * i + 8 * j : 16 * i + 8 * j + 8], index, axis=0)
                                for j in range(2)
                            ]
                            lr[q, y, pl.ds(16 * c + 8 * i, 8), cols] = jnp.where(sub < 4, pair[0], pair[1])

        for h in range(2):

            @pl.when(step == 0)
            def _():
                build_amp(h)

            wait_bytes(agb.at[step, h, pl.ds(0, NT - 1)], gr.at[step, h])

            @pl.loop(0, 4)
            def _(a):
                cols = pl.ds(pl.multiple_of(a * 128, 128), 128)

                def weight(q, ky):
                    return amp[q, ky, pl.ds(8 * h, 8), cols]

                def store(q, ri, y, value):
                    w[q, ri, y, :, cols] = value

                y_stage(
                    [agb[step, h, y // 2, y % 2, 0, :, cols] for y in range(16)],
                    [agb[step, h, y // 2, y % 2, 1, :, cols] for y in range(16)],
                    weight,
                    store,
                )

            if h == 1:

                @pl.when(p == 8)
                def _():
                    @pl.loop(0, 4)
                    def _(a):
                        cols = pl.ds(pl.multiple_of(a * 128, 128), 128)
                        far = pl.ds(pl.multiple_of((3 - a) * 128, 128), 128)
                        near = pl.ds(pl.multiple_of(lax.rem(4 - a, 4) * 128, 128), 128)
                        index = (128 - lane) % 128

                        def load(y, ri):
                            v0 = jnp.take_along_axis(agb[step, 1, y // 2, y % 2, ri, :, near], index, axis=1)
                            v1 = jnp.take_along_axis(agb[step, 1, y // 2, y % 2, ri, :, far], index, axis=1)
                            return jnp.where(lane == 0, v0, v1)

                        def weight(q, ky):
                            return bmp[q, ky, :, cols]

                        def store(q, ri, y, value):
                            w[q, ri, y, :, cols] += value

                        y_stage(
                            [load(y, 0) for y in range(16)],
                            [-load(y, 1) for y in range(16)],
                            weight,
                            store,
                        )

            @pl.loop(0, 2)
            def _(q):
                low = [w[q, ri, :, :, pl.ds(0, 256)].reshape(128, 256) for ri in range(2)]
                high = [w[q, ri, :, :, pl.ds(256, 256)].reshape(128, 256) for ri in range(2)]
                for c in range(2):
                    mix = [(lo + hi) if c == 0 else (lo - hi) for lo, hi in zip(low, high)]
                    lhs = split(jnp.concatenate(mix, axis=1))
                    xo[c] = dot3(lhs, (xt[c, 0], xt[c, 1]), 1, 0).reshape(16, 8, 512)

                @pl.loop(0, 16)
                def _(n):
                    yh = n // 4
                    ra = lax.rem(n, 4)
                    ri = ra // 2
                    first = 8 * lax.rem(ra, 2)
                    cols = pl.ds(pl.multiple_of(ra * 128, 128), 128)
                    tiles = exchange_groups([xo[i % 2, 4 * yh + i // 2, :, cols] for i in range(8)])
                    for i in range(8):
                        snd[h, first + i, q, yh, ri] = tiles[i]

                if h == 0:
                    for d in pencil_peers():
                        remote(
                            snd.at[0, d, q], rcv.at[step, 0, p, q], as0.at[0], ar0.at[step], (t, d)
                        ).start()

            if h == 1:

                @pl.loop(0, 4)
                def _(i):
                    yh = lax.rem(t // 2 + 1 + i, 4)
                    for d in pencil_peers():
                        remote(
                            snd.at[1, d, :, yh], rcv.at[step, 1, p, :, yh], as1.at[0], ar1.at[step, yh], (t, d)
                        ).start()

            rcv[step, h, p] = snd[h, p]

        for h in range(2):
            wait_bytes(agb.at[step, h, pl.ds(0, NT - 1)], gs.at[h])

        @pl.when(step == 1)
        def _():
            heat_late()

        wait_bytes(rcv.at[step, 0, pl.ds(0, NP - 1)], ar0.at[step])

        @pl.loop(0, 4)
        def _(i):
            yh = lax.rem(t // 2 + 1 + i, 4)
            wait_bytes(rcv.at[step, 1, pl.ds(0, NP - 1), :, yh], ar1.at[step, yh])
            total = None
            for q in range(2):
                d = jnp.concatenate(
                    [rcv[step, h, :, q, yh].reshape(256, 128) for h in range(2)], axis=0
                )
                field = dot3(split(d), (zt[0], zt[1]), 0, 0)
                field = field * lr[q, pl.ds(4 * yh, 4)].reshape(128, 512)
                total = field if total is None else total + field
            psend[pl.ds(2 * yh, 2)] = total.reshape(2, 64, 512)
            for j in range(2):
                d = 2 * yh + j

                @pl.when(d != t)
                def _():
                    remote(psend.at[d], rsr.at[step, t], rs.at[0], rr.at[step], (d, p)).start()

        wait_bytes(snd.at[0, pl.ds(0, NP - 1)], as0.at[0])
        wait_bytes(snd.at[1, pl.ds(0, NP - 1)], as1.at[0])
        rsr[step, t] = psend[t]
        wait_bytes(rsr.at[step, pl.ds(0, NT - 1)], rr.at[step])
        wait_bytes(psend.at[pl.ds(0, NT - 1)], rs.at[0])
        total = rsr[step, 0]
        for i in range(1, NT):
            total = total + rsr[step, i]
        advanced = SCALE * total - prev[...]
        dose[...] = dose[...] + advanced * advanced
        prev[...] = cur[...]
        cur[...] = advanced

        @pl.when(step == 0)
        def _():
            forward_z()
            forward_send(1)

    heat_finish()
    for y in range(2):
        for x in range(XR):
            row = y * XR + (x % 2) * 16 + x // 2
            heat_o[x, pl.ds(y, 1), :] = heat[pl.ds(row, 1), :]


def wave(pres, prior, loc, spec, kinds, props, thermal):
    brick = jax.ShapeDtypeStruct((XR, 2, NZ), F32)
    any_spec = pl.BlockSpec(memory_space=pl.ANY)
    vmem_spec = pl.BlockSpec(memory_space=pltpu.VMEM)
    scratch = [
        pltpu.VMEM((XR, NY, NZ), F32),
        pltpu.VMEM((XR, NY, NZ), F32),
        pltpu.VMEM((2, XR, NY, NZ), F32),
        pltpu.VMEM((2, NY, XR, NZ), F32),
        pltpu.VMEM((2, NY, 32, NX), F32),
        pltpu.VMEM((2, 2, NY, 8, NX), F32),
        pltpu.VMEM((32, 1, NX), F32),
        pltpu.VMEM((32, 1, NX), F32),
        pltpu.VMEM((2, NY, 16, NX), F32),
        pltpu.VMEM((2, NY, 8, NX), F32),
        pltpu.VMEM((2, NZ, NZ), BF16),
        pltpu.VMEM((2, 2, NX, NX), BF16),
        pltpu.VMEM((XR, 2, NZ), jnp.int32),
        pltpu.VMEM((XR, 2, NZ), F32),
        pltpu.VMEM((64, NZ), F32),
        pltpu.VMEM((64, NZ), F32),
        pltpu.VMEM((64, NZ), F32),
        pltpu.VMEM((3, 64, NZ), F32),
        pltpu.VMEM((3, 2, 2, NZ), F32),
        pltpu.VMEM((3, 2, 2, NZ), F32),
        pltpu.VMEM((3, 2, 32, NZ), F32),
        pltpu.VMEM((64, NZ), F32),
        pltpu.VMEM((64, NZ), F32),
        pltpu.VMEM((64, NZ), F32),
        pltpu.VMEM((NP, 16, 128), F32),
        pltpu.VMEM((2, NP, 16, 128), F32),
        pltpu.VMEM((2, 2, 2, 8, NX), F32),
        pltpu.VMEM((2, 2, NT, 2, 2, 8, NX), F32),
        pltpu.VMEM((2, 2, NY, 8, NX), F32),
        pltpu.VMEM((2, NY, 8, NX), F32),
        pltpu.VMEM((2, NP, 2, 4, 2, 8, 128), F32),
        pltpu.VMEM((2, 2, NP, 2, 4, 2, 8, 128), F32),
        pltpu.VMEM((NT, 64, NZ), F32),
        pltpu.VMEM((2, NT, 64, NZ), F32),
        pltpu.SemaphoreType.DMA((8,)),
        pltpu.SemaphoreType.DMA((6,)),
        pltpu.SemaphoreType.DMA((1,)),
        pltpu.SemaphoreType.DMA((2,)),
        pltpu.SemaphoreType.DMA((2,)),
        pltpu.SemaphoreType.DMA((2, 2)),
        pltpu.SemaphoreType.DMA((1,)),
        pltpu.SemaphoreType.DMA((2,)),
        pltpu.SemaphoreType.DMA((1,)),
        pltpu.SemaphoreType.DMA((2, 4)),
        pltpu.SemaphoreType.DMA((1,)),
        pltpu.SemaphoreType.DMA((2,)),
        pltpu.SemaphoreType.DMA((3, 4)),
        pltpu.SemaphoreType.DMA((3, 4)),
    ]
    return pl.pallas_call(
        wave_kernel,
        name="wave",
        out_shape=(brick, brick),
        in_specs=[any_spec] * 8 + [pl.BlockSpec(memory_space=pltpu.SMEM)],
        out_specs=(vmem_spec, vmem_spec),
        scratch_shapes=scratch,
        compiler_params=pltpu.CompilerParams(
            collective_id=0, has_side_effects=True, vmem_limit_bytes=60 * 2**20
        ),
    )(pres, prior, loc, spec, jnp.asarray(z_table()), jnp.asarray(x_table()), kinds, thermal, props)


def solution(mesh):
    return jax.shard_map(
        wave,
        mesh=mesh,
        in_specs=(
            P("pencil", None, None),
            P("pencil", None, None),
            P("term", "pencil", None, None),
            P("term", None, "pencil", None),
            P("pencil", "term", None),
            P(),
            P("pencil", "term", None),
        ),
        out_specs=(P("pencil", "term", None), P("pencil", "term", None)),
        check_vma=False,
    )
```

```python
import math

import numpy as np

import jax
import jax.numpy as jnp
from jax import lax
from jax.experimental import pallas as pl
from jax.experimental.pallas import tpu as pltpu
from jax.sharding import PartitionSpec as P

WAVE_STEPS = 2
DIFFUSION = 0.125
MESH = pl.DeviceIdType.MESH
F32 = jnp.float32
BF16 = jnp.bfloat16

NX = 512
NY = 16
NZ = 512
NT = 8
NP = 16
XR = NX // NP
SCALE = 2.0 / (NX * NY * NZ)


PENCIL_ORDER = (
    (1, 0, 0), (0, 1, 0), (3, 1, 1), (2, 0, 0), (0, 1, 1), (1, 1, 0), (3, 0, 0), (2, 1, 1),
    (1, 0, 1), (3, 1, 0), (2, 0, 1), (2, 1, 0), (3, 0, 1), (1, 1, 1), (0, 0, 1),
)


TERM_ORDER = ((2, 0), (0, 1), (1, 1), (3, 1), (1, 0), (3, 0), (2, 1))


def high_low(table):
    high = table.astype(BF16)
    low = (table - high.astype(np.float32)).astype(BF16)
    return np.stack([high, low])


def z_table():
    rows = np.zeros((2, NP, 2, 8, NZ), np.float64)
    z = np.arange(NZ)
    for h in range(2):
        for p in range(NP):
            for i in range(8):
                if h == 1 and i == 0 and p == 8:
                    rows[h, p, 0, i] = 1.0
                    rows[h, p, 1, i] = 1.0 - 2.0 * (z % 2)
                    continue
                j = 8 * h + i
                if i == 0:
                    j = 8 if h == 0 else (16 if p < 8 else 0)
                kz = 32 * p + j
                angle = 2.0 * math.pi * ((kz * z) % NZ) / NZ
                rows[h, p, 0, i] = np.cos(angle)
                rows[h, p, 1, i] = -np.sin(angle)
    return high_low(rows.reshape(NZ, NZ).astype(np.float32))


def x_table():
    k = np.arange(256)[:, None]
    tables = []
    for c in range(2):
        x = 2 * np.arange(256)[None, :] + c
        angle = 2.0 * math.pi * ((k * x) % NX) / NX
        co, si = np.cos(angle), np.sin(angle)
        tables.append(high_low(np.block([[co, si], [-si, co]]).astype(np.float32)))
    return np.stack(tables)


def split(x):
    high = x.astype(BF16)
    low = (x - high.astype(F32)).astype(BF16)
    return high, low


def dot(a, b, ca, cb):
    return lax.dot_general(a, b, (((ca,), (cb,)), ((), ())), preferred_element_type=F32)


def dot3(a, b, ca, cb):
    return dot(a[0], b[0], ca, cb) + dot(a[0], b[1], ca, cb) + dot(a[1], b[0], ca, cb)


def fft16(re, im, sign):
    n = len(re)
    if n == 1:
        return re, im
    er, ei = fft16(re[0::2], im[0::2], sign)
    orr, oi = fft16(re[1::2], im[1::2], sign)
    half = n // 2
    out_r, out_i = [None] * n, [None] * n
    for k in range(half):
        angle = sign * 2.0 * math.pi * k / n
        c, s = math.cos(angle), math.sin(angle)
        a, b = orr[k], oi[k]
        if k == 0:
            tr, ti = a, b
        elif 4 * k == n:
            tr, ti = (b, -a) if sign < 0 else (-b, a)
        elif abs(abs(c) - abs(s)) < 1e-12:
            r = math.sqrt(0.5)
            sc, ss = math.copysign(1.0, c), math.copysign(1.0, s)
            tr = r * ((a if sc > 0 else -a) - (b if ss > 0 else -b))
            ti = r * ((b if sc > 0 else -b) + (a if ss > 0 else -a))
        else:
            tr = c * a - s * b
            ti = c * b + s * a
        out_r[k], out_i[k] = er[k] + tr, ei[k] + ti
        out_r[k + half], out_i[k + half] = er[k] - tr, ei[k] - ti
    return out_r, out_i


def exchange_groups(tiles):
    rows = tiles[0].shape[0]
    lane = lax.broadcasted_iota(jnp.int32, (rows, 128), 1)
    tiles = list(tiles)
    for bit in (4, 2, 1):
        width = bit * 16
        keep_low = (lane % (2 * width)) < width
        new = list(tiles)
        for i in range(8):
            if i & bit:
                continue
            a, b = tiles[i], tiles[i + bit]
            new[i] = jnp.where(keep_low, a, pltpu.roll(b, width, 1))
            new[i + bit] = jnp.where(keep_low, pltpu.roll(a, 128 - width, 1), b)
        tiles = new
    return tiles


def reverse_lanes(tiles):
    lane = lax.broadcasted_iota(jnp.int32, (8, 128), 1)
    index = (128 - lane) % 128
    moved = [jnp.take_along_axis(x, index, axis=1) for x in tiles]
    return [jnp.where(lane == 0, moved[(4 - a) % 4], moved[3 - a]) for a in range(4)]


def wave_kernel(
    pres, prior, loc, spec, ztab, xtab, kinds, thermal, props, final_o, heat_o,
    pres_v, prior_v, loc_v, lr, spec_v, srecv, row0, row0r, amp, bmp, zt, xt,
    kind_v, heat_v, absorb, perfuse, heat, field, hxs, hx, hy,
    cur, prev, dose, fsend, frecv, vsend, agb, w, xo, snd, rcv, psend, rsr, psum, ptake,
    lsem, sx, fs, fr, gs, gr, gy, sent, came, rs, rr, ps, pr, hs, hr,
):
    t = lax.axis_index("term")
    p = lax.axis_index("pencil")

    barrier = pltpu.get_barrier_semaphore()

    @pl.loop(1, NP)
    def _(o):
        pl.semaphore_signal(barrier, inc=1, device_id=(t, lax.rem(p + o, NP)), device_id_type=MESH)

    @pl.loop(1, NT)
    def _(o):
        pl.semaphore_signal(barrier, inc=1, device_id=(lax.rem(t + o, NT), p), device_id_type=MESH)

    loads = [
        pltpu.make_async_copy(src, dst, lsem.at[i])
        for i, (src, dst) in enumerate(
            [
                (pres, pres_v), (ztab, zt), (thermal, heat_v), (kinds, kind_v),
                (spec, spec_v), (xtab, xt), (prior, prior_v), (loc, loc_v),
            ]
        )
    ]
    for load in loads:
        load.start()

    def remote(src, dst, send, recv, device):
        return pltpu.make_async_remote_copy(
            src_ref=src, dst_ref=dst, send_sem=send, recv_sem=recv, device_id=device, device_id_type=MESH
        )

    def pencil_peers():
        for dx, dy, dc in PENCIL_ORDER:
            yield (
                lax.rem(p // 4 + dx, 4) * 4 + lax.rem(lax.rem(p // 2, 2) + dy, 2) * 2 + lax.rem(lax.rem(p, 2) + dc, 2)
            )

    z_place, y_place = t // 2, lax.rem(t, 2)
    partner = t + 1 - 2 * y_place

    def chunk(i):
        return lax.rem(z_place + lax.rem(2 + 3 * i + 3 * (i // 2) + 2 * (i // 3), 4), 4)

    def z_peers():
        for dz in (1, 3, 2):
            yield lax.rem(z_place + dz, 4) * 2 + y_place

    mirror = (t, NP - 1 - p)
    swaps = [
        remote(spec.at[:, :, pl.ds(24 - 8 * h, 8), :], srecv.at[h], sx.at[h], sx.at[2 + h], mirror)
        for h in range(2)
    ]
    give = jnp.where(p == 0, 8, lax.rem(NP - p, NP))
    rowcopy = remote(row0, row0r, sx.at[4], sx.at[5], (t, give))

    lane = lax.broadcasted_iota(jnp.int32, (8, 128), 1)
    sub = lax.broadcasted_iota(jnp.int32, (8, 128), 0)
    flip = (8 - sub) % 8

    edges = [
        (t > 0, (t - 1, p)),
        (t < NT - 1, (t + 1, p)),
        (p > 0, (t, p - 1)),
        (p < NP - 1, (t, p + 1)),
    ]

    def halo_copy(k, e):
        if e < 2:
            src, dst = field.at[k, pl.ds(32 * e, 32)], hy.at[k, 1 - e]
        else:
            src, dst = hxs.at[k, e - 2], hx.at[k, 3 - e]
        return remote(src, dst, hs.at[k, e], hr.at[k, 1 - e if e < 2 else 5 - e], edges[e][1])

    def halo_start(k):
        for y in range(2):
            hxs[k, 0, pl.ds(y, 1), :] = field[k, pl.ds(32 * y, 1), :]
            hxs[k, 1, pl.ds(y, 1), :] = field[k, pl.ds(32 * y + 31, 1), :]
        for e in range(4):

            @pl.when(edges[e][0])
            def _():
                halo_copy(k, e).start()

            @pl.when(jnp.logical_not(edges[e][0]))
            def _():
                if e < 2:
                    hy[k, e] = jnp.zeros((32, NZ), F32)
                else:
                    hx[k, e - 2] = jnp.zeros((2, NZ), F32)

    def halo_wait(k):
        for e in range(4):

            @pl.when(edges[e][0])
            def _():
                halo_copy(k, e).wait_send()
                ref = hy.at[k, e] if e < 2 else hx.at[k, e - 2]
                pltpu.make_async_copy(ref, ref, hr.at[k, e]).wait()

    row16 = lax.broadcasted_iota(jnp.int32, (16, NZ), 0)
    col16 = lax.broadcasted_iota(jnp.int32, (16, NZ), 1)

    def heat_apply(k, y, c):
        mine = field[k, pl.ds(32 * y + 16 * c, 16), :]
        other = field[k, pl.ds(32 * y + 16 * (1 - c), 16), :]
        if c == 0:
            shifted = jnp.where(row16 == 0, hx[k, 0, pl.ds(y, 1), :], pltpu.roll(other, 1, 0))
        else:
            shifted = jnp.where(row16 == 15, hx[k, 1, pl.ds(y, 1), :], pltpu.roll(other, 15, 0))
        near = other + shifted
        near = near + field[k, pl.ds(32 * (1 - y) + 16 * c, 16), :] + hy[k, y, pl.ds(16 * c, 16), :]
        near = near + jnp.where(col16 == 0, 0.0, pltpu.roll(mine, 1, 1))
        near = near + jnp.where(col16 == NZ - 1, 0.0, pltpu.roll(mine, NZ - 1, 1))
        rows = pl.ds(32 * y + 16 * c, 16)
        return mine + DIFFUSION * (near - 6.0 * mine) - perfuse[rows, :] * mine

    def heat_begin():
        loads[2].wait()
        for y in range(2):
            for x in range(XR):
                row = y * XR + (x % 2) * 16 + x // 2
                field[0, pl.ds(row, 1), :] = heat_v[x, pl.ds(y, 1), :]

    def heat_coefficients():
        loads[3].wait()
        for y in range(2):
            for x in range(XR):
                row = y * XR + (x % 2) * 16 + x // 2
                kind = kind_v[x, pl.ds(y, 1), :]
                for ref, j in ((absorb, 0), (perfuse, 1)):
                    ref[pl.ds(row, 1), :] = jnp.where(
                        kind == 0, props[0, j], jnp.where(kind == 1, props[1, j], props[2, j])
                    )

    def heat_middle():
        halo_wait(0)
        for y in range(2):
            for c in range(2):
                field[1, pl.ds(32 * y + 16 * c, 16), :] = heat_apply(0, y, c)
        halo_start(1)

    def heat_late():
        halo_wait(1)
        for y in range(2):
            for c in range(2):
                heat[pl.ds(32 * y + 16 * c, 16), :] = heat_apply(1, y, c)

    def heat_finish():
        field[2] = absorb[...] * dose[...]
        halo_start(2)
        for y in range(2):
            for x in range(XR):
                row = y * XR + (x % 2) * 16 + x // 2
                final_o[x, pl.ds(y, 1), :] = cur[pl.ds(row, 1), :]
        halo_wait(2)
        for y in range(2):
            for c in range(2):
                rows = pl.ds(32 * y + 16 * c, 16)
                heat[rows, :] = heat[rows, :] + (field[2, rows, :] + heat_apply(2, y, c))

    def build_amp(h):
        swaps[h].wait()
        if h == 1:

            @pl.when(p < 8)
            def _():
                rowcopy.wait_send()

            @pl.when(p >= 8)
            def _():
                rowcopy.wait_recv()

        low_p = jnp.where(p < 8, 1, 0)
        special = pl.multiple_of(16 * low_p, 8)

        pick_row = (sub == 0) & (low_p == 0)

        @pl.loop(0, 8)
        def _(m4):
            for j in range(4):
                n = 4 * m4 + j
                q = n // 16
                ky = lax.rem(n, 16)
                kr = lax.rem(16 - ky, 16)
                mirrored = []
                for a in range(4):
                    cols = pl.ds(128 * a, 128)
                    m = jnp.take_along_axis(srecv[h, q, kr, :, cols], flip, axis=0)
                    if h == 1:
                        extra = jnp.broadcast_to(row0r[16 * q + kr, :, cols], (8, 128))
                        m = jnp.where(pick_row, extra, m)
                    mirrored.append(m)
                mirrored = reverse_lanes(mirrored)
                for a in range(4):
                    cols = pl.ds(128 * a, 128)
                    if h == 0:
                        first, rest = spec_v[q, ky, pl.ds(8, 8), cols], spec_v[q, ky, pl.ds(0, 8), cols]
                    else:
                        first, rest = spec_v[q, ky, pl.ds(special, 8), cols], spec_v[q, ky, pl.ds(8, 8), cols]
                    amp[q, ky, pl.ds(8 * h, 8), cols] = jnp.where(sub == 0, first, rest) + mirrored[a]

        if h == 0:
            return

        @pl.when(p == 8)
        def _():
            @pl.loop(0, 32)
            def _(n):
                q = n // 16
                ky = lax.rem(n, 16)
                kr = lax.rem(16 - ky, 16)
                own_r, zero_r = [], []
                for a in range(4):
                    cols = pl.ds(128 * a, 128)
                    own_r.append(spec_v[q, kr, pl.ds(0, 8), cols])
                    zero_r.append(jnp.broadcast_to(row0r[16 * q + kr, :, cols], (8, 128)))
                own_r = reverse_lanes(own_r)
                zero_r = reverse_lanes(zero_r)
                for a in range(4):
                    cols = pl.ds(128 * a, 128)
                    last = spec_v[q, ky, pl.ds(0, 8), cols] + own_r[a]
                    first = jnp.broadcast_to(row0r[16 * q + ky, :, cols], (8, 128)) + zero_r[a]
                    old = amp[q, ky, pl.ds(8, 8), cols]
                    amp[q, ky, pl.ds(8, 8), cols] = jnp.where(sub == 0, 0.25 * (first + last), old)
                    bmp[q, ky, :, cols] = jnp.where(sub == 0, 0.25 * (first - last), 0.0)

    def y_stage(re, im, weight, store):
        re, im = fft16(re, im, -1)
        for q in range(2):
            wr, wi = [], []
            for ky in range(16):
                m = weight(q, ky)
                wr.append(m * re[ky])
                wi.append(m * im[ky])
            wr, wi = fft16(wr, wi, 1)
            for y in range(16):
                store(q, 0, y, wr[y])
                store(q, 1, y, wi[y])

    def wait_bytes(ref, sem):
        pltpu.make_async_copy(ref, ref, sem).wait()

    def forward_z():
        b = split(cur[...])
        b = tuple(jnp.concatenate([v, v], axis=0) for v in b)
        out = dot3((zt[0], zt[1]), b, 1, 1).reshape(2, NP, 2, 8, 128)
        wide = lax.broadcasted_iota(jnp.int32, (NP, 8, 128), 2)
        for h in range(2):
            fsend[:, pl.ds(8 * h, 8), :] = jnp.where(wide < 64, out[h, :, 0], out[h, :, 1])

    def forward_send(step):
        for d in pencil_peers():
            remote(fsend.at[d], frecv.at[step, p], fs.at[0], fr.at[step], (t, d)).start()

    loads[0].wait()
    for y in range(2):
        for x in range(XR):
            row = y * XR + (x % 2) * 16 + x // 2
            cur[pl.ds(row, 1), :] = pres_v[x, pl.ds(2 * t + y, 1), :]
    loads[1].wait()
    forward_z()
    heat_begin()
    loads[4].wait()
    for q in range(2):
        row0[pl.ds(16 * q, 16), 0, :] = spec_v[q, :, 0, :]

    pl.semaphore_wait(barrier, NP + NT - 2)
    forward_send(0)
    halo_start(0)

    @pl.when(p < 8)
    def _():
        rowcopy.start()

    for swap in swaps:
        swap.start()
    loads[5].wait()

    @pl.loop(0, WAVE_STEPS)
    def _(step):
        frecv[step, p] = fsend[p]
        wait_bytes(frecv.at[step, pl.ds(0, NP - 1)], fr.at[step])

        groups = [exchange_groups([frecv[step, 8 * a + i] for i in range(8)]) for a in range(2)]
        parts = []
        for c in range(2):
            rows = [
                jnp.concatenate(
                    [groups[0][y * 2 + c], groups[1][y * 2 + c], groups[0][4 + y * 2 + c], groups[1][4 + y * 2 + c]],
                    axis=1,
                )
                for y in range(2)
            ]
            lhs = split(jnp.concatenate(rows, axis=0))
            parts.append(dot3(lhs, (xt[c, 0], xt[c, 1]), 1, 1))
        for lo, v in ((0, parts[0] + parts[1]), (256, parts[0] - parts[1])):
            for h in range(2):
                for y in range(2):
                    for ri in range(2):
                        vsend[h, y, ri, :, pl.ds(lo, 256)] = v[
                            y * 16 + 8 * h : y * 16 + 8 * h + 8, ri * 256 : ri * 256 + 256
                        ]
        wait_bytes(fsend.at[pl.ds(0, NP - 1)], fs.at[0])

        for dz, dy in TERM_ORDER:
            d = lax.rem(z_place + dz, 4) * 2 + lax.rem(y_place + dy, 2)
            remote(vsend.at[0], agb.at[step, 0, t], gs.at[0], gr.at[step, 0], (d, p)).start()
        remote(vsend.at[1], agb.at[step, 1, t], gs.at[1], gy.at[step], (partner, p)).start()
        for d in z_peers():
            remote(vsend.at[1], agb.at[step, 1, t], gs.at[1], gr.at[step, 1], (d, p)).start()
        for h in range(2):
            agb[step, h, t] = vsend[h]

        @pl.when(step == 0)
        def _():
            loads[6].wait()
            for y in range(2):
                for x in range(XR):
                    row = y * XR + (x % 2) * 16 + x // 2
                    prev[pl.ds(row, 1), :] = prior_v[x, pl.ds(2 * t + y, 1), :]
            dose[...] = jnp.zeros_like(dose)
            heat_coefficients()
            heat_middle()
            loads[7].wait()
            @pl.loop(0, 8)
            def _(n):
                q = n // 4
                cols = pl.ds(pl.multiple_of(lax.rem(n, 4) * 128, 128), 128)
                for y in range(NY):
                    rows = loc_v[q, :, y, cols]
                    for c in range(2):
                        index = (2 * sub + c) % 8
                        for i in range(2):
                            pair = [
                                jnp.take_along_axis(rows[16 * i + 8 * j : 16 * i + 8 * j + 8], index, axis=0)
                                for j in range(2)
                            ]
                            lr[q, y, pl.ds(16 * c + 8 * i, 8), cols] = jnp.where(sub < 4, pair[0], pair[1])

        for h in range(2):

            @pl.when(step == 0)
            def _():
                build_amp(h)

            wait_bytes(agb.at[step, h, pl.ds(0, NT - 1 - h)], gr.at[step, h])
            if h == 0:
                theirs = agb.at[step, 1, partner]
                wait_bytes(theirs, gy.at[step])
                for d in z_peers():
                    remote(theirs, theirs, gs.at[1], gr.at[step, 1], (d, p)).start()

            @pl.loop(0, 4)
            def _(a):
                cols = pl.ds(pl.multiple_of(a * 128, 128), 128)

                def weight(q, ky):
                    return amp[q, ky, pl.ds(8 * h, 8), cols]

                def store(q, ri, y, value):
                    w[q, ri, y, :, cols] = value

                y_stage(
                    [agb[step, h, y // 2, y % 2, 0, :, cols] for y in range(16)],
                    [agb[step, h, y // 2, y % 2, 1, :, cols] for y in range(16)],
                    weight,
                    store,
                )

            if h == 1:

                @pl.when(p == 8)
                def _():
                    @pl.loop(0, 4)
                    def _(a):
                        cols = pl.ds(pl.multiple_of(a * 128, 128), 128)
                        far = pl.ds(pl.multiple_of((3 - a) * 128, 128), 128)
                        near = pl.ds(pl.multiple_of(lax.rem(4 - a, 4) * 128, 128), 128)
                        index = (128 - lane) % 128

                        def load(y, ri):
                            v0 = jnp.take_along_axis(agb[step, 1, y // 2, y % 2, ri, :, near], index, axis=1)
                            v1 = jnp.take_along_axis(agb[step, 1, y // 2, y % 2, ri, :, far], index, axis=1)
                            return jnp.where(lane == 0, v0, v1)

                        def weight(q, ky):
                            return bmp[q, ky, :, cols]

                        def store(q, ri, y, value):
                            w[q, ri, y, :, cols] += value

                        y_stage(
                            [load(y, 0) for y in range(16)],
                            [-load(y, 1) for y in range(16)],
                            weight,
                            store,
                        )

            @pl.loop(0, 2)
            def _(q):
                low = [w[q, ri, :, :, pl.ds(0, 256)].reshape(128, 256) for ri in range(2)]
                high = [w[q, ri, :, :, pl.ds(256, 256)].reshape(128, 256) for ri in range(2)]
                for c in range(2):
                    mix = [(lo + hi) if c == 0 else (lo - hi) for lo, hi in zip(low, high)]
                    lhs = split(jnp.concatenate(mix, axis=1))
                    xo[c] = dot3(lhs, (xt[c, 0], xt[c, 1]), 1, 0).reshape(16, 8, 512)

                @pl.loop(0, 4)
                def _(ra):
                    ri = ra // 2
                    first = 8 * lax.rem(ra, 2)
                    cols = pl.ds(pl.multiple_of(ra * 128, 128), 128)
                    for yh in range(4):
                        tiles = exchange_groups([xo[i % 2, 4 * yh + i // 2, :, cols] for i in range(8)])
                        for i in range(8):
                            snd[first + i, yh, h, q, ri] = tiles[i]

            rcv[step, p, :, h] = snd[p, :, h]

            @pl.loop(0, 2)
            def _(i):
                yh = chunk(i)
                for d in pencil_peers():
                    remote(
                        snd.at[d, yh, h], rcv.at[step, p, yh, h], sent.at[0], came.at[step, yh], (t, d)
                    ).start()

        @pl.loop(2, 4)
        def _(i):
            yh = chunk(i)
            for d in pencil_peers():
                remote(snd.at[d, yh], rcv.at[step, p, yh], sent.at[0], came.at[step, yh], (t, d)).start()

        for h in range(2):
            wait_bytes(agb.at[step, h, pl.ds(0, NT - 1)], gs.at[h])

        @pl.when(step == 1)
        def _():
            heat_late()

        @pl.loop(0, 4)
        def _(i):
            yh = chunk(i)
            wait_bytes(rcv.at[step, pl.ds(0, NP - 1), yh], came.at[step, yh])
            total = None
            for q in range(2):
                d = jnp.concatenate(
                    [rcv[step, :, yh, h, q].reshape(256, 128) for h in range(2)], axis=0
                )
                field = dot3(split(d), (zt[0], zt[1]), 0, 0)
                field = field * lr[q, pl.ds(4 * yh, 4)].reshape(128, 512)
                total = field if total is None else total + field
            psend[yh] = total.reshape(2, 64, 512)

            @pl.when(yh != z_place)
            def _():
                remote(
                    psend.at[yh], rsr.at[step, z_place], rs.at[0], rr.at[step], (2 * yh + y_place, p)
                ).start()

        wait_bytes(snd.at[pl.ds(0, NP - 1)], sent.at[0])
        wait_bytes(rsr.at[step, pl.ds(0, 3)], rr.at[step])

        def z_sum(j):
            total = psend[z_place, j]
            for dz in range(1, 4):
                total = total + rsr[step, lax.rem(z_place + dz, 4), j]
            return total

        psum[...] = z_sum(1 - y_place)
        give_sum = remote(psum, ptake.at[step], ps.at[0], pr.at[step], (partner, p))
        give_sum.start()
        total = z_sum(y_place)
        wait_bytes(psend.at[pl.ds(0, 3)], rs.at[0])
        give_sum.wait_send()
        wait_bytes(ptake.at[step], pr.at[step])
        total = total + ptake[step]
        advanced = SCALE * total - prev[...]
        dose[...] = dose[...] + advanced * advanced
        prev[...] = cur[...]
        cur[...] = advanced

        @pl.when(step == 0)
        def _():
            forward_z()
            forward_send(1)

    heat_finish()
    for y in range(2):
        for x in range(XR):
            row = y * XR + (x % 2) * 16 + x // 2
            heat_o[x, pl.ds(y, 1), :] = heat[pl.ds(row, 1), :]


def wave(pres, prior, loc, spec, kinds, props, thermal):
    brick = jax.ShapeDtypeStruct((XR, 2, NZ), F32)
    any_spec = pl.BlockSpec(memory_space=pl.ANY)
    vmem_spec = pl.BlockSpec(memory_space=pltpu.VMEM)
    scratch = [
        pltpu.VMEM((XR, NY, NZ), F32),
        pltpu.VMEM((XR, NY, NZ), F32),
        pltpu.VMEM((2, XR, NY, NZ), F32),
        pltpu.VMEM((2, NY, XR, NZ), F32),
        pltpu.VMEM((2, NY, 32, NX), F32),
        pltpu.VMEM((2, 2, NY, 8, NX), F32),
        pltpu.VMEM((32, 1, NX), F32),
        pltpu.VMEM((32, 1, NX), F32),
        pltpu.VMEM((2, NY, 16, NX), F32),
        pltpu.VMEM((2, NY, 8, NX), F32),
        pltpu.VMEM((2, NZ, NZ), BF16),
        pltpu.VMEM((2, 2, NX, NX), BF16),
        pltpu.VMEM((XR, 2, NZ), jnp.int32),
        pltpu.VMEM((XR, 2, NZ), F32),
        pltpu.VMEM((64, NZ), F32),
        pltpu.VMEM((64, NZ), F32),
        pltpu.VMEM((64, NZ), F32),
        pltpu.VMEM((3, 64, NZ), F32),
        pltpu.VMEM((3, 2, 2, NZ), F32),
        pltpu.VMEM((3, 2, 2, NZ), F32),
        pltpu.VMEM((3, 2, 32, NZ), F32),
        pltpu.VMEM((64, NZ), F32),
        pltpu.VMEM((64, NZ), F32),
        pltpu.VMEM((64, NZ), F32),
        pltpu.VMEM((NP, 16, 128), F32),
        pltpu.VMEM((2, NP, 16, 128), F32),
        pltpu.VMEM((2, 2, 2, 8, NX), F32),
        pltpu.VMEM((2, 2, NT, 2, 2, 8, NX), F32),
        pltpu.VMEM((2, 2, NY, 8, NX), F32),
        pltpu.VMEM((2, NY, 8, NX), F32),
        pltpu.VMEM((NP, 4, 2, 2, 2, 8, 128), F32),
        pltpu.VMEM((2, NP, 4, 2, 2, 2, 8, 128), F32),
        pltpu.VMEM((4, 2, 64, NZ), F32),
        pltpu.VMEM((2, 4, 2, 64, NZ), F32),
        pltpu.VMEM((64, NZ), F32),
        pltpu.VMEM((2, 64, NZ), F32),
        pltpu.SemaphoreType.DMA((8,)),
        pltpu.SemaphoreType.DMA((6,)),
        pltpu.SemaphoreType.DMA((1,)),
        pltpu.SemaphoreType.DMA((2,)),
        pltpu.SemaphoreType.DMA((2,)),
        pltpu.SemaphoreType.DMA((2, 2)),
        pltpu.SemaphoreType.DMA((2,)),
        pltpu.SemaphoreType.DMA((1,)),
        pltpu.SemaphoreType.DMA((2, 4)),
        pltpu.SemaphoreType.DMA((1,)),
        pltpu.SemaphoreType.DMA((2,)),
        pltpu.SemaphoreType.DMA((1,)),
        pltpu.SemaphoreType.DMA((2,)),
        pltpu.SemaphoreType.DMA((3, 4)),
        pltpu.SemaphoreType.DMA((3, 4)),
    ]
    return pl.pallas_call(
        wave_kernel,
        name="wave",
        out_shape=(brick, brick),
        in_specs=[any_spec] * 8 + [pl.BlockSpec(memory_space=pltpu.SMEM)],
        out_specs=(vmem_spec, vmem_spec),
        scratch_shapes=scratch,
        compiler_params=pltpu.CompilerParams(
            collective_id=0, has_side_effects=True, vmem_limit_bytes=60 * 2**20
        ),
    )(pres, prior, loc, spec, jnp.asarray(z_table()), jnp.asarray(x_table()), kinds, thermal, props)


def solution(mesh):
    return jax.shard_map(
        wave,
        mesh=mesh,
        in_specs=(
            P("pencil", None, None),
            P("pencil", None, None),
            P("term", "pencil", None, None),
            P("term", None, "pencil", None),
            P("pencil", "term", None),
            P(),
            P("pencil", "term", None),
        ),
        out_specs=(P("pencil", "term", None), P("pencil", "term", None)),
        check_vma=False,
    )
```

```python
import math

import numpy as np

import jax
import jax.numpy as jnp
from jax import lax
from jax.experimental import pallas as pl
from jax.experimental.pallas import tpu as pltpu
from jax.sharding import PartitionSpec as P

WAVE_STEPS = 2
DIFFUSION = 0.125
MESH = pl.DeviceIdType.MESH
F32 = jnp.float32
BF16 = jnp.bfloat16

NX = 512
NY = 16
NZ = 512
NT = 8
NP = 16
XR = NX // NP
SCALE = 2.0 / (NX * NY * NZ)


PENCIL_ORDER = (
    (1, 0, 0), (0, 1, 0), (3, 1, 1), (2, 0, 0), (0, 1, 1), (1, 1, 0), (3, 0, 0), (2, 1, 1),
    (1, 0, 1), (3, 1, 0), (2, 0, 1), (2, 1, 0), (3, 0, 1), (1, 1, 1), (0, 0, 1),
)


TERM_ORDER = ((2, 0), (0, 1), (1, 1), (3, 1), (1, 0), (3, 0), (2, 1))


def high_low(table):
    high = table.astype(BF16)
    low = (table - high.astype(np.float32)).astype(BF16)
    return np.stack([high, low])


def z_table():
    rows = np.zeros((2, NP, 2, 8, NZ), np.float64)
    z = np.arange(NZ)
    for h in range(2):
        for p in range(NP):
            for i in range(8):
                if h == 1 and i == 0 and p == 8:
                    rows[h, p, 0, i] = 1.0
                    rows[h, p, 1, i] = 1.0 - 2.0 * (z % 2)
                    continue
                j = 8 * h + i
                if i == 0:
                    j = 8 if h == 0 else (16 if p < 8 else 0)
                kz = 32 * p + j
                angle = 2.0 * math.pi * ((kz * z) % NZ) / NZ
                rows[h, p, 0, i] = np.cos(angle)
                rows[h, p, 1, i] = -np.sin(angle)
    return high_low(rows.reshape(NZ, NZ).astype(np.float32))


def x_table():
    k = np.arange(256)[:, None]
    tables = []
    for c in range(2):
        x = 2 * np.arange(256)[None, :] + c
        angle = 2.0 * math.pi * ((k * x) % NX) / NX
        co, si = np.cos(angle), np.sin(angle)
        tables.append(high_low(np.block([[co, si], [-si, co]]).astype(np.float32)))
    return np.stack(tables)


def split(x):
    high = x.astype(BF16)
    low = (x - high.astype(F32)).astype(BF16)
    return high, low


def dot(a, b, ca, cb):
    return lax.dot_general(a, b, (((ca,), (cb,)), ((), ())), preferred_element_type=F32)


def dot3(a, b, ca, cb):
    return dot(a[0], b[0], ca, cb) + dot(a[0], b[1], ca, cb) + dot(a[1], b[0], ca, cb)


def fft16(re, im, sign):
    n = len(re)
    if n == 1:
        return re, im
    er, ei = fft16(re[0::2], im[0::2], sign)
    orr, oi = fft16(re[1::2], im[1::2], sign)
    half = n // 2
    out_r, out_i = [None] * n, [None] * n
    for k in range(half):
        angle = sign * 2.0 * math.pi * k / n
        c, s = math.cos(angle), math.sin(angle)
        a, b = orr[k], oi[k]
        if k == 0:
            tr, ti = a, b
        elif 4 * k == n:
            tr, ti = (b, -a) if sign < 0 else (-b, a)
        elif abs(abs(c) - abs(s)) < 1e-12:
            r = math.sqrt(0.5)
            sc, ss = math.copysign(1.0, c), math.copysign(1.0, s)
            tr = r * ((a if sc > 0 else -a) - (b if ss > 0 else -b))
            ti = r * ((b if sc > 0 else -b) + (a if ss > 0 else -a))
        else:
            tr = c * a - s * b
            ti = c * b + s * a
        out_r[k], out_i[k] = er[k] + tr, ei[k] + ti
        out_r[k + half], out_i[k + half] = er[k] - tr, ei[k] - ti
    return out_r, out_i


def exchange_groups(tiles):
    rows = tiles[0].shape[0]
    lane = lax.broadcasted_iota(jnp.int32, (rows, 128), 1)
    tiles = list(tiles)
    for bit in (4, 2, 1):
        width = bit * 16
        keep_low = (lane % (2 * width)) < width
        new = list(tiles)
        for i in range(8):
            if i & bit:
                continue
            a, b = tiles[i], tiles[i + bit]
            new[i] = jnp.where(keep_low, a, pltpu.roll(b, width, 1))
            new[i + bit] = jnp.where(keep_low, pltpu.roll(a, 128 - width, 1), b)
        tiles = new
    return tiles


def reverse_lanes(tiles):
    lane = lax.broadcasted_iota(jnp.int32, (8, 128), 1)
    index = (128 - lane) % 128
    moved = [jnp.take_along_axis(x, index, axis=1) for x in tiles]
    return [jnp.where(lane == 0, moved[(4 - a) % 4], moved[3 - a]) for a in range(4)]


def wave_kernel(
    pres, prior, loc, spec, ztab, xtab, kinds, thermal, props, result,
    pres_v, prior_v, loc_v, lr, spec_v, srecv, row0, row0r, amp, bmp, zt, xt,
    kind_v, heat_v, absorb, perfuse, heat, field, hxs, hx, hy,
    cur, prev, dose, fsend, frecv, vsend, agb, w, xo, snd, rcv, psend, rsr, psum, ptake,
    lsem, sx, fs, fr, gs, gr, gy, sent, came, rs, rr, ps, pr, hs, hr,
):
    t = lax.axis_index("term")
    p = lax.axis_index("pencil")

    barrier = pltpu.get_barrier_semaphore()

    @pl.loop(1, NP)
    def _(o):
        pl.semaphore_signal(barrier, inc=1, device_id=(t, lax.rem(p + o, NP)), device_id_type=MESH)

    @pl.loop(1, NT)
    def _(o):
        pl.semaphore_signal(barrier, inc=1, device_id=(lax.rem(t + o, NT), p), device_id_type=MESH)

    loads = [
        pltpu.make_async_copy(src, dst, lsem.at[i])
        for i, (src, dst) in enumerate(
            [
                (pres, pres_v), (ztab, zt), (thermal, heat_v), (kinds, kind_v),
                (spec, spec_v), (xtab, xt), (prior, prior_v), (loc, loc_v),
            ]
        )
    ]
    for load in loads:
        load.start()

    def remote(src, dst, send, recv, device):
        return pltpu.make_async_remote_copy(
            src_ref=src, dst_ref=dst, send_sem=send, recv_sem=recv, device_id=device, device_id_type=MESH
        )

    def pencil_peers():
        for dx, dy, dc in PENCIL_ORDER:
            yield (
                lax.rem(p // 4 + dx, 4) * 4 + lax.rem(lax.rem(p // 2, 2) + dy, 2) * 2 + lax.rem(lax.rem(p, 2) + dc, 2)
            )

    z_place, y_place = t // 2, lax.rem(t, 2)
    partner = t + 1 - 2 * y_place

    def chunk(i):
        return lax.rem(z_place + lax.rem(2 + 3 * i + 3 * (i // 2) + 2 * (i // 3), 4), 4)

    def z_peers():
        for dz in (1, 3, 2):
            yield lax.rem(z_place + dz, 4) * 2 + y_place

    mirror = (t, NP - 1 - p)
    swaps = [
        remote(spec.at[:, :, pl.ds(24 - 8 * h, 8), :], srecv.at[h], sx.at[h], sx.at[2 + h], mirror)
        for h in range(2)
    ]
    give = jnp.where(p == 0, 8, lax.rem(NP - p, NP))
    rowcopy = remote(row0, row0r, sx.at[4], sx.at[5], (t, give))

    lane = lax.broadcasted_iota(jnp.int32, (8, 128), 1)
    sub = lax.broadcasted_iota(jnp.int32, (8, 128), 0)
    flip = (8 - sub) % 8

    edges = [
        (t > 0, (t - 1, p)),
        (t < NT - 1, (t + 1, p)),
        (p > 0, (t, p - 1)),
        (p < NP - 1, (t, p + 1)),
    ]

    def halo_copy(k, e):
        if e < 2:
            src, dst = field.at[k, pl.ds(32 * e, 32)], hy.at[k, 1 - e]
        else:
            src, dst = hxs.at[k, e - 2], hx.at[k, 3 - e]
        return remote(src, dst, hs.at[k, e], hr.at[k, 1 - e if e < 2 else 5 - e], edges[e][1])

    def halo_start(k):
        for y in range(2):
            hxs[k, 0, pl.ds(y, 1), :] = field[k, pl.ds(32 * y, 1), :]
            hxs[k, 1, pl.ds(y, 1), :] = field[k, pl.ds(32 * y + 31, 1), :]
        for e in range(4):

            @pl.when(edges[e][0])
            def _():
                halo_copy(k, e).start()

            @pl.when(jnp.logical_not(edges[e][0]))
            def _():
                if e < 2:
                    hy[k, e] = jnp.zeros((32, NZ), F32)
                else:
                    hx[k, e - 2] = jnp.zeros((2, NZ), F32)

    def halo_wait(k):
        for e in range(4):

            @pl.when(edges[e][0])
            def _():
                halo_copy(k, e).wait_send()
                ref = hy.at[k, e] if e < 2 else hx.at[k, e - 2]
                pltpu.make_async_copy(ref, ref, hr.at[k, e]).wait()

    row16 = lax.broadcasted_iota(jnp.int32, (16, NZ), 0)
    col16 = lax.broadcasted_iota(jnp.int32, (16, NZ), 1)

    def heat_apply(k, y, c):
        mine = field[k, pl.ds(32 * y + 16 * c, 16), :]
        other = field[k, pl.ds(32 * y + 16 * (1 - c), 16), :]
        if c == 0:
            shifted = jnp.where(row16 == 0, hx[k, 0, pl.ds(y, 1), :], pltpu.roll(other, 1, 0))
        else:
            shifted = jnp.where(row16 == 15, hx[k, 1, pl.ds(y, 1), :], pltpu.roll(other, 15, 0))
        near = other + shifted
        near = near + field[k, pl.ds(32 * (1 - y) + 16 * c, 16), :] + hy[k, y, pl.ds(16 * c, 16), :]
        near = near + jnp.where(col16 == 0, 0.0, pltpu.roll(mine, 1, 1))
        near = near + jnp.where(col16 == NZ - 1, 0.0, pltpu.roll(mine, NZ - 1, 1))
        rows = pl.ds(32 * y + 16 * c, 16)
        return mine + DIFFUSION * (near - 6.0 * mine) - perfuse[rows, :] * mine

    def heat_begin():
        loads[2].wait()
        for y in range(2):
            for x in range(XR):
                row = y * XR + (x % 2) * 16 + x // 2
                field[0, pl.ds(row, 1), :] = heat_v[x, pl.ds(y, 1), :]

    def heat_coefficients():
        loads[3].wait()
        for y in range(2):
            for x in range(XR):
                row = y * XR + (x % 2) * 16 + x // 2
                kind = kind_v[x, pl.ds(y, 1), :]
                for ref, j in ((absorb, 0), (perfuse, 1)):
                    ref[pl.ds(row, 1), :] = jnp.where(
                        kind == 0, props[j, 0], jnp.where(kind == 1, props[j, 1], props[j, 2])
                    )

    def heat_middle():
        halo_wait(0)
        for y in range(2):
            for c in range(2):
                field[1, pl.ds(32 * y + 16 * c, 16), :] = heat_apply(0, y, c)
        halo_start(1)

    def heat_late():
        halo_wait(1)
        for y in range(2):
            for c in range(2):
                heat[pl.ds(32 * y + 16 * c, 16), :] = heat_apply(1, y, c)

    def heat_finish():
        field[2] = absorb[...] * dose[...]
        halo_start(2)
        for y in range(2):
            for x in range(XR):
                row = y * XR + (x % 2) * 16 + x // 2
                result[0, x, pl.ds(y, 1), :] = cur[pl.ds(row, 1), :]
        halo_wait(2)
        for y in range(2):
            for c in range(2):
                rows = pl.ds(32 * y + 16 * c, 16)
                heat[rows, :] = heat[rows, :] + (field[2, rows, :] + heat_apply(2, y, c))

    def build_amp(h):
        swaps[h].wait()
        if h == 1:

            @pl.when(p < 8)
            def _():
                rowcopy.wait_send()

            @pl.when(p >= 8)
            def _():
                rowcopy.wait_recv()

        low_p = jnp.where(p < 8, 1, 0)
        special = pl.multiple_of(16 * low_p, 8)

        pick_row = (sub == 0) & (low_p == 0)

        @pl.loop(0, 8)
        def _(m4):
            for j in range(4):
                n = 4 * m4 + j
                q = n // 16
                ky = lax.rem(n, 16)
                kr = lax.rem(16 - ky, 16)
                mirrored = []
                for a in range(4):
                    cols = pl.ds(128 * a, 128)
                    m = jnp.take_along_axis(srecv[h, q, kr, :, cols], flip, axis=0)
                    if h == 1:
                        extra = jnp.broadcast_to(row0r[16 * q + kr, :, cols], (8, 128))
                        m = jnp.where(pick_row, extra, m)
                    mirrored.append(m)
                mirrored = reverse_lanes(mirrored)
                for a in range(4):
                    cols = pl.ds(128 * a, 128)
                    if h == 0:
                        first, rest = spec_v[q, ky, pl.ds(8, 8), cols], spec_v[q, ky, pl.ds(0, 8), cols]
                    else:
                        first, rest = spec_v[q, ky, pl.ds(special, 8), cols], spec_v[q, ky, pl.ds(8, 8), cols]
                    amp[q, ky, pl.ds(8 * h, 8), cols] = jnp.where(sub == 0, first, rest) + mirrored[a]

        if h == 0:
            return

        @pl.when(p == 8)
        def _():
            @pl.loop(0, 32)
            def _(n):
                q = n // 16
                ky = lax.rem(n, 16)
                kr = lax.rem(16 - ky, 16)
                own_r, zero_r = [], []
                for a in range(4):
                    cols = pl.ds(128 * a, 128)
                    own_r.append(spec_v[q, kr, pl.ds(0, 8), cols])
                    zero_r.append(jnp.broadcast_to(row0r[16 * q + kr, :, cols], (8, 128)))
                own_r = reverse_lanes(own_r)
                zero_r = reverse_lanes(zero_r)
                for a in range(4):
                    cols = pl.ds(128 * a, 128)
                    last = spec_v[q, ky, pl.ds(0, 8), cols] + own_r[a]
                    first = jnp.broadcast_to(row0r[16 * q + ky, :, cols], (8, 128)) + zero_r[a]
                    old = amp[q, ky, pl.ds(8, 8), cols]
                    amp[q, ky, pl.ds(8, 8), cols] = jnp.where(sub == 0, 0.25 * (first + last), old)
                    bmp[q, ky, :, cols] = jnp.where(sub == 0, 0.25 * (first - last), 0.0)

    def y_stage(re, im, weight, store):
        re, im = fft16(re, im, -1)
        for q in range(2):
            wr, wi = [], []
            for ky in range(16):
                m = weight(q, ky)
                wr.append(m * re[ky])
                wi.append(m * im[ky])
            wr, wi = fft16(wr, wi, 1)
            for y in range(16):
                store(q, 0, y, wr[y])
                store(q, 1, y, wi[y])

    def wait_bytes(ref, sem):
        pltpu.make_async_copy(ref, ref, sem).wait()

    def forward_z():
        b = split(cur[...])
        b = tuple(jnp.concatenate([v, v], axis=0) for v in b)
        out = dot3((zt[0], zt[1]), b, 1, 1).reshape(2, NP, 2, 8, 128)
        wide = lax.broadcasted_iota(jnp.int32, (NP, 8, 128), 2)
        for h in range(2):
            fsend[:, pl.ds(8 * h, 8), :] = jnp.where(wide < 64, out[h, :, 0], out[h, :, 1])

    def forward_send(step):
        for d in pencil_peers():
            remote(fsend.at[d], frecv.at[step, p], fs.at[0], fr.at[step], (t, d)).start()

    loads[0].wait()
    for y in range(2):
        for x in range(XR):
            row = y * XR + (x % 2) * 16 + x // 2
            cur[pl.ds(row, 1), :] = pres_v[x, pl.ds(2 * t + y, 1), :]
    loads[1].wait()
    forward_z()
    heat_begin()
    loads[4].wait()
    for q in range(2):
        row0[pl.ds(16 * q, 16), 0, :] = spec_v[q, :, 0, :]

    pl.semaphore_wait(barrier, NP + NT - 2)
    forward_send(0)
    swaps[0].start()
    loads[5].wait()

    @pl.loop(0, WAVE_STEPS)
    def _(step):
        frecv[step, p] = fsend[p]
        wait_bytes(frecv.at[step, pl.ds(0, NP - 1)], fr.at[step])

        groups = [exchange_groups([frecv[step, 8 * a + i] for i in range(8)]) for a in range(2)]
        parts = []
        for c in range(2):
            rows = [
                jnp.concatenate(
                    [groups[0][y * 2 + c], groups[1][y * 2 + c], groups[0][4 + y * 2 + c], groups[1][4 + y * 2 + c]],
                    axis=1,
                )
                for y in range(2)
            ]
            lhs = split(jnp.concatenate(rows, axis=0))
            parts.append(dot3(lhs, (xt[c, 0], xt[c, 1]), 1, 1))
        for lo, v in ((0, parts[0] + parts[1]), (256, parts[0] - parts[1])):
            for h in range(2):
                for y in range(2):
                    for ri in range(2):
                        vsend[h, y, ri, :, pl.ds(lo, 256)] = v[
                            y * 16 + 8 * h : y * 16 + 8 * h + 8, ri * 256 : ri * 256 + 256
                        ]
        wait_bytes(fsend.at[pl.ds(0, NP - 1)], fs.at[0])

        for dz, dy in TERM_ORDER:
            d = lax.rem(z_place + dz, 4) * 2 + lax.rem(y_place + dy, 2)
            remote(vsend.at[0], agb.at[step, 0, t], gs.at[0], gr.at[step, 0], (d, p)).start()
        remote(vsend.at[1], agb.at[step, 1, t], gs.at[1], gy.at[step], (partner, p)).start()
        for d in z_peers():
            remote(vsend.at[1], agb.at[step, 1, t], gs.at[1], gr.at[step, 1], (d, p)).start()
        for h in range(2):
            agb[step, h, t] = vsend[h]

        @pl.when(step == 0)
        def _():
            swaps[1].start()

            @pl.when(p < 8)
            def _():
                rowcopy.start()

            halo_start(0)
            loads[6].wait()
            for y in range(2):
                for x in range(XR):
                    row = y * XR + (x % 2) * 16 + x // 2
                    prev[pl.ds(row, 1), :] = prior_v[x, pl.ds(2 * t + y, 1), :]
            dose[...] = jnp.zeros_like(dose)
            heat_coefficients()
            loads[7].wait()
            @pl.loop(0, 8)
            def _(n):
                q = n // 4
                cols = pl.ds(pl.multiple_of(lax.rem(n, 4) * 128, 128), 128)
                for y in range(NY):
                    rows = loc_v[q, :, y, cols]
                    for c in range(2):
                        index = (2 * sub + c) % 8
                        for i in range(2):
                            pair = [
                                jnp.take_along_axis(rows[16 * i + 8 * j : 16 * i + 8 * j + 8], index, axis=0)
                                for j in range(2)
                            ]
                            lr[q, y, pl.ds(16 * c + 8 * i, 8), cols] = jnp.where(sub < 4, pair[0], pair[1])

        for h in range(2):

            @pl.when(step == 0)
            def _():
                build_amp(h)

            wait_bytes(agb.at[step, h, pl.ds(0, NT - 1 - h)], gr.at[step, h])
            if h == 0:
                theirs = agb.at[step, 1, partner]
                wait_bytes(theirs, gy.at[step])
                for d in z_peers():
                    remote(theirs, theirs, gs.at[1], gr.at[step, 1], (d, p)).start()

            @pl.loop(0, 4)
            def _(a):
                cols = pl.ds(pl.multiple_of(a * 128, 128), 128)

                def weight(q, ky):
                    return amp[q, ky, pl.ds(8 * h, 8), cols]

                def store(q, ri, y, value):
                    w[q, ri, y, :, cols] = value

                y_stage(
                    [agb[step, h, y // 2, y % 2, 0, :, cols] for y in range(16)],
                    [agb[step, h, y // 2, y % 2, 1, :, cols] for y in range(16)],
                    weight,
                    store,
                )

            if h == 1:

                @pl.when(p == 8)
                def _():
                    @pl.loop(0, 4)
                    def _(a):
                        cols = pl.ds(pl.multiple_of(a * 128, 128), 128)
                        far = pl.ds(pl.multiple_of((3 - a) * 128, 128), 128)
                        near = pl.ds(pl.multiple_of(lax.rem(4 - a, 4) * 128, 128), 128)
                        index = (128 - lane) % 128

                        def load(y, ri):
                            v0 = jnp.take_along_axis(agb[step, 1, y // 2, y % 2, ri, :, near], index, axis=1)
                            v1 = jnp.take_along_axis(agb[step, 1, y // 2, y % 2, ri, :, far], index, axis=1)
                            return jnp.where(lane == 0, v0, v1)

                        def weight(q, ky):
                            return bmp[q, ky, :, cols]

                        def store(q, ri, y, value):
                            w[q, ri, y, :, cols] += value

                        y_stage(
                            [load(y, 0) for y in range(16)],
                            [-load(y, 1) for y in range(16)],
                            weight,
                            store,
                        )

            @pl.loop(0, 2)
            def _(q):
                low = [w[q, ri, :, :, pl.ds(0, 256)].reshape(128, 256) for ri in range(2)]
                high = [w[q, ri, :, :, pl.ds(256, 256)].reshape(128, 256) for ri in range(2)]
                for c in range(2):
                    mix = [(lo + hi) if c == 0 else (lo - hi) for lo, hi in zip(low, high)]
                    lhs = split(jnp.concatenate(mix, axis=1))
                    xo[c] = dot3(lhs, (xt[c, 0], xt[c, 1]), 1, 0).reshape(16, 8, 512)

                @pl.loop(0, 4)
                def _(ra):
                    ri = ra // 2
                    first = 8 * lax.rem(ra, 2)
                    cols = pl.ds(pl.multiple_of(ra * 128, 128), 128)
                    for yh in range(4):
                        tiles = exchange_groups([xo[i % 2, 4 * yh + i // 2, :, cols] for i in range(8)])
                        for i in range(8):
                            snd[first + i, yh, h, q, ri] = tiles[i]

            rcv[step, p, :, h] = snd[p, :, h]

            @pl.loop(0, 2)
            def _(i):
                yh = chunk(i)
                for d in pencil_peers():
                    remote(
                        snd.at[d, yh, h], rcv.at[step, p, yh, h], sent.at[0], came.at[step, yh], (t, d)
                    ).start()

        @pl.loop(2, 4)
        def _(i):
            yh = chunk(i)
            for d in pencil_peers():
                remote(snd.at[d, yh], rcv.at[step, p, yh], sent.at[0], came.at[step, yh], (t, d)).start()

        for h in range(2):
            wait_bytes(agb.at[step, h, pl.ds(0, NT - 1)], gs.at[h])

        @pl.when(step == 0)
        def _():
            heat_middle()

        @pl.when(step == 1)
        def _():
            heat_late()

        @pl.loop(0, 4)
        def _(i):
            yh = chunk(i)
            wait_bytes(rcv.at[step, pl.ds(0, NP - 1), yh], came.at[step, yh])
            total = None
            for q in range(2):
                d = jnp.concatenate(
                    [rcv[step, :, yh, h, q].reshape(256, 128) for h in range(2)], axis=0
                )
                field = dot3(split(d), (zt[0], zt[1]), 0, 0)
                field = field * lr[q, pl.ds(4 * yh, 4)].reshape(128, 512)
                total = field if total is None else total + field
            psend[yh] = total.reshape(2, 64, 512)

            @pl.when(yh != z_place)
            def _():
                remote(
                    psend.at[yh], rsr.at[step, z_place], rs.at[0], rr.at[step], (2 * yh + y_place, p)
                ).start()

        wait_bytes(snd.at[pl.ds(0, NP - 1)], sent.at[0])
        wait_bytes(rsr.at[step, pl.ds(0, 3)], rr.at[step])

        def z_sum(j):
            total = psend[z_place, j]
            for dz in range(1, 4):
                total = total + rsr[step, lax.rem(z_place + dz, 4), j]
            return total

        psum[...] = z_sum(1 - y_place)
        give_sum = remote(psum, ptake.at[step], ps.at[0], pr.at[step], (partner, p))
        give_sum.start()
        total = z_sum(y_place)
        wait_bytes(psend.at[pl.ds(0, 3)], rs.at[0])
        give_sum.wait_send()
        wait_bytes(ptake.at[step], pr.at[step])
        total = total + ptake[step]
        advanced = SCALE * total - prev[...]
        dose[...] = dose[...] + advanced * advanced
        prev[...] = cur[...]
        cur[...] = advanced

        @pl.when(step == 0)
        def _():
            forward_z()
            forward_send(1)

    heat_finish()
    for y in range(2):
        for x in range(XR):
            row = y * XR + (x % 2) * 16 + x // 2
            result[1, x, pl.ds(y, 1), :] = heat[pl.ds(row, 1), :]


def wave(pres, prior, loc, spec, kinds, props, thermal):
    bricks = jax.ShapeDtypeStruct((2, XR, 2, NZ), F32)
    any_spec = pl.BlockSpec(memory_space=pl.ANY)
    vmem_spec = pl.BlockSpec(memory_space=pltpu.VMEM)
    scratch = [
        pltpu.VMEM((XR, NY, NZ), F32),
        pltpu.VMEM((XR, NY, NZ), F32),
        pltpu.VMEM((2, XR, NY, NZ), F32),
        pltpu.VMEM((2, NY, XR, NZ), F32),
        pltpu.VMEM((2, NY, 32, NX), F32),
        pltpu.VMEM((2, 2, NY, 8, NX), F32),
        pltpu.VMEM((32, 1, NX), F32),
        pltpu.VMEM((32, 1, NX), F32),
        pltpu.VMEM((2, NY, 16, NX), F32),
        pltpu.VMEM((2, NY, 8, NX), F32),
        pltpu.VMEM((2, NZ, NZ), BF16),
        pltpu.VMEM((2, 2, NX, NX), BF16),
        pltpu.VMEM((XR, 2, NZ), jnp.int32),
        pltpu.VMEM((XR, 2, NZ), F32),
        pltpu.VMEM((64, NZ), F32),
        pltpu.VMEM((64, NZ), F32),
        pltpu.VMEM((64, NZ), F32),
        pltpu.VMEM((3, 64, NZ), F32),
        pltpu.VMEM((3, 2, 2, NZ), F32),
        pltpu.VMEM((3, 2, 2, NZ), F32),
        pltpu.VMEM((3, 2, 32, NZ), F32),
        pltpu.VMEM((64, NZ), F32),
        pltpu.VMEM((64, NZ), F32),
        pltpu.VMEM((64, NZ), F32),
        pltpu.VMEM((NP, 16, 128), F32),
        pltpu.VMEM((2, NP, 16, 128), F32),
        pltpu.VMEM((2, 2, 2, 8, NX), F32),
        pltpu.VMEM((2, 2, NT, 2, 2, 8, NX), F32),
        pltpu.VMEM((2, 2, NY, 8, NX), F32),
        pltpu.VMEM((2, NY, 8, NX), F32),
        pltpu.VMEM((NP, 4, 2, 2, 2, 8, 128), F32),
        pltpu.VMEM((2, NP, 4, 2, 2, 2, 8, 128), F32),
        pltpu.VMEM((4, 2, 64, NZ), F32),
        pltpu.VMEM((2, 4, 2, 64, NZ), F32),
        pltpu.VMEM((64, NZ), F32),
        pltpu.VMEM((2, 64, NZ), F32),
        pltpu.SemaphoreType.DMA((8,)),
        pltpu.SemaphoreType.DMA((6,)),
        pltpu.SemaphoreType.DMA((1,)),
        pltpu.SemaphoreType.DMA((2,)),
        pltpu.SemaphoreType.DMA((2,)),
        pltpu.SemaphoreType.DMA((2, 2)),
        pltpu.SemaphoreType.DMA((2,)),
        pltpu.SemaphoreType.DMA((1,)),
        pltpu.SemaphoreType.DMA((2, 4)),
        pltpu.SemaphoreType.DMA((1,)),
        pltpu.SemaphoreType.DMA((2,)),
        pltpu.SemaphoreType.DMA((1,)),
        pltpu.SemaphoreType.DMA((2,)),
        pltpu.SemaphoreType.DMA((3, 4)),
        pltpu.SemaphoreType.DMA((3, 4)),
    ]
    both = pl.pallas_call(
        wave_kernel,
        name="wave",
        out_shape=bricks,
        in_specs=[any_spec] * 8 + [pl.BlockSpec(memory_space=pltpu.SMEM)],
        out_specs=vmem_spec,
        scratch_shapes=scratch,
        compiler_params=pltpu.CompilerParams(
            collective_id=0, has_side_effects=True, vmem_limit_bytes=60 * 2**20
        ),
    )(pres, prior, loc, spec, jnp.asarray(z_table()), jnp.asarray(x_table()), kinds, thermal, props.T)
    return both[0], both[1]


def solution(mesh):
    return jax.shard_map(
        wave,
        mesh=mesh,
        in_specs=(
            P("pencil", None, None),
            P("pencil", None, None),
            P("term", "pencil", None, None),
            P("term", None, "pencil", None),
            P("pencil", "term", None),
            P(),
            P("pencil", "term", None),
        ),
        out_specs=(P("pencil", "term", None), P("pencil", "term", None)),
        check_vma=False,
    )
```

```python
import math

import numpy as np

import jax
import jax.numpy as jnp
from jax import lax
from jax.experimental import pallas as pl
from jax.experimental.pallas import tpu as pltpu
from jax.sharding import PartitionSpec as P

WAVE_STEPS = 2
DIFFUSION = 0.125
MESH = pl.DeviceIdType.MESH
F32 = jnp.float32
BF16 = jnp.bfloat16

NX = 512
NY = 16
NZ = 512
NT = 8
NP = 16
XR = NX // NP
SCALE = 2.0 / (NX * NY * NZ)


PENCIL_ORDER = (
    (1, 0, 0), (0, 1, 0), (3, 1, 1), (2, 0, 0), (0, 1, 1), (1, 1, 0), (3, 0, 0), (2, 1, 1),
    (1, 0, 1), (3, 1, 0), (2, 0, 1), (2, 1, 0), (3, 0, 1), (1, 1, 1), (0, 0, 1),
)


TERM_ORDER = ((2, 0), (0, 1), (1, 1), (3, 1), (1, 0), (3, 0), (2, 1))


def high_low(table):
    high = table.astype(BF16)
    low = (table - high.astype(np.float32)).astype(BF16)
    return np.stack([high, low])


def z_table():
    rows = np.zeros((2, NP, 2, 8, NZ), np.float64)
    z = np.arange(NZ)
    for h in range(2):
        for p in range(NP):
            for i in range(8):
                if h == 1 and i == 0 and p == 8:
                    rows[h, p, 0, i] = 1.0
                    rows[h, p, 1, i] = 1.0 - 2.0 * (z % 2)
                    continue
                j = 8 * h + i
                if i == 0:
                    j = 8 if h == 0 else (16 if p < 8 else 0)
                kz = 32 * p + j
                angle = 2.0 * math.pi * ((kz * z) % NZ) / NZ
                rows[h, p, 0, i] = np.cos(angle)
                rows[h, p, 1, i] = -np.sin(angle)
    return high_low(rows.reshape(NZ, NZ).astype(np.float32))


def x_table():
    k = np.arange(256)[:, None]
    tables = []
    for c in range(2):
        x = 2 * np.arange(256)[None, :] + c
        angle = 2.0 * math.pi * ((k * x) % NX) / NX
        co, si = np.cos(angle), np.sin(angle)
        tables.append(high_low(np.block([[co, si], [-si, co]]).astype(np.float32)))
    return np.stack(tables)


def split(x):
    high = x.astype(BF16)
    low = (x - high.astype(F32)).astype(BF16)
    return high, low


def dot(a, b, ca, cb):
    return lax.dot_general(a, b, (((ca,), (cb,)), ((), ())), preferred_element_type=F32)


def dot3(a, b, ca, cb):
    return dot(a[0], b[0], ca, cb) + dot(a[0], b[1], ca, cb) + dot(a[1], b[0], ca, cb)


def fft16(re, im, sign):
    n = len(re)
    if n == 1:
        return re, im
    er, ei = fft16(re[0::2], im[0::2], sign)
    orr, oi = fft16(re[1::2], im[1::2], sign)
    half = n // 2
    out_r, out_i = [None] * n, [None] * n
    for k in range(half):
        angle = sign * 2.0 * math.pi * k / n
        c, s = math.cos(angle), math.sin(angle)
        a, b = orr[k], oi[k]
        if k == 0:
            tr, ti = a, b
        elif 4 * k == n:
            tr, ti = (b, -a) if sign < 0 else (-b, a)
        elif abs(abs(c) - abs(s)) < 1e-12:
            r = math.sqrt(0.5)
            sc, ss = math.copysign(1.0, c), math.copysign(1.0, s)
            tr = r * ((a if sc > 0 else -a) - (b if ss > 0 else -b))
            ti = r * ((b if sc > 0 else -b) + (a if ss > 0 else -a))
        else:
            tr = c * a - s * b
            ti = c * b + s * a
        out_r[k], out_i[k] = er[k] + tr, ei[k] + ti
        out_r[k + half], out_i[k + half] = er[k] - tr, ei[k] - ti
    return out_r, out_i


def exchange_groups(tiles):
    rows = tiles[0].shape[0]
    lane = lax.broadcasted_iota(jnp.int32, (rows, 128), 1)
    tiles = list(tiles)
    for bit in (4, 2, 1):
        width = bit * 16
        keep_low = (lane % (2 * width)) < width
        new = list(tiles)
        for i in range(8):
            if i & bit:
                continue
            a, b = tiles[i], tiles[i + bit]
            new[i] = jnp.where(keep_low, a, pltpu.roll(b, width, 1))
            new[i + bit] = jnp.where(keep_low, pltpu.roll(a, 128 - width, 1), b)
        tiles = new
    return tiles


def reverse_lanes(tiles):
    lane = lax.broadcasted_iota(jnp.int32, (8, 128), 1)
    index = (128 - lane) % 128
    moved = [jnp.take_along_axis(x, index, axis=1) for x in tiles]
    return [jnp.where(lane == 0, moved[(4 - a) % 4], moved[3 - a]) for a in range(4)]


def wave_kernel(
    pres, prior, loc, spec, ztab, xtab, kinds, thermal, props, result,
    pres_v, prior_v, loc_v, lr, spec_v, srecv, row0, row0r, amp, bmp, zt, xt,
    kind_v, heat_v, absorb, perfuse, heat, field, hxs, hx, hy,
    cur, prev, dose, fsend, frecv, vsend, agb, w, xo, snd, rcv, psend, rsr, psum, ptake,
    lsem, sx, fs, fr, gs, gr, gy, sent, came, rs, rr, ps, pr, hs, hr,
):
    t = lax.axis_index("term")
    p = lax.axis_index("pencil")

    barrier = pltpu.get_barrier_semaphore()

    @pl.loop(1, NP)
    def _(o):
        pl.semaphore_signal(barrier, inc=1, device_id=(t, lax.rem(p + o, NP)), device_id_type=MESH)

    @pl.loop(1, NT)
    def _(o):
        pl.semaphore_signal(barrier, inc=1, device_id=(lax.rem(t + o, NT), p), device_id_type=MESH)

    loads = [
        pltpu.make_async_copy(src, dst, lsem.at[i])
        for i, (src, dst) in enumerate(
            [
                (pres, pres_v), (ztab, zt), (thermal, heat_v), (kinds, kind_v),
                (spec, spec_v), (xtab, xt), (prior, prior_v), (loc, loc_v),
            ]
        )
    ]
    for load in loads:
        load.start()

    def remote(src, dst, send, recv, device):
        return pltpu.make_async_remote_copy(
            src_ref=src, dst_ref=dst, send_sem=send, recv_sem=recv, device_id=device, device_id_type=MESH
        )

    def pencil_peers():
        for dx, dy, dc in PENCIL_ORDER:
            yield (
                lax.rem(p // 4 + dx, 4) * 4 + lax.rem(lax.rem(p // 2, 2) + dy, 2) * 2 + lax.rem(lax.rem(p, 2) + dc, 2)
            )

    z_place, y_place = t // 2, lax.rem(t, 2)
    partner = t + 1 - 2 * y_place

    def chunk(i):
        return lax.rem(z_place + lax.rem(2 + 3 * i + 3 * (i // 2) + 2 * (i // 3), 4), 4)

    def z_peers():
        for dz in (1, 3, 2):
            yield lax.rem(z_place + dz, 4) * 2 + y_place

    mirror = (t, NP - 1 - p)
    swaps = [
        remote(spec.at[:, :, pl.ds(24 - 8 * h, 8), :], srecv.at[h], sx.at[h], sx.at[2 + h], mirror)
        for h in range(2)
    ]
    give = jnp.where(p == 0, 8, lax.rem(NP - p, NP))
    rowcopy = remote(row0, row0r, sx.at[4], sx.at[5], (t, give))

    lane = lax.broadcasted_iota(jnp.int32, (8, 128), 1)
    sub = lax.broadcasted_iota(jnp.int32, (8, 128), 0)
    flip = (8 - sub) % 8

    edges = [
        (t > 0, (t - 1, p)),
        (t < NT - 1, (t + 1, p)),
        (p > 0, (t, p - 1)),
        (p < NP - 1, (t, p + 1)),
    ]

    def halo_copy(k, e):
        if e < 2:
            src, dst = field.at[k, pl.ds(32 * e, 32)], hy.at[k, 1 - e]
        else:
            src, dst = hxs.at[k, e - 2], hx.at[k, 3 - e]
        return remote(src, dst, hs.at[k, e], hr.at[k, 1 - e if e < 2 else 5 - e], edges[e][1])

    def halo_start(k):
        for y in range(2):
            hxs[k, 0, pl.ds(y, 1), :] = field[k, pl.ds(32 * y, 1), :]
            hxs[k, 1, pl.ds(y, 1), :] = field[k, pl.ds(32 * y + 31, 1), :]
        for e in range(4):

            @pl.when(edges[e][0])
            def _():
                halo_copy(k, e).start()

            @pl.when(jnp.logical_not(edges[e][0]))
            def _():
                if e < 2:
                    hy[k, e] = jnp.zeros((32, NZ), F32)
                else:
                    hx[k, e - 2] = jnp.zeros((2, NZ), F32)

    def halo_wait(k):
        for e in range(4):

            @pl.when(edges[e][0])
            def _():
                halo_copy(k, e).wait_send()
                ref = hy.at[k, e] if e < 2 else hx.at[k, e - 2]
                pltpu.make_async_copy(ref, ref, hr.at[k, e]).wait()

    row16 = lax.broadcasted_iota(jnp.int32, (16, NZ), 0)
    col16 = lax.broadcasted_iota(jnp.int32, (16, NZ), 1)

    def heat_apply(k, y, c):
        mine = field[k, pl.ds(32 * y + 16 * c, 16), :]
        other = field[k, pl.ds(32 * y + 16 * (1 - c), 16), :]
        if c == 0:
            shifted = jnp.where(row16 == 0, hx[k, 0, pl.ds(y, 1), :], pltpu.roll(other, 1, 0))
        else:
            shifted = jnp.where(row16 == 15, hx[k, 1, pl.ds(y, 1), :], pltpu.roll(other, 15, 0))
        near = other + shifted
        near = near + field[k, pl.ds(32 * (1 - y) + 16 * c, 16), :] + hy[k, y, pl.ds(16 * c, 16), :]
        near = near + jnp.where(col16 == 0, 0.0, pltpu.roll(mine, 1, 1))
        near = near + jnp.where(col16 == NZ - 1, 0.0, pltpu.roll(mine, NZ - 1, 1))
        rows = pl.ds(32 * y + 16 * c, 16)
        return mine + DIFFUSION * (near - 6.0 * mine) - perfuse[rows, :] * mine

    def heat_begin():
        loads[2].wait()
        for y in range(2):
            for x in range(XR):
                row = y * XR + (x % 2) * 16 + x // 2
                field[0, pl.ds(row, 1), :] = heat_v[x, pl.ds(y, 1), :]

    def heat_coefficients():
        loads[3].wait()
        for y in range(2):
            for x in range(XR):
                row = y * XR + (x % 2) * 16 + x // 2
                kind = kind_v[x, pl.ds(y, 1), :]
                for ref, j in ((absorb, 0), (perfuse, 1)):
                    ref[pl.ds(row, 1), :] = jnp.where(
                        kind == 0, props[j, 0], jnp.where(kind == 1, props[j, 1], props[j, 2])
                    )

    def heat_middle():
        halo_wait(0)
        for y in range(2):
            for c in range(2):
                field[1, pl.ds(32 * y + 16 * c, 16), :] = heat_apply(0, y, c)
        halo_start(1)

    def heat_late():
        halo_wait(1)
        for y in range(2):
            for c in range(2):
                heat[pl.ds(32 * y + 16 * c, 16), :] = heat_apply(1, y, c)

    def heat_finish():
        field[2] = absorb[...] * dose[...]
        halo_start(2)
        for y in range(2):
            for x in range(XR):
                row = y * XR + (x % 2) * 16 + x // 2
                result[0, x, pl.ds(y, 1), :] = cur[pl.ds(row, 1), :]
        halo_wait(2)
        for y in range(2):
            for c in range(2):
                rows = pl.ds(32 * y + 16 * c, 16)
                heat[rows, :] = heat[rows, :] + (field[2, rows, :] + heat_apply(2, y, c))

    def build_amp(h):
        swaps[h].wait()
        if h == 1:

            @pl.when(p < 8)
            def _():
                rowcopy.wait_send()

            @pl.when(p >= 8)
            def _():
                rowcopy.wait_recv()

        low_p = jnp.where(p < 8, 1, 0)
        special = pl.multiple_of(16 * low_p, 8)

        pick_row = (sub == 0) & (low_p == 0)

        @pl.loop(0, 8)
        def _(m4):
            for j in range(4):
                n = 4 * m4 + j
                q = n // 16
                ky = lax.rem(n, 16)
                kr = lax.rem(16 - ky, 16)
                mirrored = []
                for a in range(4):
                    cols = pl.ds(128 * a, 128)
                    m = jnp.take_along_axis(srecv[h, q, kr, :, cols], flip, axis=0)
                    if h == 1:
                        extra = jnp.broadcast_to(row0r[16 * q + kr, :, cols], (8, 128))
                        m = jnp.where(pick_row, extra, m)
                    mirrored.append(m)
                mirrored = reverse_lanes(mirrored)
                for a in range(4):
                    cols = pl.ds(128 * a, 128)
                    if h == 0:
                        first, rest = spec_v[q, ky, pl.ds(8, 8), cols], spec_v[q, ky, pl.ds(0, 8), cols]
                    else:
                        first, rest = spec_v[q, ky, pl.ds(special, 8), cols], spec_v[q, ky, pl.ds(8, 8), cols]
                    amp[q, ky, pl.ds(8 * h, 8), cols] = jnp.where(sub == 0, first, rest) + mirrored[a]

        if h == 0:
            return

        @pl.when(p == 8)
        def _():
            @pl.loop(0, 32)
            def _(n):
                q = n // 16
                ky = lax.rem(n, 16)
                kr = lax.rem(16 - ky, 16)
                own_r, zero_r = [], []
                for a in range(4):
                    cols = pl.ds(128 * a, 128)
                    own_r.append(spec_v[q, kr, pl.ds(0, 8), cols])
                    zero_r.append(jnp.broadcast_to(row0r[16 * q + kr, :, cols], (8, 128)))
                own_r = reverse_lanes(own_r)
                zero_r = reverse_lanes(zero_r)
                for a in range(4):
                    cols = pl.ds(128 * a, 128)
                    last = spec_v[q, ky, pl.ds(0, 8), cols] + own_r[a]
                    first = jnp.broadcast_to(row0r[16 * q + ky, :, cols], (8, 128)) + zero_r[a]
                    old = amp[q, ky, pl.ds(8, 8), cols]
                    amp[q, ky, pl.ds(8, 8), cols] = jnp.where(sub == 0, 0.25 * (first + last), old)
                    bmp[q, ky, :, cols] = jnp.where(sub == 0, 0.25 * (first - last), 0.0)

    def y_stage(re, im, weight, store):
        re, im = fft16(re, im, -1)
        for q in range(2):
            wr, wi = [], []
            for ky in range(16):
                m = weight(q, ky)
                wr.append(m * re[ky])
                wi.append(m * im[ky])
            wr, wi = fft16(wr, wi, 1)
            for y in range(16):
                store(q, 0, y, wr[y])
                store(q, 1, y, wi[y])

    def wait_bytes(ref, sem):
        pltpu.make_async_copy(ref, ref, sem).wait()

    def forward_z():
        b = split(cur[...])
        b = tuple(jnp.concatenate([v, v], axis=0) for v in b)
        out = dot3((zt[0], zt[1]), b, 1, 1).reshape(2, NP, 2, 8, 128)
        wide = lax.broadcasted_iota(jnp.int32, (NP, 8, 128), 2)
        for h in range(2):
            fsend[:, pl.ds(8 * h, 8), :] = jnp.where(wide < 64, out[h, :, 0], out[h, :, 1])

    def forward_send(step):
        for d in pencil_peers():
            remote(fsend.at[d], frecv.at[step, p], fs.at[0], fr.at[step], (t, d)).start()

    loads[0].wait()
    for y in range(2):
        for x in range(XR):
            row = y * XR + (x % 2) * 16 + x // 2
            cur[pl.ds(row, 1), :] = pres_v[x, pl.ds(2 * t + y, 1), :]
    loads[1].wait()
    forward_z()
    heat_begin()
    loads[4].wait()
    for q in range(2):
        row0[pl.ds(16 * q, 16), 0, :] = spec_v[q, :, 0, :]

    pl.semaphore_wait(barrier, NP + NT - 2)
    forward_send(0)
    swaps[0].start()
    loads[5].wait()

    @pl.loop(0, WAVE_STEPS)
    def _(step):
        frecv[step, p] = fsend[p]
        wait_bytes(frecv.at[step, pl.ds(0, NP - 1)], fr.at[step])

        groups = [exchange_groups([frecv[step, 8 * a + i] for i in range(8)]) for a in range(2)]
        parts = []
        for c in range(2):
            rows = [
                jnp.concatenate(
                    [groups[0][y * 2 + c], groups[1][y * 2 + c], groups[0][4 + y * 2 + c], groups[1][4 + y * 2 + c]],
                    axis=1,
                )
                for y in range(2)
            ]
            lhs = split(jnp.concatenate(rows, axis=0))
            parts.append(dot3(lhs, (xt[c, 0], xt[c, 1]), 1, 1))
        for lo, v in ((0, parts[0] + parts[1]), (256, parts[0] - parts[1])):
            for h in range(2):
                for y in range(2):
                    for ri in range(2):
                        vsend[h, y, ri, :, pl.ds(lo, 256)] = v[
                            y * 16 + 8 * h : y * 16 + 8 * h + 8, ri * 256 : ri * 256 + 256
                        ]
        wait_bytes(fsend.at[pl.ds(0, NP - 1)], fs.at[0])

        for dz, dy in TERM_ORDER:
            d = lax.rem(z_place + dz, 4) * 2 + lax.rem(y_place + dy, 2)
            remote(vsend.at[0], agb.at[step, 0, t], gs.at[0], gr.at[step, 0], (d, p)).start()
        remote(vsend.at[1], agb.at[step, 1, t], gs.at[1], gy.at[step], (partner, p)).start()
        for d in z_peers():
            remote(vsend.at[1], agb.at[step, 1, t], gs.at[1], gr.at[step, 1], (d, p)).start()
        for h in range(2):
            agb[step, h, t] = vsend[h]

        @pl.when(step == 0)
        def _():
            swaps[1].start()

            @pl.when(p < 8)
            def _():
                rowcopy.start()

            halo_start(0)
            loads[6].wait()
            for y in range(2):
                for x in range(XR):
                    row = y * XR + (x % 2) * 16 + x // 2
                    prev[pl.ds(row, 1), :] = prior_v[x, pl.ds(2 * t + y, 1), :]
            dose[...] = jnp.zeros_like(dose)
            heat_coefficients()
            loads[7].wait()
            @pl.loop(0, 8)
            def _(n):
                q = n // 4
                cols = pl.ds(pl.multiple_of(lax.rem(n, 4) * 128, 128), 128)
                for y in range(NY):
                    rows = loc_v[q, :, y, cols]
                    for c in range(2):
                        index = (2 * sub + c) % 8
                        for i in range(2):
                            pair = [
                                jnp.take_along_axis(rows[16 * i + 8 * j : 16 * i + 8 * j + 8], index, axis=0)
                                for j in range(2)
                            ]
                            lr[q, y, pl.ds(16 * c + 8 * i, 8), cols] = jnp.where(sub < 4, pair[0], pair[1])

        for h in range(2):

            @pl.when(step == 0)
            def _():
                build_amp(h)

            wait_bytes(agb.at[step, h, pl.ds(0, NT - 1 - h)], gr.at[step, h])

            @pl.loop(0, 4)
            def _(a):
                cols = pl.ds(pl.multiple_of(a * 128, 128), 128)

                def weight(q, ky):
                    return amp[q, ky, pl.ds(8 * h, 8), cols]

                def store(q, ri, y, value):
                    w[q, ri, y, :, cols] = value

                y_stage(
                    [agb[step, h, y // 2, y % 2, 0, :, cols] for y in range(16)],
                    [agb[step, h, y // 2, y % 2, 1, :, cols] for y in range(16)],
                    weight,
                    store,
                )

            if h == 1:

                @pl.when(p == 8)
                def _():
                    @pl.loop(0, 4)
                    def _(a):
                        cols = pl.ds(pl.multiple_of(a * 128, 128), 128)
                        far = pl.ds(pl.multiple_of((3 - a) * 128, 128), 128)
                        near = pl.ds(pl.multiple_of(lax.rem(4 - a, 4) * 128, 128), 128)
                        index = (128 - lane) % 128

                        def load(y, ri):
                            v0 = jnp.take_along_axis(agb[step, 1, y // 2, y % 2, ri, :, near], index, axis=1)
                            v1 = jnp.take_along_axis(agb[step, 1, y // 2, y % 2, ri, :, far], index, axis=1)
                            return jnp.where(lane == 0, v0, v1)

                        def weight(q, ky):
                            return bmp[q, ky, :, cols]

                        def store(q, ri, y, value):
                            w[q, ri, y, :, cols] += value

                        y_stage(
                            [load(y, 0) for y in range(16)],
                            [-load(y, 1) for y in range(16)],
                            weight,
                            store,
                        )

            if h == 0:
                theirs = agb.at[step, 1, partner]
                wait_bytes(theirs, gy.at[step])
                for d in z_peers():
                    remote(theirs, theirs, gs.at[1], gr.at[step, 1], (d, p)).start()

            low = [w[:, ri, :, :, pl.ds(0, 256)].reshape(256, 256) for ri in range(2)]
            high = [w[:, ri, :, :, pl.ds(256, 256)].reshape(256, 256) for ri in range(2)]
            for c in range(2):
                mix = [(lo + hi) if c == 0 else (lo - hi) for lo, hi in zip(low, high)]
                lhs = split(jnp.concatenate(mix, axis=1))
                xo[c] = dot3(lhs, (xt[c, 0], xt[c, 1]), 1, 0).reshape(2, 16, 8, 512)

            @pl.loop(0, 8)
            def _(n):
                q = n // 4
                ra = lax.rem(n, 4)
                ri = ra // 2
                first = 8 * lax.rem(ra, 2)
                cols = pl.ds(pl.multiple_of(ra * 128, 128), 128)
                for yh in range(4):
                    tiles = exchange_groups([xo[i % 2, q, 4 * yh + i // 2, :, cols] for i in range(8)])
                    for i in range(8):
                        snd[first + i, yh, h, q, ri] = tiles[i]

            rcv[step, p, :, h] = snd[p, :, h]

            @pl.loop(0, 2)
            def _(i):
                yh = chunk(i)
                for d in pencil_peers():
                    remote(
                        snd.at[d, yh, h], rcv.at[step, p, yh, h], sent.at[0], came.at[step, yh], (t, d)
                    ).start()

        @pl.loop(2, 4)
        def _(i):
            yh = chunk(i)
            for d in pencil_peers():
                remote(snd.at[d, yh], rcv.at[step, p, yh], sent.at[0], came.at[step, yh], (t, d)).start()

        for h in range(2):
            wait_bytes(agb.at[step, h, pl.ds(0, NT - 1)], gs.at[h])

        @pl.when(step == 0)
        def _():
            heat_middle()

        @pl.when(step == 1)
        def _():
            heat_late()

        @pl.loop(0, 4)
        def _(i):
            yh = chunk(i)
            wait_bytes(rcv.at[step, pl.ds(0, NP - 1), yh], came.at[step, yh])
            d = jnp.concatenate(
                [
                    jnp.concatenate([rcv[step, :, yh, h, q].reshape(256, 128) for q in range(2)], axis=1)
                    for h in range(2)
                ],
                axis=0,
            )
            fields = dot3(split(d), (zt[0], zt[1]), 0, 0)
            total = fields[:128] * lr[0, pl.ds(4 * yh, 4)].reshape(128, 512)
            total = total + fields[128:] * lr[1, pl.ds(4 * yh, 4)].reshape(128, 512)
            psend[yh] = total.reshape(2, 64, 512)

            @pl.when(yh != z_place)
            def _():
                remote(
                    psend.at[yh], rsr.at[step, z_place], rs.at[0], rr.at[step], (2 * yh + y_place, p)
                ).start()

        wait_bytes(snd.at[pl.ds(0, NP - 1)], sent.at[0])
        wait_bytes(rsr.at[step, pl.ds(0, 3)], rr.at[step])

        def z_sum(j):
            total = psend[z_place, j]
            for dz in range(1, 4):
                total = total + rsr[step, lax.rem(z_place + dz, 4), j]
            return total

        psum[...] = z_sum(1 - y_place)
        give_sum = remote(psum, ptake.at[step], ps.at[0], pr.at[step], (partner, p))
        give_sum.start()
        total = z_sum(y_place)
        wait_bytes(psend.at[pl.ds(0, 3)], rs.at[0])
        give_sum.wait_send()
        wait_bytes(ptake.at[step], pr.at[step])
        total = total + ptake[step]
        advanced = SCALE * total - prev[...]
        dose[...] = dose[...] + advanced * advanced
        prev[...] = cur[...]
        cur[...] = advanced

        @pl.when(step == 0)
        def _():
            forward_z()
            forward_send(1)

    heat_finish()
    for y in range(2):
        for x in range(XR):
            row = y * XR + (x % 2) * 16 + x // 2
            result[1, x, pl.ds(y, 1), :] = heat[pl.ds(row, 1), :]


def wave(pres, prior, loc, spec, kinds, props, thermal):
    bricks = jax.ShapeDtypeStruct((2, XR, 2, NZ), F32)
    any_spec = pl.BlockSpec(memory_space=pl.ANY)
    vmem_spec = pl.BlockSpec(memory_space=pltpu.VMEM)
    scratch = [
        pltpu.VMEM((XR, NY, NZ), F32),
        pltpu.VMEM((XR, NY, NZ), F32),
        pltpu.VMEM((2, XR, NY, NZ), F32),
        pltpu.VMEM((2, NY, XR, NZ), F32),
        pltpu.VMEM((2, NY, 32, NX), F32),
        pltpu.VMEM((2, 2, NY, 8, NX), F32),
        pltpu.VMEM((32, 1, NX), F32),
        pltpu.VMEM((32, 1, NX), F32),
        pltpu.VMEM((2, NY, 16, NX), F32),
        pltpu.VMEM((2, NY, 8, NX), F32),
        pltpu.VMEM((2, NZ, NZ), BF16),
        pltpu.VMEM((2, 2, NX, NX), BF16),
        pltpu.VMEM((XR, 2, NZ), jnp.int32),
        pltpu.VMEM((XR, 2, NZ), F32),
        pltpu.VMEM((64, NZ), F32),
        pltpu.VMEM((64, NZ), F32),
        pltpu.VMEM((64, NZ), F32),
        pltpu.VMEM((3, 64, NZ), F32),
        pltpu.VMEM((3, 2, 2, NZ), F32),
        pltpu.VMEM((3, 2, 2, NZ), F32),
        pltpu.VMEM((3, 2, 32, NZ), F32),
        pltpu.VMEM((64, NZ), F32),
        pltpu.VMEM((64, NZ), F32),
        pltpu.VMEM((64, NZ), F32),
        pltpu.VMEM((NP, 16, 128), F32),
        pltpu.VMEM((2, NP, 16, 128), F32),
        pltpu.VMEM((2, 2, 2, 8, NX), F32),
        pltpu.VMEM((2, 2, NT, 2, 2, 8, NX), F32),
        pltpu.VMEM((2, 2, NY, 8, NX), F32),
        pltpu.VMEM((2, 2, NY, 8, NX), F32),
        pltpu.VMEM((NP, 4, 2, 2, 2, 8, 128), F32),
        pltpu.VMEM((2, NP, 4, 2, 2, 2, 8, 128), F32),
        pltpu.VMEM((4, 2, 64, NZ), F32),
        pltpu.VMEM((2, 4, 2, 64, NZ), F32),
        pltpu.VMEM((64, NZ), F32),
        pltpu.VMEM((2, 64, NZ), F32),
        pltpu.SemaphoreType.DMA((8,)),
        pltpu.SemaphoreType.DMA((6,)),
        pltpu.SemaphoreType.DMA((1,)),
        pltpu.SemaphoreType.DMA((2,)),
        pltpu.SemaphoreType.DMA((2,)),
        pltpu.SemaphoreType.DMA((2, 2)),
        pltpu.SemaphoreType.DMA((2,)),
        pltpu.SemaphoreType.DMA((1,)),
        pltpu.SemaphoreType.DMA((2, 4)),
        pltpu.SemaphoreType.DMA((1,)),
        pltpu.SemaphoreType.DMA((2,)),
        pltpu.SemaphoreType.DMA((1,)),
        pltpu.SemaphoreType.DMA((2,)),
        pltpu.SemaphoreType.DMA((3, 4)),
        pltpu.SemaphoreType.DMA((3, 4)),
    ]
    both = pl.pallas_call(
        wave_kernel,
        name="wave",
        out_shape=bricks,
        in_specs=[any_spec] * 8 + [pl.BlockSpec(memory_space=pltpu.SMEM)],
        out_specs=vmem_spec,
        scratch_shapes=scratch,
        compiler_params=pltpu.CompilerParams(
            collective_id=0, has_side_effects=True, vmem_limit_bytes=60 * 2**20
        ),
    )(pres, prior, loc, spec, jnp.asarray(z_table()), jnp.asarray(x_table()), kinds, thermal, props.T)
    return both[0], both[1]


def solution(mesh):
    return jax.shard_map(
        wave,
        mesh=mesh,
        in_specs=(
            P("pencil", None, None),
            P("pencil", None, None),
            P("term", "pencil", None, None),
            P("term", None, "pencil", None),
            P("pencil", "term", None),
            P(),
            P("pencil", "term", None),
        ),
        out_specs=(P("pencil", "term", None), P("pencil", "term", None)),
        check_vma=False,
    )
```

```python
import math

import numpy as np

import jax
import jax.numpy as jnp
from jax import lax
from jax.experimental import pallas as pl
from jax.experimental.pallas import tpu as pltpu
from jax.sharding import PartitionSpec as P

WAVE_STEPS = 2
DIFFUSION = 0.125
MESH = pl.DeviceIdType.MESH
F32 = jnp.float32
BF16 = jnp.bfloat16

NX = 512
NY = 16
NZ = 512
NT = 8
NP = 16
XR = NX // NP
SCALE = 2.0 / (NX * NY * NZ)


PENCIL_ORDER = (
    (1, 0, 0), (0, 1, 0), (3, 1, 1), (2, 0, 0), (0, 1, 1), (1, 1, 0), (3, 0, 0), (2, 1, 1),
    (1, 0, 1), (3, 1, 0), (2, 0, 1), (2, 1, 0), (3, 0, 1), (1, 1, 1), (0, 0, 1),
)


TERM_ORDER = ((2, 0), (0, 1), (1, 1), (3, 1), (1, 0), (3, 0), (2, 1))


def high_low(table):
    high = table.astype(BF16)
    low = (table - high.astype(np.float32)).astype(BF16)
    return np.stack([high, low])


def z_table():
    rows = np.zeros((2, NP, 2, 8, NZ), np.float64)
    z = np.arange(NZ)
    for h in range(2):
        for p in range(NP):
            for i in range(8):
                if h == 1 and i == 0 and p == 8:
                    rows[h, p, 0, i] = 1.0
                    rows[h, p, 1, i] = 1.0 - 2.0 * (z % 2)
                    continue
                j = 8 * h + i
                if i == 0:
                    j = 8 if h == 0 else (16 if p < 8 else 0)
                kz = 32 * p + j
                angle = 2.0 * math.pi * ((kz * z) % NZ) / NZ
                rows[h, p, 0, i] = np.cos(angle)
                rows[h, p, 1, i] = -np.sin(angle)
    return high_low(rows.reshape(NZ, NZ).astype(np.float32))


def x_table():
    k = np.arange(256)[:, None]
    tables = []
    for c in range(2):
        x = 2 * np.arange(256)[None, :] + c
        angle = 2.0 * math.pi * ((k * x) % NX) / NX
        co, si = np.cos(angle), np.sin(angle)
        tables.append(high_low(np.block([[co, si], [-si, co]]).astype(np.float32)))
    return np.stack(tables)


def split(x):
    high = x.astype(BF16)
    low = (x - high.astype(F32)).astype(BF16)
    return high, low


def dot(a, b, ca, cb):
    return lax.dot_general(a, b, (((ca,), (cb,)), ((), ())), preferred_element_type=F32)


def dot3(a, b, ca, cb):
    return dot(a[0], b[0], ca, cb) + dot(a[0], b[1], ca, cb) + dot(a[1], b[0], ca, cb)


def fft16(re, im, sign):
    n = len(re)
    if n == 1:
        return re, im
    er, ei = fft16(re[0::2], im[0::2], sign)
    orr, oi = fft16(re[1::2], im[1::2], sign)
    half = n // 2
    out_r, out_i = [None] * n, [None] * n
    for k in range(half):
        angle = sign * 2.0 * math.pi * k / n
        c, s = math.cos(angle), math.sin(angle)
        a, b = orr[k], oi[k]
        if k == 0:
            tr, ti = a, b
        elif 4 * k == n:
            tr, ti = (b, -a) if sign < 0 else (-b, a)
        elif abs(abs(c) - abs(s)) < 1e-12:
            r = math.sqrt(0.5)
            sc, ss = math.copysign(1.0, c), math.copysign(1.0, s)
            tr = r * ((a if sc > 0 else -a) - (b if ss > 0 else -b))
            ti = r * ((b if sc > 0 else -b) + (a if ss > 0 else -a))
        else:
            tr = c * a - s * b
            ti = c * b + s * a
        out_r[k], out_i[k] = er[k] + tr, ei[k] + ti
        out_r[k + half], out_i[k + half] = er[k] - tr, ei[k] - ti
    return out_r, out_i


def exchange_groups(tiles):
    rows = tiles[0].shape[0]
    lane = lax.broadcasted_iota(jnp.int32, (rows, 128), 1)
    tiles = list(tiles)
    for bit in (4, 2, 1):
        width = bit * 16
        keep_low = (lane % (2 * width)) < width
        new = list(tiles)
        for i in range(8):
            if i & bit:
                continue
            a, b = tiles[i], tiles[i + bit]
            new[i] = jnp.where(keep_low, a, pltpu.roll(b, width, 1))
            new[i + bit] = jnp.where(keep_low, pltpu.roll(a, 128 - width, 1), b)
        tiles = new
    return tiles


def reverse_lanes(tiles):
    lane = lax.broadcasted_iota(jnp.int32, (8, 128), 1)
    index = (128 - lane) % 128
    moved = [jnp.take_along_axis(x, index, axis=1) for x in tiles]
    return [jnp.where(lane == 0, moved[(4 - a) % 4], moved[3 - a]) for a in range(4)]


def wave_kernel(
    pres, prior, loc, spec, ztab, xtab, kinds, thermal, props, result,
    pres_v, prior_v, loc_v, lr, spec_v, srecv, row0, row0r, amp, bmp, zt, xt,
    kind_v, heat_v, absorb, perfuse, heat, field, hxs, hx, hy,
    cur, prev, dose, fsend, frecv, vsend, agb, w, xo, snd, rcv, psend, rsr, psum, ptake,
    lsem, sx, fs, fr, gs, gr, gy, sent, came, rs, rr, ps, pr, hs, hr,
):
    t = lax.axis_index("term")
    p = lax.axis_index("pencil")

    barrier = pltpu.get_barrier_semaphore()

    @pl.loop(1, NP)
    def _(o):
        pl.semaphore_signal(barrier, inc=1, device_id=(t, lax.rem(p + o, NP)), device_id_type=MESH)

    @pl.loop(1, NT)
    def _(o):
        pl.semaphore_signal(barrier, inc=1, device_id=(lax.rem(t + o, NT), p), device_id_type=MESH)

    loads = [
        pltpu.make_async_copy(src, dst, lsem.at[i])
        for i, (src, dst) in enumerate(
            [
                (pres, pres_v), (ztab, zt), (thermal, heat_v), (kinds, kind_v),
                (spec, spec_v), (xtab, xt), (prior, prior_v), (loc, loc_v),
            ]
        )
    ]
    for load in loads:
        load.start()

    def remote(src, dst, send, recv, device):
        return pltpu.make_async_remote_copy(
            src_ref=src, dst_ref=dst, send_sem=send, recv_sem=recv, device_id=device, device_id_type=MESH
        )

    def pencil_peers():
        for dx, dy, dc in PENCIL_ORDER:
            yield (
                lax.rem(p // 4 + dx, 4) * 4 + lax.rem(lax.rem(p // 2, 2) + dy, 2) * 2 + lax.rem(lax.rem(p, 2) + dc, 2)
            )

    z_place, y_place = t // 2, lax.rem(t, 2)
    partner = t + 1 - 2 * y_place

    def chunk(i):
        return lax.rem(z_place + lax.rem(2 + 3 * i + 3 * (i // 2) + 2 * (i // 3), 4), 4)

    def z_peers():
        for dz in (1, 3, 2):
            yield lax.rem(z_place + dz, 4) * 2 + y_place

    mirror = (t, NP - 1 - p)
    swaps = [
        remote(spec.at[:, :, pl.ds(24 - 8 * h, 8), :], srecv.at[h], sx.at[h], sx.at[2 + h], mirror)
        for h in range(2)
    ]
    give = jnp.where(p == 0, 8, lax.rem(NP - p, NP))
    rowcopy = remote(row0, row0r, sx.at[4], sx.at[5], (t, give))

    lane = lax.broadcasted_iota(jnp.int32, (8, 128), 1)
    sub = lax.broadcasted_iota(jnp.int32, (8, 128), 0)
    flip = (8 - sub) % 8

    edges = [
        (t > 0, (t - 1, p)),
        (t < NT - 1, (t + 1, p)),
        (p > 0, (t, p - 1)),
        (p < NP - 1, (t, p + 1)),
    ]

    def halo_copy(k, e):
        if e < 2:
            src, dst = field.at[k, pl.ds(32 * e, 32)], hy.at[k, 1 - e]
        else:
            src, dst = hxs.at[k, e - 2], hx.at[k, 3 - e]
        return remote(src, dst, hs.at[k, e], hr.at[k, 1 - e if e < 2 else 5 - e], edges[e][1])

    def halo_start(k):
        for y in range(2):
            hxs[k, 0, pl.ds(y, 1), :] = field[k, pl.ds(32 * y, 1), :]
            hxs[k, 1, pl.ds(y, 1), :] = field[k, pl.ds(32 * y + 31, 1), :]
        for e in range(4):

            @pl.when(edges[e][0])
            def _():
                halo_copy(k, e).start()

            @pl.when(jnp.logical_not(edges[e][0]))
            def _():
                if e < 2:
                    hy[k, e] = jnp.zeros((32, NZ), F32)
                else:
                    hx[k, e - 2] = jnp.zeros((2, NZ), F32)

    def halo_wait(k):
        for e in range(4):

            @pl.when(edges[e][0])
            def _():
                halo_copy(k, e).wait_send()
                ref = hy.at[k, e] if e < 2 else hx.at[k, e - 2]
                pltpu.make_async_copy(ref, ref, hr.at[k, e]).wait()

    row16 = lax.broadcasted_iota(jnp.int32, (16, NZ), 0)
    col16 = lax.broadcasted_iota(jnp.int32, (16, NZ), 1)

    def heat_apply(k, y, c):
        mine = field[k, pl.ds(32 * y + 16 * c, 16), :]
        other = field[k, pl.ds(32 * y + 16 * (1 - c), 16), :]
        if c == 0:
            shifted = jnp.where(row16 == 0, hx[k, 0, pl.ds(y, 1), :], pltpu.roll(other, 1, 0))
        else:
            shifted = jnp.where(row16 == 15, hx[k, 1, pl.ds(y, 1), :], pltpu.roll(other, 15, 0))
        near = other + shifted
        near = near + field[k, pl.ds(32 * (1 - y) + 16 * c, 16), :] + hy[k, y, pl.ds(16 * c, 16), :]
        near = near + jnp.where(col16 == 0, 0.0, pltpu.roll(mine, 1, 1))
        near = near + jnp.where(col16 == NZ - 1, 0.0, pltpu.roll(mine, NZ - 1, 1))
        rows = pl.ds(32 * y + 16 * c, 16)
        return mine + DIFFUSION * (near - 6.0 * mine) - perfuse[rows, :] * mine

    def heat_begin():
        loads[2].wait()
        for y in range(2):
            for x in range(XR):
                row = y * XR + (x % 2) * 16 + x // 2
                field[0, pl.ds(row, 1), :] = heat_v[x, pl.ds(y, 1), :]

    def heat_coefficients():
        loads[3].wait()
        for y in range(2):
            for x in range(XR):
                row = y * XR + (x % 2) * 16 + x // 2
                kind = kind_v[x, pl.ds(y, 1), :]
                for ref, j in ((absorb, 0), (perfuse, 1)):
                    ref[pl.ds(row, 1), :] = jnp.where(
                        kind == 0, props[j, 0], jnp.where(kind == 1, props[j, 1], props[j, 2])
                    )

    def heat_middle():
        halo_wait(0)
        for y in range(2):
            for c in range(2):
                field[1, pl.ds(32 * y + 16 * c, 16), :] = heat_apply(0, y, c)
        halo_start(1)

    def heat_late():
        halo_wait(1)
        for y in range(2):
            for c in range(2):
                heat[pl.ds(32 * y + 16 * c, 16), :] = heat_apply(1, y, c)

    def heat_finish():
        field[2] = absorb[...] * dose[...]
        halo_start(2)
        for y in range(2):
            for x in range(XR):
                row = y * XR + (x % 2) * 16 + x // 2
                result[0, x, pl.ds(y, 1), :] = cur[pl.ds(row, 1), :]
        halo_wait(2)
        for y in range(2):
            for c in range(2):
                rows = pl.ds(32 * y + 16 * c, 16)
                heat[rows, :] = heat[rows, :] + (field[2, rows, :] + heat_apply(2, y, c))

    def build_amp(h):
        swaps[h].wait()
        if h == 1:

            @pl.when(p < 8)
            def _():
                rowcopy.wait_send()

            @pl.when(p >= 8)
            def _():
                rowcopy.wait_recv()

        low_p = jnp.where(p < 8, 1, 0)
        special = pl.multiple_of(16 * low_p, 8)

        pick_row = (sub == 0) & (low_p == 0)

        @pl.loop(0, 8)
        def _(m4):
            for j in range(4):
                n = 4 * m4 + j
                q = n // 16
                ky = lax.rem(n, 16)
                kr = lax.rem(16 - ky, 16)
                mirrored = []
                for a in range(4):
                    cols = pl.ds(128 * a, 128)
                    m = jnp.take_along_axis(srecv[h, q, kr, :, cols], flip, axis=0)
                    if h == 1:
                        extra = jnp.broadcast_to(row0r[16 * q + kr, :, cols], (8, 128))
                        m = jnp.where(pick_row, extra, m)
                    mirrored.append(m)
                mirrored = reverse_lanes(mirrored)
                for a in range(4):
                    cols = pl.ds(128 * a, 128)
                    if h == 0:
                        first, rest = spec_v[q, ky, pl.ds(8, 8), cols], spec_v[q, ky, pl.ds(0, 8), cols]
                    else:
                        first, rest = spec_v[q, ky, pl.ds(special, 8), cols], spec_v[q, ky, pl.ds(8, 8), cols]
                    amp[q, ky, pl.ds(8 * h, 8), cols] = jnp.where(sub == 0, first, rest) + mirrored[a]

        if h == 0:
            return

        @pl.when(p == 8)
        def _():
            @pl.loop(0, 32)
            def _(n):
                q = n // 16
                ky = lax.rem(n, 16)
                kr = lax.rem(16 - ky, 16)
                own_r, zero_r = [], []
                for a in range(4):
                    cols = pl.ds(128 * a, 128)
                    own_r.append(spec_v[q, kr, pl.ds(0, 8), cols])
                    zero_r.append(jnp.broadcast_to(row0r[16 * q + kr, :, cols], (8, 128)))
                own_r = reverse_lanes(own_r)
                zero_r = reverse_lanes(zero_r)
                for a in range(4):
                    cols = pl.ds(128 * a, 128)
                    last = spec_v[q, ky, pl.ds(0, 8), cols] + own_r[a]
                    first = jnp.broadcast_to(row0r[16 * q + ky, :, cols], (8, 128)) + zero_r[a]
                    old = amp[q, ky, pl.ds(8, 8), cols]
                    amp[q, ky, pl.ds(8, 8), cols] = jnp.where(sub == 0, 0.25 * (first + last), old)
                    bmp[q, ky, :, cols] = jnp.where(sub == 0, 0.25 * (first - last), 0.0)

    def y_stage(re, im, weight, store):
        re, im = fft16(re, im, -1)
        for q in range(2):
            wr, wi = [], []
            for ky in range(16):
                m = weight(q, ky)
                wr.append(m * re[ky])
                wi.append(m * im[ky])
            wr, wi = fft16(wr, wi, 1)
            for y in range(16):
                store(q, 0, y, wr[y])
                store(q, 1, y, wi[y])

    def wait_bytes(ref, sem):
        pltpu.make_async_copy(ref, ref, sem).wait()

    def forward_z():
        b = split(cur[...])
        b = tuple(jnp.concatenate([v, v], axis=0) for v in b)
        out = dot3((zt[0], zt[1]), b, 1, 1).reshape(2, NP, 2, 8, 128)
        wide = lax.broadcasted_iota(jnp.int32, (NP, 8, 128), 2)
        for h in range(2):
            fsend[:, pl.ds(8 * h, 8), :] = jnp.where(wide < 64, out[h, :, 0], out[h, :, 1])

    def forward_send(step):
        for d in pencil_peers():
            remote(fsend.at[d], frecv.at[step, p], fs.at[0], fr.at[step], (t, d)).start()

    loads[0].wait()
    for y in range(2):
        for x in range(XR):
            row = y * XR + (x % 2) * 16 + x // 2
            cur[pl.ds(row, 1), :] = pres_v[x, pl.ds(2 * t + y, 1), :]
    loads[1].wait()
    forward_z()
    heat_begin()
    loads[4].wait()
    for q in range(2):
        row0[pl.ds(16 * q, 16), 0, :] = spec_v[q, :, 0, :]

    pl.semaphore_wait(barrier, NP + NT - 2)
    forward_send(0)
    swaps[0].start()
    loads[5].wait()

    @pl.loop(0, WAVE_STEPS)
    def _(step):
        frecv[step, p] = fsend[p]
        wait_bytes(frecv.at[step, pl.ds(0, NP - 1)], fr.at[step])

        groups = [exchange_groups([frecv[step, 8 * a + i] for i in range(8)]) for a in range(2)]
        parts = []
        for c in range(2):
            rows = [
                jnp.concatenate(
                    [groups[0][y * 2 + c], groups[1][y * 2 + c], groups[0][4 + y * 2 + c], groups[1][4 + y * 2 + c]],
                    axis=1,
                )
                for y in range(2)
            ]
            lhs = split(jnp.concatenate(rows, axis=0))
            parts.append(dot3(lhs, (xt[c, 0], xt[c, 1]), 1, 1))
        for lo, v in ((0, parts[0] + parts[1]), (256, parts[0] - parts[1])):
            for h in range(2):
                for y in range(2):
                    for ri in range(2):
                        vsend[h, y, ri, :, pl.ds(lo, 256)] = v[
                            y * 16 + 8 * h : y * 16 + 8 * h + 8, ri * 256 : ri * 256 + 256
                        ]
        wait_bytes(fsend.at[pl.ds(0, NP - 1)], fs.at[0])

        for dz, dy in TERM_ORDER:
            d = lax.rem(z_place + dz, 4) * 2 + lax.rem(y_place + dy, 2)
            remote(vsend.at[0], agb.at[step, 0, t], gs.at[0], gr.at[step, 0], (d, p)).start()
        remote(vsend.at[1], agb.at[step, 1, t], gs.at[1], gy.at[step], (partner, p)).start()
        for d in z_peers():
            remote(vsend.at[1], agb.at[step, 1, t], gs.at[1], gr.at[step, 1], (d, p)).start()
        for h in range(2):
            agb[step, h, t] = vsend[h]

        @pl.when(step == 0)
        def _():
            swaps[1].start()

            @pl.when(p < 8)
            def _():
                rowcopy.start()

            halo_start(0)
            loads[6].wait()
            for y in range(2):
                for x in range(XR):
                    row = y * XR + (x % 2) * 16 + x // 2
                    prev[pl.ds(row, 1), :] = prior_v[x, pl.ds(2 * t + y, 1), :]
            dose[...] = jnp.zeros_like(dose)
            heat_coefficients()
            loads[7].wait()
            @pl.loop(0, 8)
            def _(n):
                q = n // 4
                cols = pl.ds(pl.multiple_of(lax.rem(n, 4) * 128, 128), 128)
                for y in range(NY):
                    rows = loc_v[q, :, y, cols]
                    for c in range(2):
                        index = (2 * sub + c) % 8
                        for i in range(2):
                            pair = [
                                jnp.take_along_axis(rows[16 * i + 8 * j : 16 * i + 8 * j + 8], index, axis=0)
                                for j in range(2)
                            ]
                            lr[q, y, pl.ds(16 * c + 8 * i, 8), cols] = jnp.where(sub < 4, pair[0], pair[1])

        for h in range(2):

            @pl.when(step == 0)
            def _():
                build_amp(h)

            wait_bytes(agb.at[step, h, pl.ds(0, NT - 1 - h)], gr.at[step, h])

            @pl.loop(0, 4)
            def _(a):
                cols = pl.ds(pl.multiple_of(a * 128, 128), 128)

                def weight(q, ky):
                    return amp[q, ky, pl.ds(8 * h, 8), cols]

                def store(q, ri, y, value):
                    w[q, ri, y, :, cols] = value

                y_stage(
                    [agb[step, h, y // 2, y % 2, 0, :, cols] for y in range(16)],
                    [agb[step, h, y // 2, y % 2, 1, :, cols] for y in range(16)],
                    weight,
                    store,
                )

            if h == 1:

                @pl.when(p == 8)
                def _():
                    @pl.loop(0, 4)
                    def _(a):
                        cols = pl.ds(pl.multiple_of(a * 128, 128), 128)
                        far = pl.ds(pl.multiple_of((3 - a) * 128, 128), 128)
                        near = pl.ds(pl.multiple_of(lax.rem(4 - a, 4) * 128, 128), 128)
                        index = (128 - lane) % 128

                        def load(y, ri):
                            v0 = jnp.take_along_axis(agb[step, 1, y // 2, y % 2, ri, :, near], index, axis=1)
                            v1 = jnp.take_along_axis(agb[step, 1, y // 2, y % 2, ri, :, far], index, axis=1)
                            return jnp.where(lane == 0, v0, v1)

                        def weight(q, ky):
                            return bmp[q, ky, :, cols]

                        def store(q, ri, y, value):
                            w[q, ri, y, :, cols] += value

                        y_stage(
                            [load(y, 0) for y in range(16)],
                            [-load(y, 1) for y in range(16)],
                            weight,
                            store,
                        )

            if h == 0:
                theirs = agb.at[step, 1, partner]
                wait_bytes(theirs, gy.at[step])
                for d in z_peers():
                    remote(theirs, theirs, gs.at[1], gr.at[step, 1], (d, p)).start()

            low = [w[:, ri, :, :, pl.ds(0, 256)].reshape(256, 256) for ri in range(2)]
            high = [w[:, ri, :, :, pl.ds(256, 256)].reshape(256, 256) for ri in range(2)]
            for c in range(2):
                mix = [(lo + hi) if c == 0 else (lo - hi) for lo, hi in zip(low, high)]
                lhs = split(jnp.concatenate(mix, axis=1))
                xo[c] = dot3(lhs, (xt[c, 0], xt[c, 1]), 1, 0).reshape(2, 16, 8, 512)

            @pl.loop(0, 8)
            def _(n):
                q = n // 4
                ra = lax.rem(n, 4)
                ri = ra // 2
                first = 8 * lax.rem(ra, 2)
                cols = pl.ds(pl.multiple_of(ra * 128, 128), 128)
                for yh in range(4):
                    tiles = exchange_groups([xo[i % 2, q, 4 * yh + i // 2, :, cols] for i in range(8)])
                    for i in range(8):
                        snd[first + i, yh, h, q, ri] = tiles[i]

            rcv[step, p, :, h] = snd[p, :, h]

            @pl.loop(0, 3)
            def _(i):
                yh = chunk(i)
                for d in pencil_peers():
                    remote(
                        snd.at[d, yh, h], rcv.at[step, p, yh, h], sent.at[0], came.at[step, yh], (t, d)
                    ).start()

        @pl.loop(3, 4)
        def _(i):
            yh = chunk(i)
            for d in pencil_peers():
                remote(snd.at[d, yh], rcv.at[step, p, yh], sent.at[0], came.at[step, yh], (t, d)).start()

        for h in range(2):
            wait_bytes(agb.at[step, h, pl.ds(0, NT - 1)], gs.at[h])

        @pl.when(step == 0)
        def _():
            heat_middle()

        @pl.when(step == 1)
        def _():
            heat_late()

        @pl.loop(0, 4)
        def _(i):
            yh = chunk(i)
            wait_bytes(rcv.at[step, pl.ds(0, NP - 1), yh], came.at[step, yh])
            d = jnp.concatenate(
                [
                    jnp.concatenate([rcv[step, :, yh, h, q].reshape(256, 128) for q in range(2)], axis=1)
                    for h in range(2)
                ],
                axis=0,
            )
            fields = dot3(split(d), (zt[0], zt[1]), 0, 0)
            total = fields[:128] * lr[0, pl.ds(4 * yh, 4)].reshape(128, 512)
            total = total + fields[128:] * lr[1, pl.ds(4 * yh, 4)].reshape(128, 512)
            psend[yh] = total.reshape(2, 64, 512)

            @pl.when(yh != z_place)
            def _():
                remote(
                    psend.at[yh], rsr.at[step, z_place], rs.at[0], rr.at[step], (2 * yh + y_place, p)
                ).start()

        wait_bytes(snd.at[pl.ds(0, NP - 1)], sent.at[0])
        wait_bytes(rsr.at[step, pl.ds(0, 3)], rr.at[step])

        def z_sum(j):
            total = psend[z_place, j]
            for dz in range(1, 4):
                total = total + rsr[step, lax.rem(z_place + dz, 4), j]
            return total

        psum[...] = z_sum(1 - y_place)
        give_sum = remote(psum, ptake.at[step], ps.at[0], pr.at[step], (partner, p))
        give_sum.start()
        total = z_sum(y_place)
        wait_bytes(psend.at[pl.ds(0, 3)], rs.at[0])
        give_sum.wait_send()
        wait_bytes(ptake.at[step], pr.at[step])
        total = total + ptake[step]
        advanced = SCALE * total - prev[...]
        dose[...] = dose[...] + advanced * advanced
        prev[...] = cur[...]
        cur[...] = advanced

        @pl.when(step == 0)
        def _():
            forward_z()
            forward_send(1)

    heat_finish()
    for y in range(2):
        for x in range(XR):
            row = y * XR + (x % 2) * 16 + x // 2
            result[1, x, pl.ds(y, 1), :] = heat[pl.ds(row, 1), :]


def wave(pres, prior, loc, spec, kinds, props, thermal):
    bricks = jax.ShapeDtypeStruct((2, XR, 2, NZ), F32)
    any_spec = pl.BlockSpec(memory_space=pl.ANY)
    vmem_spec = pl.BlockSpec(memory_space=pltpu.VMEM)
    scratch = [
        pltpu.VMEM((XR, NY, NZ), F32),
        pltpu.VMEM((XR, NY, NZ), F32),
        pltpu.VMEM((2, XR, NY, NZ), F32),
        pltpu.VMEM((2, NY, XR, NZ), F32),
        pltpu.VMEM((2, NY, 32, NX), F32),
        pltpu.VMEM((2, 2, NY, 8, NX), F32),
        pltpu.VMEM((32, 1, NX), F32),
        pltpu.VMEM((32, 1, NX), F32),
        pltpu.VMEM((2, NY, 16, NX), F32),
        pltpu.VMEM((2, NY, 8, NX), F32),
        pltpu.VMEM((2, NZ, NZ), BF16),
        pltpu.VMEM((2, 2, NX, NX), BF16),
        pltpu.VMEM((XR, 2, NZ), jnp.int32),
        pltpu.VMEM((XR, 2, NZ), F32),
        pltpu.VMEM((64, NZ), F32),
        pltpu.VMEM((64, NZ), F32),
        pltpu.VMEM((64, NZ), F32),
        pltpu.VMEM((3, 64, NZ), F32),
        pltpu.VMEM((3, 2, 2, NZ), F32),
        pltpu.VMEM((3, 2, 2, NZ), F32),
        pltpu.VMEM((3, 2, 32, NZ), F32),
        pltpu.VMEM((64, NZ), F32),
        pltpu.VMEM((64, NZ), F32),
        pltpu.VMEM((64, NZ), F32),
        pltpu.VMEM((NP, 16, 128), F32),
        pltpu.VMEM((2, NP, 16, 128), F32),
        pltpu.VMEM((2, 2, 2, 8, NX), F32),
        pltpu.VMEM((2, 2, NT, 2, 2, 8, NX), F32),
        pltpu.VMEM((2, 2, NY, 8, NX), F32),
        pltpu.VMEM((2, 2, NY, 8, NX), F32),
        pltpu.VMEM((NP, 4, 2, 2, 2, 8, 128), F32),
        pltpu.VMEM((2, NP, 4, 2, 2, 2, 8, 128), F32),
        pltpu.VMEM((4, 2, 64, NZ), F32),
        pltpu.VMEM((2, 4, 2, 64, NZ), F32),
        pltpu.VMEM((64, NZ), F32),
        pltpu.VMEM((2, 64, NZ), F32),
        pltpu.SemaphoreType.DMA((8,)),
        pltpu.SemaphoreType.DMA((6,)),
        pltpu.SemaphoreType.DMA((1,)),
        pltpu.SemaphoreType.DMA((2,)),
        pltpu.SemaphoreType.DMA((2,)),
        pltpu.SemaphoreType.DMA((2, 2)),
        pltpu.SemaphoreType.DMA((2,)),
        pltpu.SemaphoreType.DMA((1,)),
        pltpu.SemaphoreType.DMA((2, 4)),
        pltpu.SemaphoreType.DMA((1,)),
        pltpu.SemaphoreType.DMA((2,)),
        pltpu.SemaphoreType.DMA((1,)),
        pltpu.SemaphoreType.DMA((2,)),
        pltpu.SemaphoreType.DMA((3, 4)),
        pltpu.SemaphoreType.DMA((3, 4)),
    ]
    both = pl.pallas_call(
        wave_kernel,
        name="wave",
        out_shape=bricks,
        in_specs=[any_spec] * 8 + [pl.BlockSpec(memory_space=pltpu.SMEM)],
        out_specs=vmem_spec,
        scratch_shapes=scratch,
        compiler_params=pltpu.CompilerParams(
            collective_id=0, has_side_effects=True, vmem_limit_bytes=60 * 2**20
        ),
    )(pres, prior, loc, spec, jnp.asarray(z_table()), jnp.asarray(x_table()), kinds, thermal, props.T)
    return both[0], both[1]


def solution(mesh):
    return jax.shard_map(
        wave,
        mesh=mesh,
        in_specs=(
            P("pencil", None, None),
            P("pencil", None, None),
            P("term", "pencil", None, None),
            P("term", None, "pencil", None),
            P("pencil", "term", None),
            P(),
            P("pencil", "term", None),
        ),
        out_specs=(P("pencil", "term", None), P("pencil", "term", None)),
        check_vma=False,
    )
```
